256 devices in a mesh: claim: 64 (over y_hi, x, z), feat: 4 (over y_lo, core).
Axes of the slice: x: 4, y: 4 (y_hi: 2, y_lo: 2; y = y_hi * 2 + y_lo), z: 8, core: 2. Of those that a mesh axis runs over, the one named last changes fastest.
Arguments:
- block_tiles: bfloat16 [64, 4, 128, 128, 128], P('claim', 'feat'), may hold values from 0.049804688 to 1
- block_scale: float32 [64, 4, 128], P('claim', 'feat'), may hold values from 1 to 12, as said below
- row_index: int32 [64, 4, 128], P('claim', 'feat'), may hold values from 0 to 63
- col_index: int32 [64, 4, 128], P('claim', 'feat'), may hold values from 0 to 31
- start_basis: float32 [16384, 64], P('feat'), may hold values from -6 to 6
Outputs:
- claim_basis: float32 [524288, 64], P(('claim', 'feat'))
- feature_basis: float32 [16384, 64], P(('feat', 'claim'))
- bidiagonal: float32 [4, 64, 64], replicated
The draws below stay inside these ranges and needn't reach their ends.
Inputs may be any that keep to these rules, and one draw needn't show every extreme that they name: `row_index`: row block within the device's 64 row blocks of claims; a few row blocks hold most stored blocks. `col_index`: column block within the device's 32 column blocks. `block_scale`: positive block scales.
All inputs are finite; a program needn't handle non-finite values.
Results may differ from the reference program's by a relative error of at most 0.012.
Values may be sent and summed in bfloat16 or wider, within the bound.
A program may use at most 64 MiB of HBM per device.

```python
import math
import jax
import jax.numpy as jnp
import numpy as np
from jax import lax

F = 16384
BLK = 128
K = 64
BLK_ROWS = 64
BLOCKS_DEV = 128
COL_BLOCKS = 32
N_CLAIM = 64
N_FEAT = 4


def draw_block_scale(key, part):
    shape = (N_CLAIM, N_FEAT, BLOCKS_DEV)
    first_key = jax.random.fold_in(key, 11)
    base = jax.random.uniform(first_key, shape, jnp.float32, 0.0, 1.0)
    ramp = 1.0 + 2.0 * jnp.arange(N_CLAIM, dtype=jnp.float32)[:, None, None] / max(N_CLAIM - 1, 1)
    spread = jnp.exp(base * math.log(4.0))
    return (spread * ramp).astype(jnp.float32)


def plant(result, own_key, least, largest):
    place = [jax.random.randint(jax.random.fold_in(own_key, axis), (), 0, length) for axis, length in enumerate(result.shape)]
    main_axis = result.shape.index(max(result.shape))
    beside = place[:main_axis] + [(place[main_axis] + 1) % result.shape[main_axis]] + place[main_axis + 1:]
    return result.at[tuple(place)].set(least).at[tuple(beside)].set(largest)


def steps_of(stream_key, dims, cuts, low, largest):
    def one(position, shards_of):
        draws = jax.random.uniform(jax.random.fold_in(jax.random.fold_in(stream_key, 6), position), (shards_of,), jnp.float32, low / len(cuts), largest / len(cuts))
        return jnp.repeat(jnp.exp(draws), dims[position] // shards_of).reshape((-1,) + (1,) * (len(dims) - position - 1))

    gain = one(*cuts[0])
    for cut in cuts[1:]:
        gain = gain * one(*cut)
    return gain


def cumulative_ranks(number_of, skew):
    portions = [(1 << 20) // math.isqrt(grade ** skew) + 1 for grade in range(1, number_of + 1)]
    deviation = 1 + sum(portions) // (1 << 30)
    return np.cumsum(np.array([max(1, weight // deviation) for weight in portions]))


def ranked_ids(stream_key, dims, amount, skew):
    table = cumulative_ranks(amount, skew)
    lot = jax.random.randint(jax.random.fold_in(stream_key, 1), dims, 0, int(table[amount - 1]))
    rank = jnp.searchsorted(jnp.asarray(table, jnp.int32), lot, side="right")
    return jax.random.permutation(jax.random.fold_in(stream_key, 2), amount)[rank].astype(jnp.int32)


def normal_values(own_key, extent, scale, most, cuts=(), kind=jnp.bfloat16):
    level = steps_of(own_key, extent, cuts, -0.22, 0.18) if cuts else 1.0
    values = jax.random.normal(own_key, extent, jnp.float32) * scale * level
    return jnp.minimum(jnp.maximum(values, -most), most).astype(kind)


def setup_inputs(seed: int = 0) -> dict:
    arg_keys = jax.random.split(jax.random.key(seed), 6)
    return {
        "block_tiles": jnp.clip(0.049804688 + 0.9501953 * jax.random.uniform(arg_keys[0], (N_CLAIM, N_FEAT, BLOCKS_DEV, BLK, BLK), jnp.float32) ** steps_of(arg_keys[0], (N_CLAIM, N_FEAT, BLOCKS_DEV, BLK, BLK), ((0, 64), (1, 4)), -0.2, 0.2), 0.049804688, 1.0).astype(jnp.bfloat16),
        "block_scale": draw_block_scale(jax.random.fold_in(arg_keys[5], 71), 0),
        "row_index": plant(ranked_ids(arg_keys[2], (N_CLAIM, N_FEAT, BLOCKS_DEV), BLK_ROWS, 2), jax.random.fold_in(arg_keys[2], 3), 0, BLK_ROWS - 1).astype(jnp.int32),
        "col_index": plant(jax.random.randint(arg_keys[3], (N_CLAIM, N_FEAT, BLOCKS_DEV), 0, COL_BLOCKS), jax.random.fold_in(arg_keys[3], 1), 0, COL_BLOCKS - 1).astype(jnp.int32),
        "start_basis": normal_values(arg_keys[4], (F, K), 1.0, 6.0, ((0, 4),), jnp.float32),
    }


HIGH = lax.Precision.HIGHEST

def forward_local(block_tiles, block_scale, row_index, col_index, operand):
    edge = block_tiles.shape[-1]
    width = operand.shape[-1]
    picked = operand.reshape(-1, edge, width)[col_index]
    products = jnp.einsum('bij,bjk->bik', block_tiles.astype(jnp.float32), picked.astype(jnp.float32), precision=HIGH)
    products = products * block_scale[:, None, None]
    selector = (row_index[None, :] == jnp.arange(BLK_ROWS, dtype=jnp.int32)[:, None]).astype(jnp.float32)
    summed = jnp.einsum('rb,bik->rik', selector, products, precision=HIGH)
    return summed.reshape(BLK_ROWS * edge, width)

def backward_local(block_tiles, block_scale, row_index, col_index, operand, col_count):
    edge = block_tiles.shape[-1]
    width = operand.shape[-1]
    picked = operand.reshape(-1, edge, width)[row_index]
    products = jnp.einsum('bij,bik->bjk', block_tiles.astype(jnp.float32), picked.astype(jnp.float32), precision=HIGH)
    products = products * block_scale[:, None, None]
    selector = (col_index[None, :] == jnp.arange(col_count, dtype=jnp.int32)[:, None]).astype(jnp.float32)
    summed = jnp.einsum('cb,bjk->cjk', selector, products, precision=HIGH)
    return summed.reshape(col_count * edge, width)

def degree_local(block_tiles, block_scale, row_index, col_index, col_count):
    row_sums = lax.optimization_barrier(jnp.sum(block_tiles.astype(jnp.float32), axis=2)) * block_scale[:, None]
    col_sums = lax.optimization_barrier(jnp.sum(block_tiles.astype(jnp.float32), axis=1)) * block_scale[:, None]
    row_select = (row_index[None, :] == jnp.arange(BLK_ROWS, dtype=jnp.int32)[:, None]).astype(jnp.float32)
    col_select = (col_index[None, :] == jnp.arange(col_count, dtype=jnp.int32)[:, None]).astype(jnp.float32)
    row_part = jnp.einsum('rb,bi->ri', row_select, row_sums, precision=HIGH).reshape(-1)
    col_part = jnp.einsum('cb,bi->ci', col_select, col_sums, precision=HIGH).reshape(-1)
    return (row_part, col_part)

def gram_of(block):
    return jnp.dot(block.T, block, precision=HIGH)

def orthonormal(block, gram_total):
    factor = jnp.linalg.cholesky(gram_total)
    basis = lax.linalg.triangular_solve(factor, block, left_side=False, lower=True, transpose_a=True)
    return (basis, factor.T)

def reference(block_tiles, block_scale, row_index, col_index, start_basis):
    col_count = F // N_FEAT // BLK

    def degrees_of(items):
        tiles_one, scale_one, rows_one, cols_one = items
        return jax.vmap(lambda tiles_here, scale_here, rows_here, cols_here: degree_local(tiles_here, scale_here, rows_here, cols_here, col_count))(tiles_one, scale_one, rows_one, cols_one)
    row_parts, col_parts = lax.map(degrees_of, (block_tiles, block_scale, row_index, col_index))
    row_degree = lax.optimization_barrier(jnp.sum(row_parts, axis=1)).reshape(-1)
    col_degree = lax.optimization_barrier(jnp.sum(col_parts, axis=0)).reshape(-1)
    row_scale = lax.rsqrt(row_degree + 1.0)
    col_scale = lax.rsqrt(col_degree + 1.0)

    def forward(basis):
        operand = (col_scale[:, None] * basis).astype(jnp.bfloat16).reshape(N_FEAT, -1, K)

        def per_claim(items):
            tiles_one, scale_one, rows_one, cols_one = items
            parts = jax.vmap(forward_local)(tiles_one, scale_one, rows_one, cols_one, operand)
            return lax.optimization_barrier(jnp.sum(parts, axis=0))
        summed = lax.map(per_claim, (block_tiles, block_scale, row_index, col_index)).reshape(-1, K)
        return row_scale[:, None] * summed

    def backward(basis):
        operand = (row_scale[:, None] * basis).astype(jnp.bfloat16).reshape(N_CLAIM, -1, K)

        def accumulate(total, items):
            tiles_one, scale_one, rows_one, cols_one, operand_one = items
            parts = jax.vmap(lambda tiles_here, scale_here, rows_here, cols_here: backward_local(tiles_here, scale_here, rows_here, cols_here, operand_one, col_count))(tiles_one, scale_one, rows_one, cols_one)
            return (total + parts, None)
        initial = jnp.zeros((N_FEAT, F // N_FEAT, K), jnp.float32)
        total, _ = lax.scan(accumulate, initial, (block_tiles, block_scale, row_index, col_index, operand))
        return col_scale[:, None] * total.reshape(F, K)
    first_basis, _ = orthonormal(start_basis, gram_of(start_basis))
    first_forward = forward(first_basis)
    u_first, b_first = orthonormal(first_forward, gram_of(first_forward))
    q_first = backward(u_first) - jnp.dot(first_basis, b_first.T, precision=HIGH)
    v_second, a_second = orthonormal(q_first, gram_of(q_first))
    p_second = forward(v_second) - jnp.dot(u_first, a_second.T, precision=HIGH)
    u_second, b_second = orthonormal(p_second, gram_of(p_second))
    q_second = backward(u_second) - jnp.dot(v_second, b_second.T, precision=HIGH)
    v_third, a_third = orthonormal(q_second, gram_of(q_second))
    bidiagonal = jnp.stack([b_first, a_second, b_second, a_third])
    return (u_second, v_third, bidiagonal)
```

```python
import jax
import jax.numpy as jnp
from jax import lax
from jax.sharding import Mesh
from jax.sharding import PartitionSpec as P

BLK_ROWS = 64

HIGH = lax.Precision.HIGHEST

FINE = ("yh", "x", "z", "yl", "c")
CLAIM = ("yh", "x", "z")
FEAT = ("yl", "c")


def forward_local(block_tiles, block_scale, row_index, col_index, operand):
    edge = block_tiles.shape[-1]
    width = operand.shape[-1]
    picked = operand.reshape(-1, edge, width)[col_index]
    products = jnp.einsum("bij,bjk->bik", block_tiles, picked, preferred_element_type=jnp.float32)
    products = products * block_scale[:, None, None]
    selector = (row_index[None, :] == jnp.arange(BLK_ROWS, dtype=jnp.int32)[:, None]).astype(
        jnp.float32
    )
    summed = jnp.einsum("rb,bik->rik", selector, products, precision=HIGH)
    return summed.reshape(BLK_ROWS * edge, width)


def backward_local(block_tiles, block_scale, row_index, col_index, operand, col_count):
    edge = block_tiles.shape[-1]
    width = operand.shape[-1]
    picked = operand.reshape(-1, edge, width)[row_index]
    products = jnp.einsum("bij,bik->bjk", block_tiles, picked, preferred_element_type=jnp.float32)
    products = products * block_scale[:, None, None]
    selector = (col_index[None, :] == jnp.arange(col_count, dtype=jnp.int32)[:, None]).astype(
        jnp.float32
    )
    summed = jnp.einsum("cb,bjk->cjk", selector, products, precision=HIGH)
    return summed.reshape(col_count * edge, width)


def degree_local(block_tiles, block_scale, row_index, col_index, col_count):
    row_sums = jnp.sum(block_tiles, axis=2, dtype=jnp.float32) * block_scale[:, None]
    col_sums = jnp.sum(block_tiles, axis=1, dtype=jnp.float32) * block_scale[:, None]
    row_select = (row_index[None, :] == jnp.arange(BLK_ROWS, dtype=jnp.int32)[:, None]).astype(
        jnp.float32
    )
    col_select = (col_index[None, :] == jnp.arange(col_count, dtype=jnp.int32)[:, None]).astype(
        jnp.float32
    )
    row_part = jnp.einsum("rb,bi->ri", row_select, row_sums, precision=HIGH).reshape(-1)
    col_part = jnp.einsum("cb,bi->ci", col_select, col_sums, precision=HIGH).reshape(-1)
    return (row_part, col_part)


def gram_of(block):
    return jnp.dot(block.T, block, precision=HIGH)


def orthonormal(block, gram_total):
    factor = jnp.linalg.cholesky(gram_total)
    basis = lax.linalg.triangular_solve(
        factor, block, left_side=False, lower=True, transpose_a=True
    )
    return (basis, factor.T)


def claim_sum(value):
    part = lax.psum_scatter(value, "z", scatter_dimension=0, tiled=True)
    part = lax.psum(part, ("yh", "x"))
    return lax.all_gather(part, "z", axis=0, tiled=True)


def all_sum(value):
    value = lax.psum(value, FEAT)
    value = lax.psum(value, "z")
    return lax.psum(value, ("yh", "x"))


def claim_scatter(value):
    size_z = lax.axis_size("z")
    size_o = lax.axis_size("yh") * lax.axis_size("x")
    rows = value.shape[0] // (size_z * size_o)
    blocks = value.reshape(size_o, size_z, rows, -1).transpose(1, 0, 2, 3).reshape(value.shape)
    part = lax.psum_scatter(blocks, "z", scatter_dimension=0, tiled=True)
    return lax.psum_scatter(part, ("yh", "x"), scatter_dimension=0, tiled=True)


def per_device(block_tiles, block_scale, row_index, col_index, start_basis):
    tiles_here = block_tiles.reshape(block_tiles.shape[-3:])
    scale_here = block_scale.reshape(-1)
    rows_here = row_index.reshape(-1)
    cols_here = col_index.reshape(-1)
    edge = tiles_here.shape[-1]
    col_count = start_basis.shape[0] // edge
    claim_count = lax.axis_size(CLAIM)
    own_cols = start_basis.shape[0] // claim_count
    own_first = lax.axis_index(CLAIM) * own_cols
    row_part, col_part = degree_local(tiles_here, scale_here, rows_here, cols_here, col_count)
    col_total = claim_sum(col_part)
    col_scale = lax.rsqrt(col_total + 1.0)
    row_total = lax.psum_scatter(row_part, FEAT, scatter_dimension=0, tiled=True)
    start_total = lax.psum(gram_of(start_basis), FEAT)
    first_basis, _ = orthonormal(start_basis, start_total)
    first_operand = (col_scale[:, None] * first_basis).astype(jnp.bfloat16)
    first_partial = forward_local(tiles_here, scale_here, rows_here, cols_here, first_operand)
    first_sums = lax.psum_scatter(first_partial, FEAT, scatter_dimension=0, tiled=True)
    row_scale = lax.rsqrt(row_total + 1.0)

    def row_orthonormal(block):
        return orthonormal(block, all_sum(gram_of(block)))

    def backward_partial(basis):
        operand = (row_scale[:, None] * basis).astype(jnp.bfloat16)
        gathered = lax.all_gather(operand, FEAT, axis=0, tiled=True)
        return backward_local(tiles_here, scale_here, rows_here, cols_here, gathered, col_count)

    u_first, b_first = row_orthonormal(row_scale[:, None] * first_sums)
    summed = claim_sum(backward_partial(u_first))
    update = col_scale[:, None] * summed - jnp.dot(first_basis, b_first.T, precision=HIGH)
    v_second, a_second = orthonormal(update, lax.psum(gram_of(update), FEAT))
    scaled = (col_scale[:, None] * v_second).astype(jnp.bfloat16)
    second_partial = forward_local(tiles_here, scale_here, rows_here, cols_here, scaled)
    second_sums = lax.psum_scatter(second_partial, FEAT, scatter_dimension=0, tiled=True)
    p_second = row_scale[:, None] * second_sums - jnp.dot(u_first, a_second.T, precision=HIGH)
    u_second, b_second = row_orthonormal(p_second)
    own_sums = claim_scatter(backward_partial(u_second))
    own_scale = lax.dynamic_slice_in_dim(col_scale, own_first, own_cols, 0)
    own_second = lax.dynamic_slice_in_dim(v_second, own_first, own_cols, 0)
    q_second = own_scale[:, None] * own_sums - jnp.dot(own_second, b_second.T, precision=HIGH)
    v_output, a_third = orthonormal(q_second, all_sum(gram_of(q_second)))
    bidiagonal = jnp.stack([b_first, a_second, b_second, a_third])
    return (u_second, v_output, bidiagonal)


def solution(mesh):
    claim_n, feat_n = mesh.devices.shape
    fine = Mesh(mesh.devices.reshape(2, claim_n // 16, 8, 2, feat_n // 2), FINE)
    placed = (
        P(CLAIM, FEAT, None, None, None),
        P(CLAIM, FEAT, None),
        P(CLAIM, FEAT, None),
        P(CLAIM, FEAT, None),
        P(FEAT, None),
    )
    return jax.shard_map(
        per_device,
        mesh=fine,
        in_specs=placed,
        out_specs=(P(CLAIM + FEAT, None), P(FEAT + CLAIM, None), P()),
        check_vma=False,
    )
```

```python
import functools

import jax
import jax.numpy as jnp
from jax import lax
from jax.experimental import pallas as pl
from jax.experimental.pallas import tpu as pltpu
from jax.sharding import Mesh
from jax.sharding import PartitionSpec as P

BLK_ROWS = 64

HIGH = lax.Precision.HIGHEST

FINE = ("yh", "x", "z", "yl", "c")
CLAIM = ("yh", "x", "z")
FEAT = ("yl", "c")


def forward_local(block_tiles, block_scale, row_index, col_index, operand):
    edge = block_tiles.shape[-1]
    width = operand.shape[-1]
    picked = operand.reshape(-1, edge, width)[col_index]
    products = jnp.einsum("bij,bjk->bik", block_tiles, picked, preferred_element_type=jnp.float32)
    products = products * block_scale[:, None, None]
    selector = (row_index[None, :] == jnp.arange(BLK_ROWS, dtype=jnp.int32)[:, None]).astype(
        jnp.float32
    )
    summed = jnp.einsum("rb,bik->rik", selector, products, precision=HIGH)
    return summed.reshape(BLK_ROWS * edge, width)


def backward_local(block_tiles, block_scale, row_index, col_index, operand, col_count):
    edge = block_tiles.shape[-1]
    width = operand.shape[-1]
    picked = operand.reshape(-1, edge, width)[row_index]
    products = jnp.einsum("bij,bik->bjk", block_tiles, picked, preferred_element_type=jnp.float32)
    products = products * block_scale[:, None, None]
    selector = (col_index[None, :] == jnp.arange(col_count, dtype=jnp.int32)[:, None]).astype(
        jnp.float32
    )
    summed = jnp.einsum("cb,bjk->cjk", selector, products, precision=HIGH)
    return summed.reshape(col_count * edge, width)


def degree_local(block_tiles, block_scale, row_index, col_index, col_count):
    row_sums = jnp.sum(block_tiles, axis=2, dtype=jnp.float32) * block_scale[:, None]
    col_sums = jnp.sum(block_tiles, axis=1, dtype=jnp.float32) * block_scale[:, None]
    row_select = (row_index[None, :] == jnp.arange(BLK_ROWS, dtype=jnp.int32)[:, None]).astype(
        jnp.float32
    )
    col_select = (col_index[None, :] == jnp.arange(col_count, dtype=jnp.int32)[:, None]).astype(
        jnp.float32
    )
    row_part = jnp.einsum("rb,bi->ri", row_select, row_sums, precision=HIGH).reshape(-1)
    col_part = jnp.einsum("cb,bi->ci", col_select, col_sums, precision=HIGH).reshape(-1)
    return (row_part, col_part)


def gram_of(block):
    return jnp.dot(block.T, block, precision=HIGH)


def orthonormal(block, gram_total):
    factor = jnp.linalg.cholesky(gram_total)
    basis = lax.linalg.triangular_solve(
        factor, block, left_side=False, lower=True, transpose_a=True
    )
    return (basis, factor.T)


def butterfly_kernel(stages, x_ref, o_ref, recv, send_sem, recv_sem):
    coords = [lax.axis_index(name) for name in FINE]
    partners = []
    for axis, step in stages:
        place = coords[axis]
        flip = place + step * (1 - 2 * ((place // step) % 2))
        partners.append(tuple(flip if i == axis else c for i, c in enumerate(coords)))
    barrier = pltpu.get_barrier_semaphore()
    for partner in partners:
        pl.semaphore_signal(barrier, inc=1, device_id=partner, device_id_type=pl.DeviceIdType.MESH)
    pl.semaphore_wait(barrier, len(partners))
    o_ref[...] = x_ref[...]
    for s, partner in enumerate(partners):
        copy = pltpu.make_async_remote_copy(
            src_ref=o_ref,
            dst_ref=recv.at[s],
            send_sem=send_sem.at[s],
            recv_sem=recv_sem.at[s],
            device_id=partner,
            device_id_type=pl.DeviceIdType.MESH,
        )
        copy.start()
        copy.wait()
        o_ref[...] = o_ref[...] + recv[s]


def butterfly_sum(value, names, cid):
    stages = []
    for name in names:
        size = lax.axis_size(name)
        step = 1
        while step < size:
            stages.append((FINE.index(name), step))
            step *= 2
    shape = value.shape
    flat = value.reshape(-1, 128) if value.ndim == 1 else value
    out = pl.pallas_call(
        functools.partial(butterfly_kernel, tuple(stages)),
        out_shape=jax.ShapeDtypeStruct(flat.shape, flat.dtype),
        in_specs=[pl.BlockSpec(memory_space=pltpu.VMEM)],
        out_specs=pl.BlockSpec(memory_space=pltpu.VMEM),
        scratch_shapes=[
            pltpu.VMEM((len(stages),) + flat.shape, flat.dtype),
            pltpu.SemaphoreType.DMA((len(stages),)),
            pltpu.SemaphoreType.DMA((len(stages),)),
        ],
        compiler_params=pltpu.CompilerParams(collective_id=cid, has_side_effects=True),
    )(flat)
    return out.reshape(shape)


def claim_sum(value):
    part = lax.psum_scatter(value, "z", scatter_dimension=0, tiled=True)
    part = lax.psum(part, ("yh", "x"))
    return lax.all_gather(part, "z", axis=0, tiled=True)


def all_sum(value):
    value = lax.psum(value, FEAT)
    value = lax.psum(value, "z")
    return lax.psum(value, ("yh", "x"))


def claim_scatter(value):
    size_z = lax.axis_size("z")
    size_o = lax.axis_size("yh") * lax.axis_size("x")
    rows = value.shape[0] // (size_z * size_o)
    blocks = value.reshape(size_o, size_z, rows, -1).transpose(1, 0, 2, 3).reshape(value.shape)
    part = lax.psum_scatter(blocks, "z", scatter_dimension=0, tiled=True)
    return lax.psum_scatter(part, ("yh", "x"), scatter_dimension=0, tiled=True)


def per_device(block_tiles, block_scale, row_index, col_index, start_basis):
    tiles_here = block_tiles.reshape(block_tiles.shape[-3:])
    scale_here = block_scale.reshape(-1)
    rows_here = row_index.reshape(-1)
    cols_here = col_index.reshape(-1)
    edge = tiles_here.shape[-1]
    col_count = start_basis.shape[0] // edge
    claim_count = lax.axis_size(CLAIM)
    own_cols = start_basis.shape[0] // claim_count
    own_first = lax.axis_index(CLAIM) * own_cols
    row_part, col_part = degree_local(tiles_here, scale_here, rows_here, cols_here, col_count)
    col_total = butterfly_sum(col_part, CLAIM, 0)
    col_scale = lax.rsqrt(col_total + 1.0)
    row_total = lax.psum_scatter(row_part, FEAT, scatter_dimension=0, tiled=True)
    start_total = lax.psum(gram_of(start_basis), FEAT)
    first_basis, _ = orthonormal(start_basis, start_total)
    first_operand = (col_scale[:, None] * first_basis).astype(jnp.bfloat16)
    first_partial = forward_local(tiles_here, scale_here, rows_here, cols_here, first_operand)
    first_sums = lax.psum_scatter(first_partial, FEAT, scatter_dimension=0, tiled=True)
    row_scale = lax.rsqrt(row_total + 1.0)

    def row_orthonormal(block, cid):
        return orthonormal(block, butterfly_sum(gram_of(block), FINE, cid))

    def backward_partial(basis):
        operand = (row_scale[:, None] * basis).astype(jnp.bfloat16)
        gathered = lax.all_gather(operand, FEAT, axis=0, tiled=True)
        return backward_local(tiles_here, scale_here, rows_here, cols_here, gathered, col_count)

    u_first, b_first = row_orthonormal(row_scale[:, None] * first_sums, 1)
    summed = claim_sum(backward_partial(u_first))
    update = col_scale[:, None] * summed - jnp.dot(first_basis, b_first.T, precision=HIGH)
    v_second, a_second = orthonormal(update, lax.psum(gram_of(update), FEAT))
    scaled = (col_scale[:, None] * v_second).astype(jnp.bfloat16)
    second_partial = forward_local(tiles_here, scale_here, rows_here, cols_here, scaled)
    second_sums = lax.psum_scatter(second_partial, FEAT, scatter_dimension=0, tiled=True)
    p_second = row_scale[:, None] * second_sums - jnp.dot(u_first, a_second.T, precision=HIGH)
    u_second, b_second = row_orthonormal(p_second, 2)
    own_sums = claim_scatter(backward_partial(u_second))
    own_scale = lax.dynamic_slice_in_dim(col_scale, own_first, own_cols, 0)
    own_second = lax.dynamic_slice_in_dim(v_second, own_first, own_cols, 0)
    q_second = own_scale[:, None] * own_sums - jnp.dot(own_second, b_second.T, precision=HIGH)
    v_output, a_third = orthonormal(q_second, butterfly_sum(gram_of(q_second), FINE, 3))
    bidiagonal = jnp.stack([b_first, a_second, b_second, a_third])
    return (u_second, v_output, bidiagonal)


def solution(mesh):
    claim_n, feat_n = mesh.devices.shape
    fine = Mesh(mesh.devices.reshape(2, claim_n // 16, 8, 2, feat_n // 2), FINE)
    placed = (
        P(CLAIM, FEAT, None, None, None),
        P(CLAIM, FEAT, None),
        P(CLAIM, FEAT, None),
        P(CLAIM, FEAT, None),
        P(FEAT, None),
    )
    return jax.shard_map(
        per_device,
        mesh=fine,
        in_specs=placed,
        out_specs=(P(CLAIM + FEAT, None), P(FEAT + CLAIM, None), P()),
        check_vma=False,
    )
```

```python
import functools

import jax
import jax.numpy as jnp
from jax import lax
from jax.experimental import pallas as pl
from jax.experimental.pallas import tpu as pltpu
from jax.sharding import Mesh
from jax.sharding import PartitionSpec as P

BLK_ROWS = 64

HIGH = lax.Precision.HIGHEST

FINE = ("yh", "x", "z", "yl", "c")
CLAIM = ("yh", "x", "z")
FEAT = ("yl", "c")


def forward_local(block_tiles, block_scale, row_index, col_index, operand):
    edge = block_tiles.shape[-1]
    width = operand.shape[-1]
    picked = operand.reshape(-1, edge, width)[col_index]
    products = jnp.einsum("bij,bjk->bik", block_tiles, picked, preferred_element_type=jnp.float32)
    products = products * block_scale[:, None, None]
    selector = (row_index[None, :] == jnp.arange(BLK_ROWS, dtype=jnp.int32)[:, None]).astype(
        jnp.float32
    )
    summed = jnp.einsum("rb,bik->rik", selector, products, precision=HIGH)
    return summed.reshape(BLK_ROWS * edge, width)


def backward_local(block_tiles, block_scale, row_index, col_index, operand, col_count):
    edge = block_tiles.shape[-1]
    width = operand.shape[-1]
    picked = operand.reshape(-1, edge, width)[row_index]
    products = jnp.einsum("bij,bik->bjk", block_tiles, picked, preferred_element_type=jnp.float32)
    products = products * block_scale[:, None, None]
    selector = (col_index[None, :] == jnp.arange(col_count, dtype=jnp.int32)[:, None]).astype(
        jnp.float32
    )
    summed = jnp.einsum("cb,bjk->cjk", selector, products, precision=HIGH)
    return summed.reshape(col_count * edge, width)


def degree_local(block_tiles, block_scale, row_index, col_index, col_count):
    row_sums = jnp.sum(block_tiles, axis=2, dtype=jnp.float32) * block_scale[:, None]
    col_sums = jnp.sum(block_tiles, axis=1, dtype=jnp.float32) * block_scale[:, None]
    row_select = (row_index[None, :] == jnp.arange(BLK_ROWS, dtype=jnp.int32)[:, None]).astype(
        jnp.float32
    )
    col_select = (col_index[None, :] == jnp.arange(col_count, dtype=jnp.int32)[:, None]).astype(
        jnp.float32
    )
    row_part = jnp.einsum("rb,bi->ri", row_select, row_sums, precision=HIGH).reshape(-1)
    col_part = jnp.einsum("cb,bi->ci", col_select, col_sums, precision=HIGH).reshape(-1)
    return (row_part, col_part)


def gram_of(block):
    return jnp.dot(block.T, block, precision=HIGH)


def orthonormal(block, gram_total):
    factor = jnp.linalg.cholesky(gram_total)
    basis = lax.linalg.triangular_solve(
        factor, block, left_side=False, lower=True, transpose_a=True
    )
    return (basis, factor.T)


def butterfly_kernel(stages, x_ref, o_ref, recv, send_sem, recv_sem):
    coords = [lax.axis_index(name) for name in FINE]
    partners = []
    for axis, step in stages:
        place = coords[axis]
        flip = place + step * (1 - 2 * ((place // step) % 2))
        partners.append(tuple(flip if i == axis else c for i, c in enumerate(coords)))
    barrier = pltpu.get_barrier_semaphore()
    for partner in partners:
        pl.semaphore_signal(barrier, inc=1, device_id=partner, device_id_type=pl.DeviceIdType.MESH)
    pl.semaphore_wait(barrier, len(partners))
    o_ref[...] = x_ref[...]
    for s, partner in enumerate(partners):
        copy = pltpu.make_async_remote_copy(
            src_ref=o_ref,
            dst_ref=recv.at[s],
            send_sem=send_sem.at[s],
            recv_sem=recv_sem.at[s],
            device_id=partner,
            device_id_type=pl.DeviceIdType.MESH,
        )
        copy.start()
        copy.wait()
        o_ref[...] = o_ref[...] + recv[s]


def butterfly_sum(value, names, cid):
    stages = []
    for name in names:
        size = lax.axis_size(name)
        step = 1
        while step < size:
            stages.append((FINE.index(name), step))
            step *= 2
    shape = value.shape
    flat = value.reshape(-1, 128) if value.ndim == 1 else value
    out = pl.pallas_call(
        functools.partial(butterfly_kernel, tuple(stages)),
        out_shape=jax.ShapeDtypeStruct(flat.shape, flat.dtype),
        in_specs=[pl.BlockSpec(memory_space=pltpu.VMEM)],
        out_specs=pl.BlockSpec(memory_space=pltpu.VMEM),
        scratch_shapes=[
            pltpu.VMEM((len(stages),) + flat.shape, flat.dtype),
            pltpu.SemaphoreType.DMA((len(stages),)),
            pltpu.SemaphoreType.DMA((len(stages),)),
        ],
        compiler_params=pltpu.CompilerParams(collective_id=cid, has_side_effects=True),
    )(flat)
    return out.reshape(shape)


def halving_kernel(stages, gather, x_ref, o_ref, *scratch):
    if gather:
        work, recv, back, rs_send, rs_recv, ag_send, ag_recv = o_ref, *scratch
    else:
        work, recv, rs_send, rs_recv = scratch
    coords = [lax.axis_index(name) for name in FINE]
    partners, bits = [], []
    for axis, step in stages:
        place = coords[axis]
        bit = (place // step) % 2
        flip = place + step * (1 - 2 * bit)
        partners.append(tuple(flip if i == axis else c for i, c in enumerate(coords)))
        bits.append(bit)
    barrier = pltpu.get_barrier_semaphore()
    for partner in partners:
        pl.semaphore_signal(barrier, inc=1, device_id=partner, device_id_type=pl.DeviceIdType.MESH)
    pl.semaphore_wait(barrier, len(partners))
    work[...] = x_ref[...]
    total = work.shape[0]
    base = 0
    pieces = []
    for s, partner in enumerate(partners):
        size = total >> s
        half = size // 2
        keep = base + bits[s] * half
        give = base + (1 - bits[s]) * half
        slot = pl.ds(total - size, half)
        copy = pltpu.make_async_remote_copy(
            src_ref=work.at[pl.ds(give, half)],
            dst_ref=recv.at[slot],
            send_sem=rs_send.at[s],
            recv_sem=rs_recv.at[s],
            device_id=partner,
            device_id_type=pl.DeviceIdType.MESH,
        )
        copy.start()
        copy.wait()
        work[pl.ds(keep, half), :] = work[pl.ds(keep, half), :] + recv[slot, :]
        pieces.append((keep, give, slot))
        base = keep
    if gather:
        for s in reversed(range(len(partners))):
            keep, give, slot = pieces[s]
            copy = pltpu.make_async_remote_copy(
                src_ref=work.at[pl.ds(keep, slot.size)],
                dst_ref=back.at[slot],
                send_sem=ag_send.at[s],
                recv_sem=ag_recv.at[s],
                device_id=partners[s],
                device_id_type=pl.DeviceIdType.MESH,
            )
            copy.start()
            copy.wait()
            work[pl.ds(give, slot.size), :] = back[slot, :]
    else:
        o_ref[...] = work[pl.ds(base, o_ref.shape[0]), :]


CLAIM_STAGES = (("z", 1), ("x", 1), ("z", 2), ("x", 2), ("yh", 1), ("z", 4))


def claim_halving(value, gather, cid):
    stages = tuple((FINE.index(name), step) for name, step in CLAIM_STAGES)
    count = len(stages)
    flat = value.reshape(-1, 128)
    rows = flat.shape[0]
    out_rows = rows if gather else rows >> count
    scratch = [] if gather else [pltpu.VMEM(flat.shape, flat.dtype)]
    scratch += [pltpu.VMEM(flat.shape, flat.dtype)] * (2 if gather else 1)
    scratch += [pltpu.SemaphoreType.DMA((count,))] * (4 if gather else 2)
    out = pl.pallas_call(
        functools.partial(halving_kernel, stages, gather),
        out_shape=jax.ShapeDtypeStruct((out_rows, 128), flat.dtype),
        in_specs=[pl.BlockSpec(memory_space=pltpu.VMEM)],
        out_specs=pl.BlockSpec(memory_space=pltpu.VMEM),
        scratch_shapes=scratch,
        compiler_params=pltpu.CompilerParams(collective_id=cid, has_side_effects=True),
    )(flat)
    return out


def claim_sum(value):
    part = lax.psum_scatter(value, "z", scatter_dimension=0, tiled=True)
    part = lax.psum(part, ("yh", "x"))
    return lax.all_gather(part, "z", axis=0, tiled=True)


def all_sum(value):
    value = lax.psum(value, FEAT)
    value = lax.psum(value, "z")
    return lax.psum(value, ("yh", "x"))


def claim_scatter(value):
    width = value.shape[-1]
    rows = value.shape[0] // lax.axis_size(CLAIM)
    bits = value.reshape(2, 2, 2, 2, 2, 2, rows, width)
    ordered = bits.transpose(5, 2, 4, 1, 0, 3, 6, 7).reshape(value.shape)
    return claim_halving(ordered, False, 5).reshape(rows, width)


def per_device(block_tiles, block_scale, row_index, col_index, start_basis):
    tiles_here = block_tiles.reshape(block_tiles.shape[-3:])
    scale_here = block_scale.reshape(-1)
    rows_here = row_index.reshape(-1)
    cols_here = col_index.reshape(-1)
    edge = tiles_here.shape[-1]
    col_count = start_basis.shape[0] // edge
    claim_count = lax.axis_size(CLAIM)
    own_cols = start_basis.shape[0] // claim_count
    own_first = lax.axis_index(CLAIM) * own_cols
    row_part, col_part = degree_local(tiles_here, scale_here, rows_here, cols_here, col_count)
    col_total = butterfly_sum(col_part, CLAIM, 0)
    col_scale = lax.rsqrt(col_total + 1.0)
    row_total = lax.psum_scatter(row_part, FEAT, scatter_dimension=0, tiled=True)
    start_total = lax.psum(gram_of(start_basis), FEAT)
    first_basis, _ = orthonormal(start_basis, start_total)
    first_operand = (col_scale[:, None] * first_basis).astype(jnp.bfloat16)
    first_partial = forward_local(tiles_here, scale_here, rows_here, cols_here, first_operand)
    first_sums = lax.psum_scatter(first_partial, FEAT, scatter_dimension=0, tiled=True)
    row_scale = lax.rsqrt(row_total + 1.0)

    def row_orthonormal(block, cid):
        return orthonormal(block, butterfly_sum(gram_of(block), FINE, cid))

    def backward_partial(basis):
        operand = (row_scale[:, None] * basis).astype(jnp.bfloat16)
        gathered = lax.all_gather(operand, FEAT, axis=0, tiled=True)
        return backward_local(tiles_here, scale_here, rows_here, cols_here, gathered, col_count)

    u_first, b_first = row_orthonormal(row_scale[:, None] * first_sums, 1)
    summed = claim_halving(backward_partial(u_first), True, 4).reshape(-1, u_first.shape[-1])
    update = col_scale[:, None] * summed - jnp.dot(first_basis, b_first.T, precision=HIGH)
    v_second, a_second = orthonormal(update, lax.psum(gram_of(update), FEAT))
    scaled = (col_scale[:, None] * v_second).astype(jnp.bfloat16)
    second_partial = forward_local(tiles_here, scale_here, rows_here, cols_here, scaled)
    second_sums = lax.psum_scatter(second_partial, FEAT, scatter_dimension=0, tiled=True)
    p_second = row_scale[:, None] * second_sums - jnp.dot(u_first, a_second.T, precision=HIGH)
    u_second, b_second = row_orthonormal(p_second, 2)
    own_sums = claim_scatter(backward_partial(u_second))
    own_scale = lax.dynamic_slice_in_dim(col_scale, own_first, own_cols, 0)
    own_second = lax.dynamic_slice_in_dim(v_second, own_first, own_cols, 0)
    q_second = own_scale[:, None] * own_sums - jnp.dot(own_second, b_second.T, precision=HIGH)
    v_output, a_third = orthonormal(q_second, butterfly_sum(gram_of(q_second), FINE, 3))
    bidiagonal = jnp.stack([b_first, a_second, b_second, a_third])
    return (u_second, v_output, bidiagonal)


def solution(mesh):
    claim_n, feat_n = mesh.devices.shape
    fine = Mesh(mesh.devices.reshape(2, claim_n // 16, 8, 2, feat_n // 2), FINE)
    placed = (
        P(CLAIM, FEAT, None, None, None),
        P(CLAIM, FEAT, None),
        P(CLAIM, FEAT, None),
        P(CLAIM, FEAT, None),
        P(FEAT, None),
    )
    return jax.shard_map(
        per_device,
        mesh=fine,
        in_specs=placed,
        out_specs=(P(CLAIM + FEAT, None), P(FEAT + CLAIM, None), P()),
        check_vma=False,
    )
```

```python
import functools

import jax
import jax.numpy as jnp
from jax import lax
from jax.experimental import pallas as pl
from jax.experimental.pallas import tpu as pltpu
from jax.sharding import Mesh
from jax.sharding import PartitionSpec as P

BLK_ROWS = 64

HIGH = lax.Precision.HIGHEST

FINE = ("yh", "x", "z", "yl", "c")
CLAIM = ("yh", "x", "z")
FEAT = ("yl", "c")


def forward_local(block_tiles, block_scale, row_index, col_index, operand):
    edge = block_tiles.shape[-1]
    width = operand.shape[-1]
    picked = operand.reshape(-1, edge, width)[col_index]
    products = jnp.einsum("bij,bjk->bik", block_tiles, picked, preferred_element_type=jnp.float32)
    products = products * block_scale[:, None, None]
    selector = (row_index[None, :] == jnp.arange(BLK_ROWS, dtype=jnp.int32)[:, None]).astype(
        jnp.float32
    )
    summed = jnp.einsum("rb,bik->rik", selector, products, precision=HIGH)
    return summed.reshape(BLK_ROWS * edge, width)


def backward_local(block_tiles, block_scale, row_index, col_index, operand, col_count):
    edge = block_tiles.shape[-1]
    width = operand.shape[-1]
    picked = operand.reshape(-1, edge, width)[row_index]
    products = jnp.einsum("bij,bik->bjk", block_tiles, picked, preferred_element_type=jnp.float32)
    products = products * block_scale[:, None, None]
    selector = (col_index[None, :] == jnp.arange(col_count, dtype=jnp.int32)[:, None]).astype(
        jnp.float32
    )
    summed = jnp.einsum("cb,bjk->cjk", selector, products, precision=HIGH)
    return summed.reshape(col_count * edge, width)


def degree_local(block_tiles, block_scale, row_index, col_index, col_count):
    row_sums = jnp.sum(block_tiles, axis=2, dtype=jnp.float32) * block_scale[:, None]
    col_sums = jnp.sum(block_tiles, axis=1, dtype=jnp.float32) * block_scale[:, None]
    row_select = (row_index[None, :] == jnp.arange(BLK_ROWS, dtype=jnp.int32)[:, None]).astype(
        jnp.float32
    )
    col_select = (col_index[None, :] == jnp.arange(col_count, dtype=jnp.int32)[:, None]).astype(
        jnp.float32
    )
    row_part = jnp.einsum("rb,bi->ri", row_select, row_sums, precision=HIGH).reshape(-1)
    col_part = jnp.einsum("cb,bi->ci", col_select, col_sums, precision=HIGH).reshape(-1)
    return (row_part, col_part)


def gram_of(block):
    return jnp.dot(block.T, block, precision=HIGH)


def orthonormal(block, gram_total):
    factor = jnp.linalg.cholesky(gram_total)
    basis = lax.linalg.triangular_solve(
        factor, block, left_side=False, lower=True, transpose_a=True
    )
    return (basis, factor.T)


def group_kernel(groups, x_ref, o_ref, slots, send_sem, recv_sem):
    coords = [lax.axis_index(name) for name in FINE]
    plans = []
    for axes, sizes in groups:
        count = 1
        for size in sizes:
            count *= size
        me = 0
        for axis, size in zip(axes, sizes):
            me = me * size + coords[axis]
        targets = []
        for k in range(1, count):
            member = (me + k) % count
            place = list(coords)
            rest = member
            for axis, size in reversed(list(zip(axes, sizes))):
                place[axis] = rest % size
                rest = rest // size
            targets.append((tuple(place), (me + count - k) % count))
        plans.append((count, me, targets))
    barrier = pltpu.get_barrier_semaphore()
    total = 0
    for count, me, targets in plans:
        for place, _ in targets:
            pl.semaphore_signal(barrier, inc=1, device_id=place, device_id_type=pl.DeviceIdType.MESH)
        total += len(targets)
    pl.semaphore_wait(barrier, total)
    o_ref[...] = x_ref[...]
    for g, (count, me, targets) in enumerate(plans):
        slots[g, me] = o_ref[...]
        copies = []
        for k, (place, _) in enumerate(targets):
            copy = pltpu.make_async_remote_copy(
                src_ref=o_ref,
                dst_ref=slots.at[g, me],
                send_sem=send_sem.at[g, k],
                recv_sem=recv_sem.at[g, me],
                device_id=place,
                device_id_type=pl.DeviceIdType.MESH,
            )
            copy.start()
            copies.append(copy)
        for copy in copies:
            copy.wait_send()
        for place, sender in targets:
            pltpu.make_async_remote_copy(
                src_ref=o_ref,
                dst_ref=slots.at[g, sender],
                send_sem=send_sem.at[g, 0],
                recv_sem=recv_sem.at[g, sender],
                device_id=place,
                device_id_type=pl.DeviceIdType.MESH,
            ).wait_recv()
        acc = slots[g, 0]
        for j in range(1, count):
            acc = acc + slots[g, j]
        o_ref[...] = acc


def group_sum(value, groups, cid):
    spec = []
    widest = 1
    for names in groups:
        sizes = tuple(lax.axis_size(name) for name in names)
        count = 1
        for size in sizes:
            count *= size
        widest = max(widest, count)
        spec.append((tuple(FINE.index(name) for name in names), sizes))
    shape = value.shape
    flat = value.reshape(-1, 128) if value.ndim == 1 else value
    out = pl.pallas_call(
        functools.partial(group_kernel, tuple(spec)),
        out_shape=jax.ShapeDtypeStruct(flat.shape, flat.dtype),
        in_specs=[pl.BlockSpec(memory_space=pltpu.VMEM)],
        out_specs=pl.BlockSpec(memory_space=pltpu.VMEM),
        scratch_shapes=[
            pltpu.VMEM((len(spec), widest) + flat.shape, flat.dtype),
            pltpu.SemaphoreType.DMA((len(spec), widest)),
            pltpu.SemaphoreType.DMA((len(spec), widest)),
        ],
        compiler_params=pltpu.CompilerParams(collective_id=cid, has_side_effects=True),
    )(flat)
    return out.reshape(shape)


ALL_GROUPS = (FEAT, ("z",), ("yh", "x"))
CLAIM_GROUPS = (("z",), ("yh", "x"))


def halving_kernel(stages, gather, x_ref, o_ref, *scratch):
    if gather:
        work, recv, back, rs_send, rs_recv, ag_send, ag_recv = o_ref, *scratch
    else:
        work, recv, rs_send, rs_recv = scratch
    coords = [lax.axis_index(name) for name in FINE]
    partners, bits = [], []
    for axis, step in stages:
        place = coords[axis]
        bit = (place // step) % 2
        flip = place + step * (1 - 2 * bit)
        partners.append(tuple(flip if i == axis else c for i, c in enumerate(coords)))
        bits.append(bit)
    barrier = pltpu.get_barrier_semaphore()
    for partner in partners:
        pl.semaphore_signal(barrier, inc=1, device_id=partner, device_id_type=pl.DeviceIdType.MESH)
    pl.semaphore_wait(barrier, len(partners))
    work[...] = x_ref[...]
    total = work.shape[0]
    base = 0
    pieces = []
    for s, partner in enumerate(partners):
        size = total >> s
        half = size // 2
        keep = base + bits[s] * half
        give = base + (1 - bits[s]) * half
        slot = pl.ds(total - size, half)
        copy = pltpu.make_async_remote_copy(
            src_ref=work.at[pl.ds(give, half)],
            dst_ref=recv.at[slot],
            send_sem=rs_send.at[s],
            recv_sem=rs_recv.at[s],
            device_id=partner,
            device_id_type=pl.DeviceIdType.MESH,
        )
        copy.start()
        copy.wait()
        work[pl.ds(keep, half), :] = work[pl.ds(keep, half), :] + recv[slot, :]
        pieces.append((keep, give, slot))
        base = keep
    if gather:
        for s in reversed(range(len(partners))):
            keep, give, slot = pieces[s]
            copy = pltpu.make_async_remote_copy(
                src_ref=work.at[pl.ds(keep, slot.size)],
                dst_ref=back.at[slot],
                send_sem=ag_send.at[s],
                recv_sem=ag_recv.at[s],
                device_id=partners[s],
                device_id_type=pl.DeviceIdType.MESH,
            )
            copy.start()
            copy.wait()
            work[pl.ds(give, slot.size), :] = back[slot, :]
    else:
        o_ref[...] = work[pl.ds(base, o_ref.shape[0]), :]


CLAIM_STAGES = (("z", 1), ("x", 1), ("z", 2), ("x", 2), ("yh", 1), ("z", 4))


def claim_halving(value, gather, cid):
    stages = tuple((FINE.index(name), step) for name, step in CLAIM_STAGES)
    count = len(stages)
    flat = value.reshape(-1, 128)
    rows = flat.shape[0]
    out_rows = rows if gather else rows >> count
    scratch = [] if gather else [pltpu.VMEM(flat.shape, flat.dtype)]
    scratch += [pltpu.VMEM(flat.shape, flat.dtype)] * (2 if gather else 1)
    scratch += [pltpu.SemaphoreType.DMA((count,))] * (4 if gather else 2)
    out = pl.pallas_call(
        functools.partial(halving_kernel, stages, gather),
        out_shape=jax.ShapeDtypeStruct((out_rows, 128), flat.dtype),
        in_specs=[pl.BlockSpec(memory_space=pltpu.VMEM)],
        out_specs=pl.BlockSpec(memory_space=pltpu.VMEM),
        scratch_shapes=scratch,
        compiler_params=pltpu.CompilerParams(collective_id=cid, has_side_effects=True),
    )(flat)
    return out


def claim_sum(value):
    part = lax.psum_scatter(value, "z", scatter_dimension=0, tiled=True)
    part = lax.psum(part, ("yh", "x"))
    return lax.all_gather(part, "z", axis=0, tiled=True)


def all_sum(value):
    value = lax.psum(value, FEAT)
    value = lax.psum(value, "z")
    return lax.psum(value, ("yh", "x"))


def claim_scatter(value):
    width = value.shape[-1]
    rows = value.shape[0] // lax.axis_size(CLAIM)
    bits = value.reshape(2, 2, 2, 2, 2, 2, rows, width)
    ordered = bits.transpose(5, 2, 4, 1, 0, 3, 6, 7).reshape(value.shape)
    return claim_halving(ordered, False, 5).reshape(rows, width)


def per_device(block_tiles, block_scale, row_index, col_index, start_basis):
    tiles_here = block_tiles.reshape(block_tiles.shape[-3:])
    scale_here = block_scale.reshape(-1)
    rows_here = row_index.reshape(-1)
    cols_here = col_index.reshape(-1)
    edge = tiles_here.shape[-1]
    col_count = start_basis.shape[0] // edge
    claim_count = lax.axis_size(CLAIM)
    own_cols = start_basis.shape[0] // claim_count
    own_first = lax.axis_index(CLAIM) * own_cols
    row_part, col_part = degree_local(tiles_here, scale_here, rows_here, cols_here, col_count)
    col_total = group_sum(col_part, CLAIM_GROUPS, 0)
    col_scale = lax.rsqrt(col_total + 1.0)
    row_total = lax.psum_scatter(row_part, FEAT, scatter_dimension=0, tiled=True)
    start_total = lax.psum(gram_of(start_basis), FEAT)
    first_basis, _ = orthonormal(start_basis, start_total)
    first_operand = (col_scale[:, None] * first_basis).astype(jnp.bfloat16)
    first_partial = forward_local(tiles_here, scale_here, rows_here, cols_here, first_operand)
    first_sums = lax.psum_scatter(first_partial, FEAT, scatter_dimension=0, tiled=True)
    row_scale = lax.rsqrt(row_total + 1.0)

    def row_orthonormal(block, cid):
        return orthonormal(block, group_sum(gram_of(block), ALL_GROUPS, cid))

    def backward_partial(basis):
        operand = (row_scale[:, None] * basis).astype(jnp.bfloat16)
        gathered = lax.all_gather(operand, FEAT, axis=0, tiled=True)
        return backward_local(tiles_here, scale_here, rows_here, cols_here, gathered, col_count)

    u_first, b_first = row_orthonormal(row_scale[:, None] * first_sums, 1)
    summed = claim_halving(backward_partial(u_first), True, 4).reshape(-1, u_first.shape[-1])
    update = col_scale[:, None] * summed - jnp.dot(first_basis, b_first.T, precision=HIGH)
    v_second, a_second = orthonormal(update, lax.psum(gram_of(update), FEAT))
    scaled = (col_scale[:, None] * v_second).astype(jnp.bfloat16)
    second_partial = forward_local(tiles_here, scale_here, rows_here, cols_here, scaled)
    second_sums = lax.psum_scatter(second_partial, FEAT, scatter_dimension=0, tiled=True)
    p_second = row_scale[:, None] * second_sums - jnp.dot(u_first, a_second.T, precision=HIGH)
    u_second, b_second = row_orthonormal(p_second, 2)
    own_sums = claim_scatter(backward_partial(u_second))
    own_scale = lax.dynamic_slice_in_dim(col_scale, own_first, own_cols, 0)
    own_second = lax.dynamic_slice_in_dim(v_second, own_first, own_cols, 0)
    q_second = own_scale[:, None] * own_sums - jnp.dot(own_second, b_second.T, precision=HIGH)
    v_output, a_third = orthonormal(q_second, group_sum(gram_of(q_second), ALL_GROUPS, 3))
    bidiagonal = jnp.stack([b_first, a_second, b_second, a_third])
    return (u_second, v_output, bidiagonal)


def solution(mesh):
    claim_n, feat_n = mesh.devices.shape
    fine = Mesh(mesh.devices.reshape(2, claim_n // 16, 8, 2, feat_n // 2), FINE)
    placed = (
        P(CLAIM, FEAT, None, None, None),
        P(CLAIM, FEAT, None),
        P(CLAIM, FEAT, None),
        P(CLAIM, FEAT, None),
        P(FEAT, None),
    )
    return jax.shard_map(
        per_device,
        mesh=fine,
        in_specs=placed,
        out_specs=(P(CLAIM + FEAT, None), P(FEAT + CLAIM, None), P()),
        check_vma=False,
    )
```

```python
import functools

import jax
import jax.numpy as jnp
from jax import lax
from jax.experimental import pallas as pl
from jax.experimental.pallas import tpu as pltpu
from jax.sharding import Mesh
from jax.sharding import PartitionSpec as P

BLK_ROWS = 64

HIGH = lax.Precision.HIGHEST

FINE = ("yh", "x", "z", "yl", "c")
CLAIM = ("yh", "x", "z")
FEAT = ("yl", "c")


TILES_PER_STEP = 16


def forward_kernel(rows_ref, cols_ref, scale_ref, tiles_ref, operand_ref, out_ref):
    step = pl.program_id(0)
    edge = tiles_ref.shape[-1]

    @pl.when(step == 0)
    def _():
        out_ref[...] = jnp.zeros_like(out_ref)

    for t in range(tiles_ref.shape[0]):
        b = step * tiles_ref.shape[0] + t
        picked = operand_ref[pl.ds(pl.multiple_of(cols_ref[b] * edge, edge), edge), :]
        product = jnp.dot(tiles_ref[t], picked, preferred_element_type=jnp.float32) * scale_ref[b]
        target = pl.ds(pl.multiple_of(rows_ref[b] * edge, edge), edge)
        out_ref[target, :] = out_ref[target, :] + product


def backward_kernel(rows_ref, cols_ref, scale_ref, tiles_ref, operand_ref, out_ref):
    step = pl.program_id(0)
    edge = tiles_ref.shape[-1]

    @pl.when(step == 0)
    def _():
        out_ref[...] = jnp.zeros_like(out_ref)

    for t in range(tiles_ref.shape[0]):
        b = step * tiles_ref.shape[0] + t
        picked = operand_ref[:, pl.ds(pl.multiple_of(rows_ref[b] * edge, edge), edge)]
        product = jnp.dot(picked, tiles_ref[t], preferred_element_type=jnp.float32) * scale_ref[b]
        target = pl.ds(pl.multiple_of(cols_ref[b] * edge, edge), edge)
        out_ref[:, target] = out_ref[:, target] + product


def block_product(kernel, block_tiles, block_scale, row_index, col_index, operand, out_shape):
    count, edge, _ = block_tiles.shape
    per = TILES_PER_STEP
    grid_spec = pltpu.PrefetchScalarGridSpec(
        num_scalar_prefetch=2,
        grid=(count // per,),
        in_specs=[
            pl.BlockSpec(memory_space=pltpu.SMEM),
            pl.BlockSpec((per, edge, edge), lambda i, rows, cols: (i, 0, 0)),
            pl.BlockSpec(operand.shape, lambda i, rows, cols: (0, 0)),
        ],
        out_specs=pl.BlockSpec(out_shape, lambda i, rows, cols: (0, 0)),
    )
    width = min(operand.shape)
    return pl.pallas_call(
        kernel,
        grid_spec=grid_spec,
        out_shape=jax.ShapeDtypeStruct(out_shape, jnp.float32),
        cost_estimate=pl.CostEstimate(
            flops=2 * count * edge * edge * width,
            bytes_accessed=block_tiles.size * 2 + operand.size * 2 + out_shape[0] * out_shape[1] * 4,
            transcendentals=0,
        ),
    )(row_index, col_index, block_scale, block_tiles, operand)


def forward_local(block_tiles, block_scale, row_index, col_index, operand):
    edge = block_tiles.shape[-1]
    out_shape = (BLK_ROWS * edge, operand.shape[-1])
    return block_product(forward_kernel, block_tiles, block_scale, row_index, col_index, operand, out_shape)


def backward_local(block_tiles, block_scale, row_index, col_index, operand, col_count):
    edge = block_tiles.shape[-1]
    out_shape = (operand.shape[-1], col_count * edge)
    flipped = block_product(
        backward_kernel, block_tiles, block_scale, row_index, col_index, operand.T, out_shape
    )
    return flipped.T


def degree_local(block_tiles, block_scale, row_index, col_index, col_count):
    row_sums = jnp.sum(block_tiles, axis=2, dtype=jnp.float32) * block_scale[:, None]
    col_sums = jnp.sum(block_tiles, axis=1, dtype=jnp.float32) * block_scale[:, None]
    row_select = (row_index[None, :] == jnp.arange(BLK_ROWS, dtype=jnp.int32)[:, None]).astype(
        jnp.float32
    )
    col_select = (col_index[None, :] == jnp.arange(col_count, dtype=jnp.int32)[:, None]).astype(
        jnp.float32
    )
    row_part = jnp.einsum("rb,bi->ri", row_select, row_sums, precision=HIGH).reshape(-1)
    col_part = jnp.einsum("cb,bi->ci", col_select, col_sums, precision=HIGH).reshape(-1)
    return (row_part, col_part)


def gram_of(block):
    return jnp.dot(block.T, block, precision=HIGH)


def orthonormal(block, gram_total):
    factor = jnp.linalg.cholesky(gram_total)
    basis = lax.linalg.triangular_solve(
        factor, block, left_side=False, lower=True, transpose_a=True
    )
    return (basis, factor.T)


def group_kernel(groups, x_ref, o_ref, slots, send_sem, recv_sem):
    coords = [lax.axis_index(name) for name in FINE]
    plans = []
    for axes, sizes in groups:
        count = 1
        for size in sizes:
            count *= size
        me = 0
        for axis, size in zip(axes, sizes):
            me = me * size + coords[axis]
        targets = []
        for k in range(1, count):
            member = (me + k) % count
            place = list(coords)
            rest = member
            for axis, size in reversed(list(zip(axes, sizes))):
                place[axis] = rest % size
                rest = rest // size
            targets.append((tuple(place), (me + count - k) % count))
        plans.append((count, me, targets))
    barrier = pltpu.get_barrier_semaphore()
    total = 0
    for count, me, targets in plans:
        for place, _ in targets:
            pl.semaphore_signal(barrier, inc=1, device_id=place, device_id_type=pl.DeviceIdType.MESH)
        total += len(targets)
    pl.semaphore_wait(barrier, total)
    o_ref[...] = x_ref[...]
    for g, (count, me, targets) in enumerate(plans):
        slots[g, me] = o_ref[...]
        copies = []
        for k, (place, _) in enumerate(targets):
            copy = pltpu.make_async_remote_copy(
                src_ref=o_ref,
                dst_ref=slots.at[g, me],
                send_sem=send_sem.at[g, k],
                recv_sem=recv_sem.at[g, me],
                device_id=place,
                device_id_type=pl.DeviceIdType.MESH,
            )
            copy.start()
            copies.append(copy)
        for copy in copies:
            copy.wait_send()
        for place, sender in targets:
            pltpu.make_async_remote_copy(
                src_ref=o_ref,
                dst_ref=slots.at[g, sender],
                send_sem=send_sem.at[g, 0],
                recv_sem=recv_sem.at[g, sender],
                device_id=place,
                device_id_type=pl.DeviceIdType.MESH,
            ).wait_recv()
        acc = slots[g, 0]
        for j in range(1, count):
            acc = acc + slots[g, j]
        o_ref[...] = acc


def group_sum(value, groups, cid):
    spec = []
    widest = 1
    for names in groups:
        sizes = tuple(lax.axis_size(name) for name in names)
        count = 1
        for size in sizes:
            count *= size
        widest = max(widest, count)
        spec.append((tuple(FINE.index(name) for name in names), sizes))
    shape = value.shape
    flat = value.reshape(-1, 128) if value.ndim == 1 else value
    out = pl.pallas_call(
        functools.partial(group_kernel, tuple(spec)),
        out_shape=jax.ShapeDtypeStruct(flat.shape, flat.dtype),
        in_specs=[pl.BlockSpec(memory_space=pltpu.VMEM)],
        out_specs=pl.BlockSpec(memory_space=pltpu.VMEM),
        scratch_shapes=[
            pltpu.VMEM((len(spec), widest) + flat.shape, flat.dtype),
            pltpu.SemaphoreType.DMA((len(spec), widest)),
            pltpu.SemaphoreType.DMA((len(spec), widest)),
        ],
        compiler_params=pltpu.CompilerParams(collective_id=cid, has_side_effects=True),
    )(flat)
    return out.reshape(shape)


ALL_GROUPS = (FEAT, ("z",), ("yh", "x"))
CLAIM_GROUPS = (("z",), ("yh", "x"))


def halving_kernel(stages, gather, x_ref, o_ref, *scratch):
    if gather:
        work, recv, back, rs_send, rs_recv, ag_send, ag_recv = o_ref, *scratch
    else:
        work, recv, rs_send, rs_recv = scratch
    coords = [lax.axis_index(name) for name in FINE]
    partners, bits = [], []
    for axis, step in stages:
        place = coords[axis]
        bit = (place // step) % 2
        flip = place + step * (1 - 2 * bit)
        partners.append(tuple(flip if i == axis else c for i, c in enumerate(coords)))
        bits.append(bit)
    barrier = pltpu.get_barrier_semaphore()
    for partner in partners:
        pl.semaphore_signal(barrier, inc=1, device_id=partner, device_id_type=pl.DeviceIdType.MESH)
    pl.semaphore_wait(barrier, len(partners))
    work[...] = x_ref[...]
    total = work.shape[0]
    base = 0
    pieces = []
    for s, partner in enumerate(partners):
        size = total >> s
        half = size // 2
        keep = base + bits[s] * half
        give = base + (1 - bits[s]) * half
        slot = pl.ds(total - size, half)
        copy = pltpu.make_async_remote_copy(
            src_ref=work.at[pl.ds(give, half)],
            dst_ref=recv.at[slot],
            send_sem=rs_send.at[s],
            recv_sem=rs_recv.at[s],
            device_id=partner,
            device_id_type=pl.DeviceIdType.MESH,
        )
        copy.start()
        copy.wait()
        work[pl.ds(keep, half), :] = work[pl.ds(keep, half), :] + recv[slot, :]
        pieces.append((keep, give, slot))
        base = keep
    if gather:
        for s in reversed(range(len(partners))):
            keep, give, slot = pieces[s]
            copy = pltpu.make_async_remote_copy(
                src_ref=work.at[pl.ds(keep, slot.size)],
                dst_ref=back.at[slot],
                send_sem=ag_send.at[s],
                recv_sem=ag_recv.at[s],
                device_id=partners[s],
                device_id_type=pl.DeviceIdType.MESH,
            )
            copy.start()
            copy.wait()
            work[pl.ds(give, slot.size), :] = back[slot, :]
    else:
        o_ref[...] = work[pl.ds(base, o_ref.shape[0]), :]


CLAIM_STAGES = (("z", 1), ("x", 1), ("z", 2), ("x", 2), ("yh", 1), ("z", 4))


def claim_halving(value, gather, cid):
    stages = tuple((FINE.index(name), step) for name, step in CLAIM_STAGES)
    count = len(stages)
    flat = value.reshape(-1, 128)
    rows = flat.shape[0]
    out_rows = rows if gather else rows >> count
    scratch = [] if gather else [pltpu.VMEM(flat.shape, flat.dtype)]
    scratch += [pltpu.VMEM(flat.shape, flat.dtype)] * (2 if gather else 1)
    scratch += [pltpu.SemaphoreType.DMA((count,))] * (4 if gather else 2)
    out = pl.pallas_call(
        functools.partial(halving_kernel, stages, gather),
        out_shape=jax.ShapeDtypeStruct((out_rows, 128), flat.dtype),
        in_specs=[pl.BlockSpec(memory_space=pltpu.VMEM)],
        out_specs=pl.BlockSpec(memory_space=pltpu.VMEM),
        scratch_shapes=scratch,
        compiler_params=pltpu.CompilerParams(collective_id=cid, has_side_effects=True),
    )(flat)
    return out


def claim_sum(value):
    part = lax.psum_scatter(value, "z", scatter_dimension=0, tiled=True)
    part = lax.psum(part, ("yh", "x"))
    return lax.all_gather(part, "z", axis=0, tiled=True)


def all_sum(value):
    value = lax.psum(value, FEAT)
    value = lax.psum(value, "z")
    return lax.psum(value, ("yh", "x"))


def claim_scatter(value):
    width = value.shape[-1]
    rows = value.shape[0] // lax.axis_size(CLAIM)
    bits = value.reshape(2, 2, 2, 2, 2, 2, rows, width)
    ordered = bits.transpose(5, 2, 4, 1, 0, 3, 6, 7).reshape(value.shape)
    return claim_halving(ordered, False, 5).reshape(rows, width)


def per_device(block_tiles, block_scale, row_index, col_index, start_basis):
    tiles_here = block_tiles.reshape(block_tiles.shape[-3:])
    scale_here = block_scale.reshape(-1)
    rows_here = row_index.reshape(-1)
    cols_here = col_index.reshape(-1)
    edge = tiles_here.shape[-1]
    col_count = start_basis.shape[0] // edge
    claim_count = lax.axis_size(CLAIM)
    own_cols = start_basis.shape[0] // claim_count
    own_first = lax.axis_index(CLAIM) * own_cols
    row_part, col_part = degree_local(tiles_here, scale_here, rows_here, cols_here, col_count)
    col_total = group_sum(col_part, CLAIM_GROUPS, 0)
    col_scale = lax.rsqrt(col_total + 1.0)
    row_total = lax.psum_scatter(row_part, FEAT, scatter_dimension=0, tiled=True)
    start_total = lax.psum(gram_of(start_basis), FEAT)
    first_basis, _ = orthonormal(start_basis, start_total)
    first_operand = (col_scale[:, None] * first_basis).astype(jnp.bfloat16)
    first_partial = forward_local(tiles_here, scale_here, rows_here, cols_here, first_operand)
    first_sums = lax.psum_scatter(first_partial, FEAT, scatter_dimension=0, tiled=True)
    row_scale = lax.rsqrt(row_total + 1.0)

    def row_orthonormal(block, cid):
        return orthonormal(block, group_sum(gram_of(block), ALL_GROUPS, cid))

    def backward_partial(basis):
        operand = (row_scale[:, None] * basis).astype(jnp.bfloat16)
        gathered = lax.all_gather(operand, FEAT, axis=0, tiled=True)
        return backward_local(tiles_here, scale_here, rows_here, cols_here, gathered, col_count)

    u_first, b_first = row_orthonormal(row_scale[:, None] * first_sums, 1)
    summed = claim_halving(backward_partial(u_first), True, 4).reshape(-1, u_first.shape[-1])
    update = col_scale[:, None] * summed - jnp.dot(first_basis, b_first.T, precision=HIGH)
    v_second, a_second = orthonormal(update, lax.psum(gram_of(update), FEAT))
    scaled = (col_scale[:, None] * v_second).astype(jnp.bfloat16)
    second_partial = forward_local(tiles_here, scale_here, rows_here, cols_here, scaled)
    second_sums = lax.psum_scatter(second_partial, FEAT, scatter_dimension=0, tiled=True)
    p_second = row_scale[:, None] * second_sums - jnp.dot(u_first, a_second.T, precision=HIGH)
    u_second, b_second = row_orthonormal(p_second, 2)
    own_sums = claim_scatter(backward_partial(u_second))
    own_scale = lax.dynamic_slice_in_dim(col_scale, own_first, own_cols, 0)
    own_second = lax.dynamic_slice_in_dim(v_second, own_first, own_cols, 0)
    q_second = own_scale[:, None] * own_sums - jnp.dot(own_second, b_second.T, precision=HIGH)
    v_output, a_third = orthonormal(q_second, group_sum(gram_of(q_second), ALL_GROUPS, 3))
    bidiagonal = jnp.stack([b_first, a_second, b_second, a_third])
    return (u_second, v_output, bidiagonal)


def solution(mesh):
    claim_n, feat_n = mesh.devices.shape
    fine = Mesh(mesh.devices.reshape(2, claim_n // 16, 8, 2, feat_n // 2), FINE)
    placed = (
        P(CLAIM, FEAT, None, None, None),
        P(CLAIM, FEAT, None),
        P(CLAIM, FEAT, None),
        P(CLAIM, FEAT, None),
        P(FEAT, None),
    )
    return jax.shard_map(
        per_device,
        mesh=fine,
        in_specs=placed,
        out_specs=(P(CLAIM + FEAT, None), P(FEAT + CLAIM, None), P()),
        check_vma=False,
    )
```

```python
import functools

import jax
import jax.numpy as jnp
from jax import lax
from jax.experimental import pallas as pl
from jax.experimental.pallas import tpu as pltpu
from jax.sharding import Mesh
from jax.sharding import PartitionSpec as P

BLK_ROWS = 64

HIGH = lax.Precision.HIGHEST

FINE = ("yh", "x", "z", "yl", "c")
CLAIM = ("yh", "x", "z")
FEAT = ("yl", "c")


TILES_PER_STEP = 16


def forward_kernel(rows_ref, cols_ref, scale_ref, tiles_ref, operand_ref, out_ref):
    step = pl.program_id(0)
    edge = tiles_ref.shape[-1]

    @pl.when(step == 0)
    def _():
        out_ref[...] = jnp.zeros_like(out_ref)

    for t in range(tiles_ref.shape[0]):
        b = step * tiles_ref.shape[0] + t
        picked = operand_ref[pl.ds(pl.multiple_of(cols_ref[b] * edge, edge), edge), :]
        product = jnp.dot(tiles_ref[t], picked, preferred_element_type=jnp.float32) * scale_ref[b]
        target = pl.ds(pl.multiple_of(rows_ref[b] * edge, edge), edge)
        out_ref[target, :] = out_ref[target, :] + product


def backward_kernel(rows_ref, cols_ref, scale_ref, tiles_ref, operand_ref, out_ref):
    step = pl.program_id(0)
    edge = tiles_ref.shape[-1]

    @pl.when(step == 0)
    def _():
        out_ref[...] = jnp.zeros_like(out_ref)

    for t in range(tiles_ref.shape[0]):
        b = step * tiles_ref.shape[0] + t
        picked = operand_ref[:, pl.ds(pl.multiple_of(rows_ref[b] * edge, edge), edge)]
        product = jnp.dot(picked, tiles_ref[t], preferred_element_type=jnp.float32) * scale_ref[b]
        target = pl.ds(pl.multiple_of(cols_ref[b] * edge, edge), edge)
        out_ref[:, target] = out_ref[:, target] + product


def block_product(kernel, block_tiles, block_scale, row_index, col_index, operand, out_shape):
    count, edge, _ = block_tiles.shape
    per = TILES_PER_STEP
    grid_spec = pltpu.PrefetchScalarGridSpec(
        num_scalar_prefetch=2,
        grid=(count // per,),
        in_specs=[
            pl.BlockSpec(memory_space=pltpu.SMEM),
            pl.BlockSpec((per, edge, edge), lambda i, rows, cols: (i, 0, 0)),
            pl.BlockSpec(operand.shape, lambda i, rows, cols: (0, 0)),
        ],
        out_specs=pl.BlockSpec(out_shape, lambda i, rows, cols: (0, 0)),
    )
    width = min(operand.shape)
    return pl.pallas_call(
        kernel,
        grid_spec=grid_spec,
        out_shape=jax.ShapeDtypeStruct(out_shape, jnp.float32),
        cost_estimate=pl.CostEstimate(
            flops=2 * count * edge * edge * width,
            bytes_accessed=block_tiles.size * 2 + operand.size * 2 + out_shape[0] * out_shape[1] * 4,
            transcendentals=0,
        ),
    )(row_index, col_index, block_scale, block_tiles, operand)


def forward_local(block_tiles, block_scale, row_index, col_index, operand):
    edge = block_tiles.shape[-1]
    out_shape = (BLK_ROWS * edge, operand.shape[-1])
    return block_product(forward_kernel, block_tiles, block_scale, row_index, col_index, operand, out_shape)


def backward_local(block_tiles, block_scale, row_index, col_index, operand, col_count):
    edge = block_tiles.shape[-1]
    out_shape = (operand.shape[-1], col_count * edge)
    flipped = block_product(
        backward_kernel, block_tiles, block_scale, row_index, col_index, operand.T, out_shape
    )
    return flipped.T


def degree_local(block_tiles, block_scale, row_index, col_index, col_count):
    row_sums = jnp.sum(block_tiles, axis=2, dtype=jnp.float32) * block_scale[:, None]
    col_sums = jnp.sum(block_tiles, axis=1, dtype=jnp.float32) * block_scale[:, None]
    row_select = (row_index[None, :] == jnp.arange(BLK_ROWS, dtype=jnp.int32)[:, None]).astype(
        jnp.float32
    )
    col_select = (col_index[None, :] == jnp.arange(col_count, dtype=jnp.int32)[:, None]).astype(
        jnp.float32
    )
    row_part = jnp.einsum("rb,bi->ri", row_select, row_sums, precision=HIGH).reshape(-1)
    col_part = jnp.einsum("cb,bi->ci", col_select, col_sums, precision=HIGH).reshape(-1)
    return (row_part, col_part)


def gram_of(block):
    return jnp.dot(block.T, block, precision=HIGH)


def factor_kernel(g_ref, o_ref):
    n = g_ref.shape[0]
    o_ref[:, :n] = g_ref[...]
    rows = lax.broadcasted_iota(jnp.int32, (n, 2 * n), 0)
    cols = lax.broadcasted_iota(jnp.int32, (n, 2 * n), 1)
    o_ref[:, n:] = jnp.where(rows[:, n:] == cols[:, n:] - n, 1.0, 0.0).astype(o_ref.dtype)
    m = o_ref[...]
    below = lax.broadcasted_iota(jnp.int32, (n, 1), 0)
    for j in range(n):
        factor = jnp.where(below > j, m[:, j : j + 1] / m[j : j + 1, j : j + 1], 0.0)
        m = m - factor * m[j : j + 1, :]
    diagonal = jnp.sum(jnp.where(rows == cols, m, 0.0), axis=1, keepdims=True)
    m = m * lax.rsqrt(diagonal)
    o_ref[...] = jnp.where((cols < n) & (cols < rows), 0.0, m)


def orthonormal(block, gram_total):
    n = gram_total.shape[0]
    both = pl.pallas_call(
        factor_kernel,
        out_shape=jax.ShapeDtypeStruct((n, 2 * n), jnp.float32),
        in_specs=[pl.BlockSpec(memory_space=pltpu.VMEM)],
        out_specs=pl.BlockSpec(memory_space=pltpu.VMEM),
    )(gram_total)
    upper, inverse = both[:, :n], both[:, n:]
    basis = jnp.dot(block, inverse.T, precision=HIGH)
    return (basis, upper)


def group_kernel(groups, x_ref, o_ref, slots, send_sem, recv_sem):
    coords = [lax.axis_index(name) for name in FINE]
    plans = []
    for axes, sizes in groups:
        count = 1
        for size in sizes:
            count *= size
        me = 0
        for axis, size in zip(axes, sizes):
            me = me * size + coords[axis]
        targets = []
        for k in range(1, count):
            member = (me + k) % count
            place = list(coords)
            rest = member
            for axis, size in reversed(list(zip(axes, sizes))):
                place[axis] = rest % size
                rest = rest // size
            targets.append((tuple(place), (me + count - k) % count))
        plans.append((count, me, targets))
    barrier = pltpu.get_barrier_semaphore()
    total = 0
    for count, me, targets in plans:
        for place, _ in targets:
            pl.semaphore_signal(barrier, inc=1, device_id=place, device_id_type=pl.DeviceIdType.MESH)
        total += len(targets)
    pl.semaphore_wait(barrier, total)
    o_ref[...] = x_ref[...]
    for g, (count, me, targets) in enumerate(plans):
        slots[g, me] = o_ref[...]
        copies = []
        for k, (place, _) in enumerate(targets):
            copy = pltpu.make_async_remote_copy(
                src_ref=o_ref,
                dst_ref=slots.at[g, me],
                send_sem=send_sem.at[g, k],
                recv_sem=recv_sem.at[g, me],
                device_id=place,
                device_id_type=pl.DeviceIdType.MESH,
            )
            copy.start()
            copies.append(copy)
        for copy in copies:
            copy.wait_send()
        for place, sender in targets:
            pltpu.make_async_remote_copy(
                src_ref=o_ref,
                dst_ref=slots.at[g, sender],
                send_sem=send_sem.at[g, 0],
                recv_sem=recv_sem.at[g, sender],
                device_id=place,
                device_id_type=pl.DeviceIdType.MESH,
            ).wait_recv()
        acc = slots[g, 0]
        for j in range(1, count):
            acc = acc + slots[g, j]
        o_ref[...] = acc


def group_sum(value, groups, cid):
    spec = []
    widest = 1
    for names in groups:
        sizes = tuple(lax.axis_size(name) for name in names)
        count = 1
        for size in sizes:
            count *= size
        widest = max(widest, count)
        spec.append((tuple(FINE.index(name) for name in names), sizes))
    shape = value.shape
    flat = value.reshape(-1, 128) if value.ndim == 1 else value
    out = pl.pallas_call(
        functools.partial(group_kernel, tuple(spec)),
        out_shape=jax.ShapeDtypeStruct(flat.shape, flat.dtype),
        in_specs=[pl.BlockSpec(memory_space=pltpu.VMEM)],
        out_specs=pl.BlockSpec(memory_space=pltpu.VMEM),
        scratch_shapes=[
            pltpu.VMEM((len(spec), widest) + flat.shape, flat.dtype),
            pltpu.SemaphoreType.DMA((len(spec), widest)),
            pltpu.SemaphoreType.DMA((len(spec), widest)),
        ],
        compiler_params=pltpu.CompilerParams(collective_id=cid, has_side_effects=True),
    )(flat)
    return out.reshape(shape)


ALL_GROUPS = (FEAT, ("z",), ("yh", "x"))
CLAIM_GROUPS = (("z",), ("yh", "x"))


def halving_kernel(stages, gather, x_ref, o_ref, *scratch):
    if gather:
        work, recv, back, rs_send, rs_recv, ag_send, ag_recv = o_ref, *scratch
    else:
        work, recv, rs_send, rs_recv = scratch
    coords = [lax.axis_index(name) for name in FINE]
    partners, bits = [], []
    for axis, step in stages:
        place = coords[axis]
        bit = (place // step) % 2
        flip = place + step * (1 - 2 * bit)
        partners.append(tuple(flip if i == axis else c for i, c in enumerate(coords)))
        bits.append(bit)
    barrier = pltpu.get_barrier_semaphore()
    for partner in partners:
        pl.semaphore_signal(barrier, inc=1, device_id=partner, device_id_type=pl.DeviceIdType.MESH)
    pl.semaphore_wait(barrier, len(partners))
    work[...] = x_ref[...]
    total = work.shape[0]
    base = 0
    pieces = []
    for s, partner in enumerate(partners):
        size = total >> s
        half = size // 2
        keep = base + bits[s] * half
        give = base + (1 - bits[s]) * half
        slot = pl.ds(total - size, half)
        copy = pltpu.make_async_remote_copy(
            src_ref=work.at[pl.ds(give, half)],
            dst_ref=recv.at[slot],
            send_sem=rs_send.at[s],
            recv_sem=rs_recv.at[s],
            device_id=partner,
            device_id_type=pl.DeviceIdType.MESH,
        )
        copy.start()
        copy.wait()
        work[pl.ds(keep, half), :] = work[pl.ds(keep, half), :] + recv[slot, :]
        pieces.append((keep, give, slot))
        base = keep
    if gather:
        for s in reversed(range(len(partners))):
            keep, give, slot = pieces[s]
            copy = pltpu.make_async_remote_copy(
                src_ref=work.at[pl.ds(keep, slot.size)],
                dst_ref=back.at[slot],
                send_sem=ag_send.at[s],
                recv_sem=ag_recv.at[s],
                device_id=partners[s],
                device_id_type=pl.DeviceIdType.MESH,
            )
            copy.start()
            copy.wait()
            work[pl.ds(give, slot.size), :] = back[slot, :]
    else:
        o_ref[...] = work[pl.ds(base, o_ref.shape[0]), :]


CLAIM_STAGES = (("z", 1), ("x", 1), ("z", 2), ("x", 2), ("yh", 1), ("z", 4))


def claim_halving(value, gather, cid):
    stages = tuple((FINE.index(name), step) for name, step in CLAIM_STAGES)
    count = len(stages)
    flat = value.reshape(-1, 128)
    rows = flat.shape[0]
    out_rows = rows if gather else rows >> count
    scratch = [] if gather else [pltpu.VMEM(flat.shape, flat.dtype)]
    scratch += [pltpu.VMEM(flat.shape, flat.dtype)] * (2 if gather else 1)
    scratch += [pltpu.SemaphoreType.DMA((count,))] * (4 if gather else 2)
    out = pl.pallas_call(
        functools.partial(halving_kernel, stages, gather),
        out_shape=jax.ShapeDtypeStruct((out_rows, 128), flat.dtype),
        in_specs=[pl.BlockSpec(memory_space=pltpu.VMEM)],
        out_specs=pl.BlockSpec(memory_space=pltpu.VMEM),
        scratch_shapes=scratch,
        compiler_params=pltpu.CompilerParams(collective_id=cid, has_side_effects=True),
    )(flat)
    return out


def claim_sum(value):
    part = lax.psum_scatter(value, "z", scatter_dimension=0, tiled=True)
    part = lax.psum(part, ("yh", "x"))
    return lax.all_gather(part, "z", axis=0, tiled=True)


def all_sum(value):
    value = lax.psum(value, FEAT)
    value = lax.psum(value, "z")
    return lax.psum(value, ("yh", "x"))


def claim_scatter(value):
    width = value.shape[-1]
    rows = value.shape[0] // lax.axis_size(CLAIM)
    bits = value.reshape(2, 2, 2, 2, 2, 2, rows, width)
    ordered = bits.transpose(5, 2, 4, 1, 0, 3, 6, 7).reshape(value.shape)
    return claim_halving(ordered, False, 5).reshape(rows, width)


def per_device(block_tiles, block_scale, row_index, col_index, start_basis):
    tiles_here = block_tiles.reshape(block_tiles.shape[-3:])
    scale_here = block_scale.reshape(-1)
    rows_here = row_index.reshape(-1)
    cols_here = col_index.reshape(-1)
    edge = tiles_here.shape[-1]
    col_count = start_basis.shape[0] // edge
    claim_count = lax.axis_size(CLAIM)
    own_cols = start_basis.shape[0] // claim_count
    own_first = lax.axis_index(CLAIM) * own_cols
    row_part, col_part = degree_local(tiles_here, scale_here, rows_here, cols_here, col_count)
    col_total = group_sum(col_part, CLAIM_GROUPS, 0)
    col_scale = lax.rsqrt(col_total + 1.0)
    row_total = lax.psum_scatter(row_part, FEAT, scatter_dimension=0, tiled=True)
    start_total = lax.psum(gram_of(start_basis), FEAT)
    first_basis, _ = orthonormal(start_basis, start_total)
    first_operand = (col_scale[:, None] * first_basis).astype(jnp.bfloat16)
    first_partial = forward_local(tiles_here, scale_here, rows_here, cols_here, first_operand)
    first_sums = lax.psum_scatter(first_partial, FEAT, scatter_dimension=0, tiled=True)
    row_scale = lax.rsqrt(row_total + 1.0)

    def row_orthonormal(block, cid):
        return orthonormal(block, group_sum(gram_of(block), ALL_GROUPS, cid))

    def backward_partial(basis):
        operand = (row_scale[:, None] * basis).astype(jnp.bfloat16)
        gathered = lax.all_gather(operand, FEAT, axis=0, tiled=True)
        return backward_local(tiles_here, scale_here, rows_here, cols_here, gathered, col_count)

    u_first, b_first = row_orthonormal(row_scale[:, None] * first_sums, 1)
    summed = claim_halving(backward_partial(u_first), True, 4).reshape(-1, u_first.shape[-1])
    update = col_scale[:, None] * summed - jnp.dot(first_basis, b_first.T, precision=HIGH)
    v_second, a_second = orthonormal(update, lax.psum(gram_of(update), FEAT))
    scaled = (col_scale[:, None] * v_second).astype(jnp.bfloat16)
    second_partial = forward_local(tiles_here, scale_here, rows_here, cols_here, scaled)
    second_sums = lax.psum_scatter(second_partial, FEAT, scatter_dimension=0, tiled=True)
    p_second = row_scale[:, None] * second_sums - jnp.dot(u_first, a_second.T, precision=HIGH)
    u_second, b_second = row_orthonormal(p_second, 2)
    own_sums = claim_scatter(backward_partial(u_second))
    own_scale = lax.dynamic_slice_in_dim(col_scale, own_first, own_cols, 0)
    own_second = lax.dynamic_slice_in_dim(v_second, own_first, own_cols, 0)
    q_second = own_scale[:, None] * own_sums - jnp.dot(own_second, b_second.T, precision=HIGH)
    v_output, a_third = orthonormal(q_second, group_sum(gram_of(q_second), ALL_GROUPS, 3))
    bidiagonal = jnp.stack([b_first, a_second, b_second, a_third])
    return (u_second, v_output, bidiagonal)


def solution(mesh):
    claim_n, feat_n = mesh.devices.shape
    fine = Mesh(mesh.devices.reshape(2, claim_n // 16, 8, 2, feat_n // 2), FINE)
    placed = (
        P(CLAIM, FEAT, None, None, None),
        P(CLAIM, FEAT, None),
        P(CLAIM, FEAT, None),
        P(CLAIM, FEAT, None),
        P(FEAT, None),
    )
    return jax.shard_map(
        per_device,
        mesh=fine,
        in_specs=placed,
        out_specs=(P(CLAIM + FEAT, None), P(FEAT + CLAIM, None), P()),
        check_vma=False,
    )
```

```python
import functools

import jax
import jax.numpy as jnp
from jax import lax
from jax.experimental import pallas as pl
from jax.experimental.pallas import tpu as pltpu
from jax.sharding import Mesh
from jax.sharding import PartitionSpec as P

BLK_ROWS = 64

HIGH = lax.Precision.HIGHEST

FINE = ("yh", "x", "z", "yl", "c")
CLAIM = ("yh", "x", "z")
FEAT = ("yl", "c")


TILES_PER_STEP = 16


def forward_kernel(rows_ref, cols_ref, scale_ref, tiles_ref, operand_ref, out_ref):
    step = pl.program_id(0)
    edge = tiles_ref.shape[-1]

    @pl.when(step == 0)
    def _():
        out_ref[...] = jnp.zeros_like(out_ref)

    for t in range(tiles_ref.shape[0]):
        b = step * tiles_ref.shape[0] + t
        picked = operand_ref[pl.ds(pl.multiple_of(cols_ref[b] * edge, edge), edge), :]
        product = jnp.dot(tiles_ref[t], picked, preferred_element_type=jnp.float32) * scale_ref[b]
        target = pl.ds(pl.multiple_of(rows_ref[b] * edge, edge), edge)
        out_ref[target, :] = out_ref[target, :] + product


def backward_kernel(rows_ref, cols_ref, scale_ref, tiles_ref, operand_ref, out_ref):
    step = pl.program_id(0)
    edge = tiles_ref.shape[-1]

    @pl.when(step == 0)
    def _():
        out_ref[...] = jnp.zeros_like(out_ref)

    for t in range(tiles_ref.shape[0]):
        b = step * tiles_ref.shape[0] + t
        picked = operand_ref[:, pl.ds(pl.multiple_of(rows_ref[b] * edge, edge), edge)]
        product = jnp.dot(picked, tiles_ref[t], preferred_element_type=jnp.float32) * scale_ref[b]
        target = pl.ds(pl.multiple_of(cols_ref[b] * edge, edge), edge)
        out_ref[:, target] = out_ref[:, target] + product


def block_product(kernel, block_tiles, block_scale, row_index, col_index, operand, out_shape):
    count, edge, _ = block_tiles.shape
    per = TILES_PER_STEP
    grid_spec = pltpu.PrefetchScalarGridSpec(
        num_scalar_prefetch=2,
        grid=(count // per,),
        in_specs=[
            pl.BlockSpec(memory_space=pltpu.SMEM),
            pl.BlockSpec((per, edge, edge), lambda i, rows, cols: (i, 0, 0)),
            pl.BlockSpec(operand.shape, lambda i, rows, cols: (0, 0)),
        ],
        out_specs=pl.BlockSpec(out_shape, lambda i, rows, cols: (0, 0)),
    )
    width = min(operand.shape)
    return pl.pallas_call(
        kernel,
        grid_spec=grid_spec,
        out_shape=jax.ShapeDtypeStruct(out_shape, jnp.float32),
        cost_estimate=pl.CostEstimate(
            flops=2 * count * edge * edge * width,
            bytes_accessed=block_tiles.size * 2 + operand.size * 2 + out_shape[0] * out_shape[1] * 4,
            transcendentals=0,
        ),
    )(row_index, col_index, block_scale, block_tiles, operand)


def forward_local(block_tiles, block_scale, row_index, col_index, operand):
    edge = block_tiles.shape[-1]
    out_shape = (BLK_ROWS * edge, operand.shape[-1])
    return block_product(forward_kernel, block_tiles, block_scale, row_index, col_index, operand, out_shape)


def backward_local(block_tiles, block_scale, row_index, col_index, operand, col_count):
    edge = block_tiles.shape[-1]
    out_shape = (operand.shape[-1], col_count * edge)
    flipped = block_product(
        backward_kernel, block_tiles, block_scale, row_index, col_index, operand.T, out_shape
    )
    return flipped.T


def degree_local(block_tiles, block_scale, row_index, col_index, col_count):
    row_sums = jnp.sum(block_tiles, axis=2, dtype=jnp.float32) * block_scale[:, None]
    col_sums = jnp.sum(block_tiles, axis=1, dtype=jnp.float32) * block_scale[:, None]
    row_select = (row_index[None, :] == jnp.arange(BLK_ROWS, dtype=jnp.int32)[:, None]).astype(
        jnp.float32
    )
    col_select = (col_index[None, :] == jnp.arange(col_count, dtype=jnp.int32)[:, None]).astype(
        jnp.float32
    )
    row_part = jnp.einsum("rb,bi->ri", row_select, row_sums, precision=HIGH).reshape(-1)
    col_part = jnp.einsum("cb,bi->ci", col_select, col_sums, precision=HIGH).reshape(-1)
    return (row_part, col_part)


def gram_of(block):
    return jnp.dot(block.T, block, precision=HIGH)


def factor_kernel(g_ref, o_ref):
    n = g_ref.shape[0]
    o_ref[:, :n] = g_ref[...]
    rows = lax.broadcasted_iota(jnp.int32, (n, 2 * n), 0)
    cols = lax.broadcasted_iota(jnp.int32, (n, 2 * n), 1)
    o_ref[:, n:] = jnp.where(rows[:, n:] == cols[:, n:] - n, 1.0, 0.0).astype(o_ref.dtype)
    m = o_ref[...]
    below = lax.broadcasted_iota(jnp.int32, (n, 1), 0)
    for j in range(n):
        factor = jnp.where(below > j, m[:, j : j + 1], 0.0) * (1.0 / m[j : j + 1, j : j + 1])
        m = m - factor * m[j : j + 1, :]
    diagonal = jnp.sum(jnp.where(rows == cols, m, 0.0), axis=1, keepdims=True)
    m = m * lax.rsqrt(diagonal)
    o_ref[...] = jnp.where((cols < n) & (cols < rows), 0.0, m)


def orthonormal(block, gram_total):
    n = gram_total.shape[0]
    both = pl.pallas_call(
        factor_kernel,
        out_shape=jax.ShapeDtypeStruct((n, 2 * n), jnp.float32),
        in_specs=[pl.BlockSpec(memory_space=pltpu.VMEM)],
        out_specs=pl.BlockSpec(memory_space=pltpu.VMEM),
    )(gram_total)
    upper, inverse = both[:, :n], both[:, n:]
    basis = jnp.dot(block, inverse.T, precision=HIGH)
    return (basis, upper)


def group_kernel(groups, x_ref, o_ref, slots, send_sem, recv_sem):
    coords = [lax.axis_index(name) for name in FINE]
    plans = []
    for axes, sizes in groups:
        count = 1
        for size in sizes:
            count *= size
        me = 0
        for axis, size in zip(axes, sizes):
            me = me * size + coords[axis]
        targets = []
        for k in range(1, count):
            member = (me + k) % count
            place = list(coords)
            rest = member
            for axis, size in reversed(list(zip(axes, sizes))):
                place[axis] = rest % size
                rest = rest // size
            targets.append((tuple(place), (me + count - k) % count))
        plans.append((count, me, targets))
    barrier = pltpu.get_barrier_semaphore()
    total = 0
    for count, me, targets in plans:
        for place, _ in targets:
            pl.semaphore_signal(barrier, inc=1, device_id=place, device_id_type=pl.DeviceIdType.MESH)
        total += len(targets)
    pl.semaphore_wait(barrier, total)
    o_ref[...] = x_ref[...]
    for g, (count, me, targets) in enumerate(plans):
        slots[g, me] = o_ref[...]
        copies = []
        for k, (place, _) in enumerate(targets):
            copy = pltpu.make_async_remote_copy(
                src_ref=o_ref,
                dst_ref=slots.at[g, me],
                send_sem=send_sem.at[g, k],
                recv_sem=recv_sem.at[g, me],
                device_id=place,
                device_id_type=pl.DeviceIdType.MESH,
            )
            copy.start()
            copies.append(copy)
        for copy in copies:
            copy.wait_send()
        for place, sender in targets:
            pltpu.make_async_remote_copy(
                src_ref=o_ref,
                dst_ref=slots.at[g, sender],
                send_sem=send_sem.at[g, 0],
                recv_sem=recv_sem.at[g, sender],
                device_id=place,
                device_id_type=pl.DeviceIdType.MESH,
            ).wait_recv()
        acc = slots[g, 0]
        for j in range(1, count):
            acc = acc + slots[g, j]
        o_ref[...] = acc


def group_sum(value, groups, cid):
    spec = []
    widest = 1
    for names in groups:
        sizes = tuple(lax.axis_size(name) for name in names)
        count = 1
        for size in sizes:
            count *= size
        widest = max(widest, count)
        spec.append((tuple(FINE.index(name) for name in names), sizes))
    shape = value.shape
    flat = value.reshape(-1, 128) if value.ndim == 1 else value
    out = pl.pallas_call(
        functools.partial(group_kernel, tuple(spec)),
        out_shape=jax.ShapeDtypeStruct(flat.shape, flat.dtype),
        in_specs=[pl.BlockSpec(memory_space=pltpu.VMEM)],
        out_specs=pl.BlockSpec(memory_space=pltpu.VMEM),
        scratch_shapes=[
            pltpu.VMEM((len(spec), widest) + flat.shape, flat.dtype),
            pltpu.SemaphoreType.DMA((len(spec), widest)),
            pltpu.SemaphoreType.DMA((len(spec), widest)),
        ],
        compiler_params=pltpu.CompilerParams(collective_id=cid, has_side_effects=True),
    )(flat)
    return out.reshape(shape)


ALL_GROUPS = (FEAT, ("z",), ("yh", "x"))
CLAIM_GROUPS = (("z",), ("yh", "x"))


def halving_kernel(stages, gather, x_ref, o_ref, *scratch):
    if gather:
        work, recv, back, rs_send, rs_recv, ag_send, ag_recv = o_ref, *scratch
    else:
        work, recv, rs_send, rs_recv = scratch
    coords = [lax.axis_index(name) for name in FINE]
    partners, bits = [], []
    for axis, step in stages:
        place = coords[axis]
        bit = (place // step) % 2
        flip = place + step * (1 - 2 * bit)
        partners.append(tuple(flip if i == axis else c for i, c in enumerate(coords)))
        bits.append(bit)
    barrier = pltpu.get_barrier_semaphore()
    for partner in partners:
        pl.semaphore_signal(barrier, inc=1, device_id=partner, device_id_type=pl.DeviceIdType.MESH)
    pl.semaphore_wait(barrier, len(partners))
    work[...] = x_ref[...]
    total = work.shape[0]
    base = 0
    pieces = []
    for s, partner in enumerate(partners):
        size = total >> s
        half = size // 2
        keep = base + bits[s] * half
        give = base + (1 - bits[s]) * half
        slot = pl.ds(total - size, half)
        copy = pltpu.make_async_remote_copy(
            src_ref=work.at[pl.ds(give, half)],
            dst_ref=recv.at[slot],
            send_sem=rs_send.at[s],
            recv_sem=rs_recv.at[s],
            device_id=partner,
            device_id_type=pl.DeviceIdType.MESH,
        )
        copy.start()
        copy.wait()
        work[pl.ds(keep, half), :] = work[pl.ds(keep, half), :] + recv[slot, :]
        pieces.append((keep, give, slot))
        base = keep
    if gather:
        for s in reversed(range(len(partners))):
            keep, give, slot = pieces[s]
            copy = pltpu.make_async_remote_copy(
                src_ref=work.at[pl.ds(keep, slot.size)],
                dst_ref=back.at[slot],
                send_sem=ag_send.at[s],
                recv_sem=ag_recv.at[s],
                device_id=partners[s],
                device_id_type=pl.DeviceIdType.MESH,
            )
            copy.start()
            copy.wait()
            work[pl.ds(give, slot.size), :] = back[slot, :]
    else:
        o_ref[...] = work[pl.ds(base, o_ref.shape[0]), :]


CLAIM_STAGES = (("z", 1), ("x", 1), ("z", 2), ("x", 2), ("yh", 1), ("z", 4))


def claim_halving(value, gather, cid):
    stages = tuple((FINE.index(name), step) for name, step in CLAIM_STAGES)
    count = len(stages)
    flat = value.reshape(-1, 128)
    rows = flat.shape[0]
    out_rows = rows if gather else rows >> count
    scratch = [] if gather else [pltpu.VMEM(flat.shape, flat.dtype)]
    scratch += [pltpu.VMEM(flat.shape, flat.dtype)] * (2 if gather else 1)
    scratch += [pltpu.SemaphoreType.DMA((count,))] * (4 if gather else 2)
    out = pl.pallas_call(
        functools.partial(halving_kernel, stages, gather),
        out_shape=jax.ShapeDtypeStruct((out_rows, 128), flat.dtype),
        in_specs=[pl.BlockSpec(memory_space=pltpu.VMEM)],
        out_specs=pl.BlockSpec(memory_space=pltpu.VMEM),
        scratch_shapes=scratch,
        compiler_params=pltpu.CompilerParams(collective_id=cid, has_side_effects=True),
    )(flat)
    return out


def claim_sum(value):
    part = lax.psum_scatter(value, "z", scatter_dimension=0, tiled=True)
    part = lax.psum(part, ("yh", "x"))
    return lax.all_gather(part, "z", axis=0, tiled=True)


def all_sum(value):
    value = lax.psum(value, FEAT)
    value = lax.psum(value, "z")
    return lax.psum(value, ("yh", "x"))


def claim_scatter(value):
    width = value.shape[-1]
    rows = value.shape[0] // lax.axis_size(CLAIM)
    bits = value.reshape(2, 2, 2, 2, 2, 2, rows, width)
    ordered = bits.transpose(5, 2, 4, 1, 0, 3, 6, 7).reshape(value.shape)
    return claim_halving(ordered, False, 5).reshape(rows, width)


def per_device(block_tiles, block_scale, row_index, col_index, start_basis):
    tiles_here = block_tiles.reshape(block_tiles.shape[-3:])
    scale_here = block_scale.reshape(-1)
    rows_here = row_index.reshape(-1)
    cols_here = col_index.reshape(-1)
    edge = tiles_here.shape[-1]
    col_count = start_basis.shape[0] // edge
    claim_count = lax.axis_size(CLAIM)
    own_cols = start_basis.shape[0] // claim_count
    own_first = lax.axis_index(CLAIM) * own_cols
    row_part, col_part = degree_local(tiles_here, scale_here, rows_here, cols_here, col_count)
    col_total = group_sum(col_part, CLAIM_GROUPS, 0)
    col_scale = lax.rsqrt(col_total + 1.0)
    row_total = lax.psum_scatter(row_part, FEAT, scatter_dimension=0, tiled=True)
    start_total = lax.psum(gram_of(start_basis), FEAT)
    first_basis, _ = orthonormal(start_basis, start_total)
    first_operand = (col_scale[:, None] * first_basis).astype(jnp.bfloat16)
    first_partial = forward_local(tiles_here, scale_here, rows_here, cols_here, first_operand)
    first_sums = lax.psum_scatter(first_partial, FEAT, scatter_dimension=0, tiled=True)
    row_scale = lax.rsqrt(row_total + 1.0)

    def row_orthonormal(block, cid):
        return orthonormal(block, group_sum(gram_of(block), ALL_GROUPS, cid))

    def backward_partial(basis):
        operand = (row_scale[:, None] * basis).astype(jnp.bfloat16)
        gathered = lax.all_gather(operand, FEAT, axis=0, tiled=True)
        return backward_local(tiles_here, scale_here, rows_here, cols_here, gathered, col_count)

    u_first, b_first = row_orthonormal(row_scale[:, None] * first_sums, 1)
    summed = claim_halving(backward_partial(u_first), True, 4).reshape(-1, u_first.shape[-1])
    update = col_scale[:, None] * summed - jnp.dot(first_basis, b_first.T, precision=HIGH)
    v_second, a_second = orthonormal(update, lax.psum(gram_of(update), FEAT))
    scaled = (col_scale[:, None] * v_second).astype(jnp.bfloat16)
    second_partial = forward_local(tiles_here, scale_here, rows_here, cols_here, scaled)
    second_sums = lax.psum_scatter(second_partial, FEAT, scatter_dimension=0, tiled=True)
    p_second = row_scale[:, None] * second_sums - jnp.dot(u_first, a_second.T, precision=HIGH)
    u_second, b_second = row_orthonormal(p_second, 2)
    own_sums = claim_scatter(backward_partial(u_second))
    own_scale = lax.dynamic_slice_in_dim(col_scale, own_first, own_cols, 0)
    own_second = lax.dynamic_slice_in_dim(v_second, own_first, own_cols, 0)
    q_second = own_scale[:, None] * own_sums - jnp.dot(own_second, b_second.T, precision=HIGH)
    v_output, a_third = orthonormal(q_second, group_sum(gram_of(q_second), ALL_GROUPS, 3))
    bidiagonal = jnp.stack([b_first, a_second, b_second, a_third])
    return (u_second, v_output, bidiagonal)


def solution(mesh):
    claim_n, feat_n = mesh.devices.shape
    fine = Mesh(mesh.devices.reshape(2, claim_n // 16, 8, 2, feat_n // 2), FINE)
    placed = (
        P(CLAIM, FEAT, None, None, None),
        P(CLAIM, FEAT, None),
        P(CLAIM, FEAT, None),
        P(CLAIM, FEAT, None),
        P(FEAT, None),
    )
    return jax.shard_map(
        per_device,
        mesh=fine,
        in_specs=placed,
        out_specs=(P(CLAIM + FEAT, None), P(FEAT + CLAIM, None), P()),
        check_vma=False,
    )
```

```python
import functools

import jax
import jax.numpy as jnp
from jax import lax
from jax.experimental import pallas as pl
from jax.experimental.pallas import tpu as pltpu
from jax.sharding import Mesh
from jax.sharding import PartitionSpec as P

BLK_ROWS = 64

HIGH = lax.Precision.HIGHEST

FINE = ("yh", "x", "z", "yl", "c")
CLAIM = ("yh", "x", "z")
FEAT = ("yl", "c")


TILES_PER_STEP = 16


def forward_kernel(rows_ref, cols_ref, scale_ref, tiles_ref, operand_ref, out_ref):
    step = pl.program_id(0)
    edge = tiles_ref.shape[-1]

    @pl.when(step == 0)
    def _():
        out_ref[...] = jnp.zeros_like(out_ref)

    for t in range(tiles_ref.shape[0]):
        b = step * tiles_ref.shape[0] + t
        picked = operand_ref[:, pl.ds(pl.multiple_of(cols_ref[b] * edge, edge), edge)]
        product = lax.dot_general(
            picked, tiles_ref[t], (((1,), (1,)), ((), ())), preferred_element_type=jnp.float32
        )
        target = pl.ds(pl.multiple_of(rows_ref[b] * edge, edge), edge)
        out_ref[:, target] = out_ref[:, target] + product * scale_ref[b]


def backward_kernel(rows_ref, cols_ref, scale_ref, tiles_ref, operand_ref, out_ref):
    step = pl.program_id(0)
    edge = tiles_ref.shape[-1]

    @pl.when(step == 0)
    def _():
        out_ref[...] = jnp.zeros_like(out_ref)

    for t in range(tiles_ref.shape[0]):
        b = step * tiles_ref.shape[0] + t
        picked = operand_ref[:, pl.ds(pl.multiple_of(rows_ref[b] * edge, edge), edge)]
        product = jnp.dot(picked, tiles_ref[t], preferred_element_type=jnp.float32) * scale_ref[b]
        target = pl.ds(pl.multiple_of(cols_ref[b] * edge, edge), edge)
        out_ref[:, target] = out_ref[:, target] + product


def block_product(kernel, block_tiles, block_scale, row_index, col_index, operand, out_shape):
    count, edge, _ = block_tiles.shape
    per = TILES_PER_STEP
    grid_spec = pltpu.PrefetchScalarGridSpec(
        num_scalar_prefetch=2,
        grid=(count // per,),
        in_specs=[
            pl.BlockSpec(memory_space=pltpu.SMEM),
            pl.BlockSpec((per, edge, edge), lambda i, rows, cols: (i, 0, 0)),
            pl.BlockSpec(operand.shape, lambda i, rows, cols: (0, 0)),
        ],
        out_specs=pl.BlockSpec(out_shape, lambda i, rows, cols: (0, 0)),
    )
    width = min(operand.shape)
    return pl.pallas_call(
        kernel,
        grid_spec=grid_spec,
        out_shape=jax.ShapeDtypeStruct(out_shape, jnp.float32),
        cost_estimate=pl.CostEstimate(
            flops=2 * count * edge * edge * width,
            bytes_accessed=block_tiles.size * 2 + operand.size * 2 + out_shape[0] * out_shape[1] * 4,
            transcendentals=0,
        ),
    )(row_index, col_index, block_scale, block_tiles, operand)


def forward_local(block_tiles, block_scale, row_index, col_index, operand):
    edge = block_tiles.shape[-1]
    out_shape = (operand.shape[-1], BLK_ROWS * edge)
    return block_product(
        forward_kernel, block_tiles, block_scale, row_index, col_index, operand.T, out_shape
    )


def backward_local(block_tiles, block_scale, row_index, col_index, operand, col_count):
    edge = block_tiles.shape[-1]
    out_shape = (operand.shape[-1], col_count * edge)
    flipped = block_product(
        backward_kernel, block_tiles, block_scale, row_index, col_index, operand.T, out_shape
    )
    return flipped.T


def degree_local(block_tiles, block_scale, row_index, col_index, col_count):
    row_sums = jnp.sum(block_tiles, axis=2, dtype=jnp.float32) * block_scale[:, None]
    col_sums = jnp.sum(block_tiles, axis=1, dtype=jnp.float32) * block_scale[:, None]
    row_select = (row_index[None, :] == jnp.arange(BLK_ROWS, dtype=jnp.int32)[:, None]).astype(
        jnp.float32
    )
    col_select = (col_index[None, :] == jnp.arange(col_count, dtype=jnp.int32)[:, None]).astype(
        jnp.float32
    )
    row_part = jnp.einsum("rb,bi->ri", row_select, row_sums, precision=HIGH).reshape(-1)
    col_part = jnp.einsum("cb,bi->ci", col_select, col_sums, precision=HIGH).reshape(-1)
    return (row_part, col_part)


def gram_of(block):
    return jnp.dot(block.T, block, precision=HIGH)


def factor_kernel(g_ref, o_ref):
    n = g_ref.shape[0]
    o_ref[:, :n] = g_ref[...]
    rows = lax.broadcasted_iota(jnp.int32, (n, 2 * n), 0)
    cols = lax.broadcasted_iota(jnp.int32, (n, 2 * n), 1)
    o_ref[:, n:] = jnp.where(rows[:, n:] == cols[:, n:] - n, 1.0, 0.0).astype(o_ref.dtype)
    m = o_ref[...]
    below = lax.broadcasted_iota(jnp.int32, (n, 1), 0)
    for j in range(n):
        factor = jnp.where(below > j, m[:, j : j + 1], 0.0) * (1.0 / m[j : j + 1, j : j + 1])
        m = m - factor * m[j : j + 1, :]
    diagonal = jnp.sum(jnp.where(rows == cols, m, 0.0), axis=1, keepdims=True)
    m = m * lax.rsqrt(diagonal)
    o_ref[...] = jnp.where((cols < n) & (cols < rows), 0.0, m)


def orthonormal(block, gram_total):
    n = gram_total.shape[0]
    both = pl.pallas_call(
        factor_kernel,
        out_shape=jax.ShapeDtypeStruct((n, 2 * n), jnp.float32),
        in_specs=[pl.BlockSpec(memory_space=pltpu.VMEM)],
        out_specs=pl.BlockSpec(memory_space=pltpu.VMEM),
    )(gram_total)
    upper, inverse = both[:, :n], both[:, n:]
    basis = jnp.dot(block, inverse.T, precision=HIGH)
    return (basis, upper)


def group_kernel(groups, x_ref, o_ref, slots, send_sem, recv_sem):
    coords = [lax.axis_index(name) for name in FINE]
    plans = []
    for axes, sizes in groups:
        count = 1
        for size in sizes:
            count *= size
        me = 0
        for axis, size in zip(axes, sizes):
            me = me * size + coords[axis]
        targets = []
        for k in range(1, count):
            member = (me + k) % count
            place = list(coords)
            rest = member
            for axis, size in reversed(list(zip(axes, sizes))):
                place[axis] = rest % size
                rest = rest // size
            targets.append((tuple(place), (me + count - k) % count))
        plans.append((count, me, targets))
    barrier = pltpu.get_barrier_semaphore()
    total = 0
    for count, me, targets in plans:
        for place, _ in targets:
            pl.semaphore_signal(barrier, inc=1, device_id=place, device_id_type=pl.DeviceIdType.MESH)
        total += len(targets)
    pl.semaphore_wait(barrier, total)
    o_ref[...] = x_ref[...]
    for g, (count, me, targets) in enumerate(plans):
        slots[g, me] = o_ref[...]
        copies = []
        for k, (place, _) in enumerate(targets):
            copy = pltpu.make_async_remote_copy(
                src_ref=o_ref,
                dst_ref=slots.at[g, me],
                send_sem=send_sem.at[g, k],
                recv_sem=recv_sem.at[g, me],
                device_id=place,
                device_id_type=pl.DeviceIdType.MESH,
            )
            copy.start()
            copies.append(copy)
        for copy in copies:
            copy.wait_send()
        for place, sender in targets:
            pltpu.make_async_remote_copy(
                src_ref=o_ref,
                dst_ref=slots.at[g, sender],
                send_sem=send_sem.at[g, 0],
                recv_sem=recv_sem.at[g, sender],
                device_id=place,
                device_id_type=pl.DeviceIdType.MESH,
            ).wait_recv()
        acc = slots[g, 0]
        for j in range(1, count):
            acc = acc + slots[g, j]
        o_ref[...] = acc


def group_sum(value, groups, cid):
    spec = []
    widest = 1
    for names in groups:
        sizes = tuple(lax.axis_size(name) for name in names)
        count = 1
        for size in sizes:
            count *= size
        widest = max(widest, count)
        spec.append((tuple(FINE.index(name) for name in names), sizes))
    shape = value.shape
    flat = value.reshape(-1, 128) if value.ndim == 1 else value
    out = pl.pallas_call(
        functools.partial(group_kernel, tuple(spec)),
        out_shape=jax.ShapeDtypeStruct(flat.shape, flat.dtype),
        in_specs=[pl.BlockSpec(memory_space=pltpu.VMEM)],
        out_specs=pl.BlockSpec(memory_space=pltpu.VMEM),
        scratch_shapes=[
            pltpu.VMEM((len(spec), widest) + flat.shape, flat.dtype),
            pltpu.SemaphoreType.DMA((len(spec), widest)),
            pltpu.SemaphoreType.DMA((len(spec), widest)),
        ],
        compiler_params=pltpu.CompilerParams(collective_id=cid, has_side_effects=True),
    )(flat)
    return out.reshape(shape)


ALL_GROUPS = (FEAT, ("z",), ("yh", "x"))
CLAIM_GROUPS = (("z",), ("yh", "x"))


def halving_kernel(stages, gather, x_ref, o_ref, *scratch):
    if gather:
        work, recv, back, rs_send, rs_recv, ag_send, ag_recv = o_ref, *scratch
    else:
        work, recv, rs_send, rs_recv = scratch
    coords = [lax.axis_index(name) for name in FINE]
    partners, bits = [], []
    for axis, step in stages:
        place = coords[axis]
        bit = (place // step) % 2
        flip = place + step * (1 - 2 * bit)
        partners.append(tuple(flip if i == axis else c for i, c in enumerate(coords)))
        bits.append(bit)
    barrier = pltpu.get_barrier_semaphore()
    for partner in partners:
        pl.semaphore_signal(barrier, inc=1, device_id=partner, device_id_type=pl.DeviceIdType.MESH)
    pl.semaphore_wait(barrier, len(partners))
    work[...] = x_ref[...]
    total = work.shape[0]
    base = 0
    pieces = []
    for s, partner in enumerate(partners):
        size = total >> s
        half = size // 2
        keep = base + bits[s] * half
        give = base + (1 - bits[s]) * half
        slot = pl.ds(total - size, half)
        copy = pltpu.make_async_remote_copy(
            src_ref=work.at[pl.ds(give, half)],
            dst_ref=recv.at[slot],
            send_sem=rs_send.at[s],
            recv_sem=rs_recv.at[s],
            device_id=partner,
            device_id_type=pl.DeviceIdType.MESH,
        )
        copy.start()
        copy.wait()
        work[pl.ds(keep, half), :] = work[pl.ds(keep, half), :] + recv[slot, :]
        pieces.append((keep, give, slot))
        base = keep
    if gather:
        for s in reversed(range(len(partners))):
            keep, give, slot = pieces[s]
            copy = pltpu.make_async_remote_copy(
                src_ref=work.at[pl.ds(keep, slot.size)],
                dst_ref=back.at[slot],
                send_sem=ag_send.at[s],
                recv_sem=ag_recv.at[s],
                device_id=partners[s],
                device_id_type=pl.DeviceIdType.MESH,
            )
            copy.start()
            copy.wait()
            work[pl.ds(give, slot.size), :] = back[slot, :]
    else:
        o_ref[...] = work[pl.ds(base, o_ref.shape[0]), :]


CLAIM_STAGES = (("z", 1), ("x", 1), ("z", 2), ("x", 2), ("yh", 1), ("z", 4))


def claim_halving(value, gather, cid):
    stages = tuple((FINE.index(name), step) for name, step in CLAIM_STAGES)
    count = len(stages)
    flat = value.reshape(-1, 128)
    rows = flat.shape[0]
    out_rows = rows if gather else rows >> count
    scratch = [] if gather else [pltpu.VMEM(flat.shape, flat.dtype)]
    scratch += [pltpu.VMEM(flat.shape, flat.dtype)] * (2 if gather else 1)
    scratch += [pltpu.SemaphoreType.DMA((count,))] * (4 if gather else 2)
    out = pl.pallas_call(
        functools.partial(halving_kernel, stages, gather),
        out_shape=jax.ShapeDtypeStruct((out_rows, 128), flat.dtype),
        in_specs=[pl.BlockSpec(memory_space=pltpu.VMEM)],
        out_specs=pl.BlockSpec(memory_space=pltpu.VMEM),
        scratch_shapes=scratch,
        compiler_params=pltpu.CompilerParams(collective_id=cid, has_side_effects=True),
    )(flat)
    return out


def claim_sum(value):
    part = lax.psum_scatter(value, "z", scatter_dimension=0, tiled=True)
    part = lax.psum(part, ("yh", "x"))
    return lax.all_gather(part, "z", axis=0, tiled=True)


def all_sum(value):
    value = lax.psum(value, FEAT)
    value = lax.psum(value, "z")
    return lax.psum(value, ("yh", "x"))


def claim_scatter(value):
    width = value.shape[-1]
    rows = value.shape[0] // lax.axis_size(CLAIM)
    bits = value.reshape(2, 2, 2, 2, 2, 2, rows, width)
    ordered = bits.transpose(5, 2, 4, 1, 0, 3, 6, 7).reshape(value.shape)
    return claim_halving(ordered, False, 5).reshape(rows, width)


def per_device(block_tiles, block_scale, row_index, col_index, start_basis):
    tiles_here = block_tiles.reshape(block_tiles.shape[-3:])
    scale_here = block_scale.reshape(-1)
    rows_here = row_index.reshape(-1)
    cols_here = col_index.reshape(-1)
    edge = tiles_here.shape[-1]
    col_count = start_basis.shape[0] // edge
    claim_count = lax.axis_size(CLAIM)
    own_cols = start_basis.shape[0] // claim_count
    own_first = lax.axis_index(CLAIM) * own_cols
    row_part, col_part = degree_local(tiles_here, scale_here, rows_here, cols_here, col_count)
    col_total = group_sum(col_part, CLAIM_GROUPS, 0)
    col_scale = lax.rsqrt(col_total + 1.0)
    row_total = lax.psum_scatter(row_part, FEAT, scatter_dimension=0, tiled=True)
    start_total = lax.psum(gram_of(start_basis), FEAT)
    first_basis, _ = orthonormal(start_basis, start_total)
    first_operand = (col_scale[:, None] * first_basis).astype(jnp.bfloat16)
    first_partial = forward_local(tiles_here, scale_here, rows_here, cols_here, first_operand)
    first_sums = lax.psum_scatter(first_partial, FEAT, scatter_dimension=1, tiled=True).T
    row_scale = lax.rsqrt(row_total + 1.0)

    def row_orthonormal(block, cid):
        return orthonormal(block, group_sum(gram_of(block), ALL_GROUPS, cid))

    def backward_partial(basis):
        operand = (row_scale[:, None] * basis).astype(jnp.bfloat16)
        gathered = lax.all_gather(operand, FEAT, axis=0, tiled=True)
        return backward_local(tiles_here, scale_here, rows_here, cols_here, gathered, col_count)

    u_first, b_first = row_orthonormal(row_scale[:, None] * first_sums, 1)
    summed = claim_halving(backward_partial(u_first), True, 4).reshape(-1, u_first.shape[-1])
    update = col_scale[:, None] * summed - jnp.dot(first_basis, b_first.T, precision=HIGH)
    v_second, a_second = orthonormal(update, lax.psum(gram_of(update), FEAT))
    scaled = (col_scale[:, None] * v_second).astype(jnp.bfloat16)
    second_partial = forward_local(tiles_here, scale_here, rows_here, cols_here, scaled)
    second_sums = lax.psum_scatter(second_partial, FEAT, scatter_dimension=1, tiled=True).T
    p_second = row_scale[:, None] * second_sums - jnp.dot(u_first, a_second.T, precision=HIGH)
    u_second, b_second = row_orthonormal(p_second, 2)
    own_sums = claim_scatter(backward_partial(u_second))
    own_scale = lax.dynamic_slice_in_dim(col_scale, own_first, own_cols, 0)
    own_second = lax.dynamic_slice_in_dim(v_second, own_first, own_cols, 0)
    q_second = own_scale[:, None] * own_sums - jnp.dot(own_second, b_second.T, precision=HIGH)
    v_output, a_third = orthonormal(q_second, group_sum(gram_of(q_second), ALL_GROUPS, 3))
    bidiagonal = jnp.stack([b_first, a_second, b_second, a_third])
    return (u_second, v_output, bidiagonal)


def solution(mesh):
    claim_n, feat_n = mesh.devices.shape
    fine = Mesh(mesh.devices.reshape(2, claim_n // 16, 8, 2, feat_n // 2), FINE)
    placed = (
        P(CLAIM, FEAT, None, None, None),
        P(CLAIM, FEAT, None),
        P(CLAIM, FEAT, None),
        P(CLAIM, FEAT, None),
        P(FEAT, None),
    )
    return jax.shard_map(
        per_device,
        mesh=fine,
        in_specs=placed,
        out_specs=(P(CLAIM + FEAT, None), P(FEAT + CLAIM, None), P()),
        check_vma=False,
    )
```

```python
import functools

import jax
import jax.numpy as jnp
from jax import lax
from jax.experimental import pallas as pl
from jax.experimental.pallas import tpu as pltpu
from jax.sharding import Mesh
from jax.sharding import PartitionSpec as P

BLK_ROWS = 64

HIGH = lax.Precision.HIGHEST

FINE = ("yh", "x", "z", "yl", "c")
CLAIM = ("yh", "x", "z")
FEAT = ("yl", "c")


TILES_PER_STEP = 16


def forward_kernel(rows_ref, cols_ref, scale_ref, tiles_ref, operand_ref, out_ref):
    step = pl.program_id(0)
    edge = tiles_ref.shape[-1]

    @pl.when(step == 0)
    def _():
        out_ref[...] = jnp.zeros_like(out_ref)

    for t in range(tiles_ref.shape[0]):
        b = step * tiles_ref.shape[0] + t
        picked = operand_ref[:, pl.ds(pl.multiple_of(cols_ref[b] * edge, edge), edge)]
        product = lax.dot_general(
            picked, tiles_ref[t], (((1,), (1,)), ((), ())), preferred_element_type=jnp.float32
        )
        target = pl.ds(pl.multiple_of(rows_ref[b] * edge, edge), edge)
        out_ref[:, target] = out_ref[:, target] + product * scale_ref[b]


def backward_kernel(rows_ref, cols_ref, scale_ref, tiles_ref, operand_ref, out_ref):
    step = pl.program_id(0)
    edge = tiles_ref.shape[-1]

    @pl.when(step == 0)
    def _():
        out_ref[...] = jnp.zeros_like(out_ref)

    for t in range(tiles_ref.shape[0]):
        b = step * tiles_ref.shape[0] + t
        picked = operand_ref[:, pl.ds(pl.multiple_of(rows_ref[b] * edge, edge), edge)]
        product = jnp.dot(picked, tiles_ref[t], preferred_element_type=jnp.float32) * scale_ref[b]
        target = pl.ds(pl.multiple_of(cols_ref[b] * edge, edge), edge)
        out_ref[:, target] = out_ref[:, target] + product


def block_product(kernel, block_tiles, block_scale, row_index, col_index, operand, out_shape):
    count, edge, _ = block_tiles.shape
    per = TILES_PER_STEP
    grid_spec = pltpu.PrefetchScalarGridSpec(
        num_scalar_prefetch=2,
        grid=(count // per,),
        in_specs=[
            pl.BlockSpec(memory_space=pltpu.SMEM),
            pl.BlockSpec((per, edge, edge), lambda i, rows, cols: (i, 0, 0)),
            pl.BlockSpec(operand.shape, lambda i, rows, cols: (0, 0)),
        ],
        out_specs=pl.BlockSpec(out_shape, lambda i, rows, cols: (0, 0)),
    )
    width = min(operand.shape)
    return pl.pallas_call(
        kernel,
        grid_spec=grid_spec,
        out_shape=jax.ShapeDtypeStruct(out_shape, jnp.float32),
        cost_estimate=pl.CostEstimate(
            flops=2 * count * edge * edge * width,
            bytes_accessed=block_tiles.size * 2 + operand.size * 2 + out_shape[0] * out_shape[1] * 4,
            transcendentals=0,
        ),
    )(row_index, col_index, block_scale, block_tiles, operand)


def forward_local(block_tiles, block_scale, row_index, col_index, operand):
    edge = block_tiles.shape[-1]
    out_shape = (operand.shape[-1], BLK_ROWS * edge)
    return block_product(
        forward_kernel, block_tiles, block_scale, row_index, col_index, operand.T, out_shape
    )


def backward_local(block_tiles, block_scale, row_index, col_index, operand_t, col_count):
    edge = block_tiles.shape[-1]
    out_shape = (operand_t.shape[0], col_count * edge)
    flipped = block_product(
        backward_kernel, block_tiles, block_scale, row_index, col_index, operand_t, out_shape
    )
    return flipped.T


def degree_local(block_tiles, block_scale, row_index, col_index, col_count):
    row_sums = jnp.sum(block_tiles, axis=2, dtype=jnp.float32) * block_scale[:, None]
    col_sums = jnp.sum(block_tiles, axis=1, dtype=jnp.float32) * block_scale[:, None]
    row_select = (row_index[None, :] == jnp.arange(BLK_ROWS, dtype=jnp.int32)[:, None]).astype(
        jnp.float32
    )
    col_select = (col_index[None, :] == jnp.arange(col_count, dtype=jnp.int32)[:, None]).astype(
        jnp.float32
    )
    row_part = jnp.einsum("rb,bi->ri", row_select, row_sums, precision=HIGH).reshape(-1)
    col_part = jnp.einsum("cb,bi->ci", col_select, col_sums, precision=HIGH).reshape(-1)
    return (row_part, col_part)


def gram_of(block):
    return jnp.dot(block.T, block, precision=HIGH)


def factor_kernel(g_ref, o_ref):
    n = g_ref.shape[0]
    o_ref[:, :n] = g_ref[...]
    rows = lax.broadcasted_iota(jnp.int32, (n, 2 * n), 0)
    cols = lax.broadcasted_iota(jnp.int32, (n, 2 * n), 1)
    o_ref[:, n:] = jnp.where(rows[:, n:] == cols[:, n:] - n, 1.0, 0.0).astype(o_ref.dtype)
    m = o_ref[...]
    below = lax.broadcasted_iota(jnp.int32, (n, 1), 0)
    for j in range(n):
        factor = jnp.where(below > j, m[:, j : j + 1], 0.0) * (1.0 / m[j : j + 1, j : j + 1])
        m = m - factor * m[j : j + 1, :]
    diagonal = jnp.sum(jnp.where(rows == cols, m, 0.0), axis=1, keepdims=True)
    m = m * lax.rsqrt(diagonal)
    o_ref[...] = jnp.where((cols < n) & (cols < rows), 0.0, m)


def factor_of(gram_total):
    n = gram_total.shape[0]
    both = pl.pallas_call(
        factor_kernel,
        out_shape=jax.ShapeDtypeStruct((n, 2 * n), jnp.float32),
        in_specs=[pl.BlockSpec(memory_space=pltpu.VMEM)],
        out_specs=pl.BlockSpec(memory_space=pltpu.VMEM),
    )(gram_total)
    return both[:, :n], both[:, n:]


def orthonormal(block, gram_total):
    upper, inverse = factor_of(gram_total)
    basis = jnp.dot(block, inverse.T, precision=HIGH)
    return (basis, upper)


def group_kernel(groups, x_ref, o_ref, slots, send_sem, recv_sem):
    coords = [lax.axis_index(name) for name in FINE]
    plans = []
    for axes, sizes in groups:
        count = 1
        for size in sizes:
            count *= size
        me = 0
        for axis, size in zip(axes, sizes):
            me = me * size + coords[axis]
        targets = []
        for k in range(1, count):
            member = (me + k) % count
            place = list(coords)
            rest = member
            for axis, size in reversed(list(zip(axes, sizes))):
                place[axis] = rest % size
                rest = rest // size
            targets.append((tuple(place), (me + count - k) % count))
        plans.append((count, me, targets))
    barrier = pltpu.get_barrier_semaphore()
    total = 0
    for count, me, targets in plans:
        for place, _ in targets:
            pl.semaphore_signal(barrier, inc=1, device_id=place, device_id_type=pl.DeviceIdType.MESH)
        total += len(targets)
    pl.semaphore_wait(barrier, total)
    o_ref[...] = x_ref[...]
    for g, (count, me, targets) in enumerate(plans):
        slots[g, me] = o_ref[...]
        copies = []
        for k, (place, _) in enumerate(targets):
            copy = pltpu.make_async_remote_copy(
                src_ref=o_ref,
                dst_ref=slots.at[g, me],
                send_sem=send_sem.at[g, k],
                recv_sem=recv_sem.at[g, me],
                device_id=place,
                device_id_type=pl.DeviceIdType.MESH,
            )
            copy.start()
            copies.append(copy)
        for copy in copies:
            copy.wait_send()
        for place, sender in targets:
            pltpu.make_async_remote_copy(
                src_ref=o_ref,
                dst_ref=slots.at[g, sender],
                send_sem=send_sem.at[g, 0],
                recv_sem=recv_sem.at[g, sender],
                device_id=place,
                device_id_type=pl.DeviceIdType.MESH,
            ).wait_recv()
        acc = slots[g, 0]
        for j in range(1, count):
            acc = acc + slots[g, j]
        o_ref[...] = acc


def group_sum(value, groups, cid):
    spec = []
    widest = 1
    for names in groups:
        sizes = tuple(lax.axis_size(name) for name in names)
        count = 1
        for size in sizes:
            count *= size
        widest = max(widest, count)
        spec.append((tuple(FINE.index(name) for name in names), sizes))
    shape = value.shape
    flat = value.reshape(-1, 128) if value.ndim == 1 else value
    out = pl.pallas_call(
        functools.partial(group_kernel, tuple(spec)),
        out_shape=jax.ShapeDtypeStruct(flat.shape, flat.dtype),
        in_specs=[pl.BlockSpec(memory_space=pltpu.VMEM)],
        out_specs=pl.BlockSpec(memory_space=pltpu.VMEM),
        scratch_shapes=[
            pltpu.VMEM((len(spec), widest) + flat.shape, flat.dtype),
            pltpu.SemaphoreType.DMA((len(spec), widest)),
            pltpu.SemaphoreType.DMA((len(spec), widest)),
        ],
        compiler_params=pltpu.CompilerParams(collective_id=cid, has_side_effects=True),
    )(flat)
    return out.reshape(shape)


ALL_GROUPS = (FEAT, ("z",), ("yh", "x"))
CLAIM_GROUPS = (("z",), ("yh", "x"))


def halving_kernel(stages, gather, x_ref, o_ref, *scratch):
    if gather:
        work, recv, back, rs_send, rs_recv, ag_send, ag_recv = o_ref, *scratch
    else:
        work, recv, rs_send, rs_recv = scratch
    coords = [lax.axis_index(name) for name in FINE]
    partners, bits = [], []
    for axis, step in stages:
        place = coords[axis]
        bit = (place // step) % 2
        flip = place + step * (1 - 2 * bit)
        partners.append(tuple(flip if i == axis else c for i, c in enumerate(coords)))
        bits.append(bit)
    barrier = pltpu.get_barrier_semaphore()
    for partner in partners:
        pl.semaphore_signal(barrier, inc=1, device_id=partner, device_id_type=pl.DeviceIdType.MESH)
    pl.semaphore_wait(barrier, len(partners))
    work[...] = x_ref[...]
    total = work.shape[0]
    base = 0
    pieces = []
    for s, partner in enumerate(partners):
        size = total >> s
        half = size // 2
        keep = base + bits[s] * half
        give = base + (1 - bits[s]) * half
        slot = pl.ds(total - size, half)
        copy = pltpu.make_async_remote_copy(
            src_ref=work.at[pl.ds(give, half)],
            dst_ref=recv.at[slot],
            send_sem=rs_send.at[s],
            recv_sem=rs_recv.at[s],
            device_id=partner,
            device_id_type=pl.DeviceIdType.MESH,
        )
        copy.start()
        copy.wait()
        work[pl.ds(keep, half), :] = work[pl.ds(keep, half), :] + recv[slot, :]
        pieces.append((keep, give, slot))
        base = keep
    if gather:
        for s in reversed(range(len(partners))):
            keep, give, slot = pieces[s]
            copy = pltpu.make_async_remote_copy(
                src_ref=work.at[pl.ds(keep, slot.size)],
                dst_ref=back.at[slot],
                send_sem=ag_send.at[s],
                recv_sem=ag_recv.at[s],
                device_id=partners[s],
                device_id_type=pl.DeviceIdType.MESH,
            )
            copy.start()
            copy.wait()
            work[pl.ds(give, slot.size), :] = back[slot, :]
    else:
        o_ref[...] = work[pl.ds(base, o_ref.shape[0]), :]


CLAIM_STAGES = (("z", 1), ("x", 1), ("z", 2), ("x", 2), ("yh", 1), ("z", 4))


def claim_halving(value, gather, cid):
    stages = tuple((FINE.index(name), step) for name, step in CLAIM_STAGES)
    count = len(stages)
    flat = value.reshape(-1, 128)
    rows = flat.shape[0]
    out_rows = rows if gather else rows >> count
    scratch = [] if gather else [pltpu.VMEM(flat.shape, flat.dtype)]
    scratch += [pltpu.VMEM(flat.shape, flat.dtype)] * (2 if gather else 1)
    scratch += [pltpu.SemaphoreType.DMA((count,))] * (4 if gather else 2)
    out = pl.pallas_call(
        functools.partial(halving_kernel, stages, gather),
        out_shape=jax.ShapeDtypeStruct((out_rows, 128), flat.dtype),
        in_specs=[pl.BlockSpec(memory_space=pltpu.VMEM)],
        out_specs=pl.BlockSpec(memory_space=pltpu.VMEM),
        scratch_shapes=scratch,
        compiler_params=pltpu.CompilerParams(collective_id=cid, has_side_effects=True),
    )(flat)
    return out


def claim_sum(value):
    part = lax.psum_scatter(value, "z", scatter_dimension=0, tiled=True)
    part = lax.psum(part, ("yh", "x"))
    return lax.all_gather(part, "z", axis=0, tiled=True)


def all_sum(value):
    value = lax.psum(value, FEAT)
    value = lax.psum(value, "z")
    return lax.psum(value, ("yh", "x"))


def claim_scatter(value):
    width = value.shape[-1]
    rows = value.shape[0] // lax.axis_size(CLAIM)
    bits = value.reshape(2, 2, 2, 2, 2, 2, rows, width)
    ordered = bits.transpose(5, 2, 4, 1, 0, 3, 6, 7).reshape(value.shape)
    return claim_halving(ordered, False, 5).reshape(rows, width)


def per_device(block_tiles, block_scale, row_index, col_index, start_basis):
    tiles_here = block_tiles.reshape(block_tiles.shape[-3:])
    scale_here = block_scale.reshape(-1)
    rows_here = row_index.reshape(-1)
    cols_here = col_index.reshape(-1)
    edge = tiles_here.shape[-1]
    col_count = start_basis.shape[0] // edge
    claim_count = lax.axis_size(CLAIM)
    own_cols = start_basis.shape[0] // claim_count
    own_first = lax.axis_index(CLAIM) * own_cols
    row_part, col_part = degree_local(tiles_here, scale_here, rows_here, cols_here, col_count)
    col_total = group_sum(col_part, CLAIM_GROUPS, 0)
    col_scale = lax.rsqrt(col_total + 1.0)
    row_total = lax.psum(row_part, FEAT)
    row_scale_all = lax.rsqrt(row_total + 1.0)
    own_rows = row_part.shape[0] // lax.axis_size(FEAT)
    own_start = lax.axis_index(FEAT) * own_rows
    row_scale = lax.dynamic_slice_in_dim(row_scale_all, own_start, own_rows, 0)
    start_total = lax.psum(gram_of(start_basis), FEAT)
    first_basis, _ = orthonormal(start_basis, start_total)
    first_operand = (col_scale[:, None] * first_basis).astype(jnp.bfloat16)
    first_partial = forward_local(tiles_here, scale_here, rows_here, cols_here, first_operand)

    def row_step(partial_t, previous_t, coupling, cid):
        sums_t = lax.psum_scatter(partial_t, FEAT, scatter_dimension=1, tiled=True)
        all_t = lax.all_gather(sums_t, FEAT, axis=1, tiled=True)
        block_t = row_scale[None, :] * sums_t
        wide_t = row_scale_all[None, :] * all_t
        if previous_t is not None:
            own_previous = lax.dynamic_slice_in_dim(previous_t, own_start, own_rows, 1)
            block_t = block_t - jnp.dot(coupling, own_previous, precision=HIGH)
            wide_t = wide_t - jnp.dot(coupling, previous_t, precision=HIGH)
        gram = jnp.dot(block_t, block_t.T, precision=HIGH)
        upper, inverse = factor_of(group_sum(gram, ALL_GROUPS, cid))
        return jnp.dot(inverse, wide_t, precision=HIGH), upper

    def backward_partial(basis_t):
        operand_t = (row_scale_all[None, :] * basis_t).astype(jnp.bfloat16)
        return backward_local(tiles_here, scale_here, rows_here, cols_here, operand_t, col_count)

    u_first, b_first = row_step(first_partial, None, None, 1)
    summed = claim_halving(backward_partial(u_first), True, 4).reshape(-1, first_basis.shape[-1])
    update = col_scale[:, None] * summed - jnp.dot(first_basis, b_first.T, precision=HIGH)
    v_second, a_second = orthonormal(update, lax.psum(gram_of(update), FEAT))
    scaled = (col_scale[:, None] * v_second).astype(jnp.bfloat16)
    second_partial = forward_local(tiles_here, scale_here, rows_here, cols_here, scaled)
    u_second, b_second = row_step(second_partial, u_first, a_second, 2)
    own_sums = claim_scatter(backward_partial(u_second))
    own_scale = lax.dynamic_slice_in_dim(col_scale, own_first, own_cols, 0)
    own_second = lax.dynamic_slice_in_dim(v_second, own_first, own_cols, 0)
    q_second = own_scale[:, None] * own_sums - jnp.dot(own_second, b_second.T, precision=HIGH)
    v_output, a_third = orthonormal(q_second, group_sum(gram_of(q_second), ALL_GROUPS, 3))
    bidiagonal = jnp.stack([b_first, a_second, b_second, a_third])
    u_output = lax.dynamic_slice_in_dim(u_second, own_start, own_rows, 1).T
    return (u_output, v_output, bidiagonal)


def solution(mesh):
    claim_n, feat_n = mesh.devices.shape
    fine = Mesh(mesh.devices.reshape(2, claim_n // 16, 8, 2, feat_n // 2), FINE)
    placed = (
        P(CLAIM, FEAT, None, None, None),
        P(CLAIM, FEAT, None),
        P(CLAIM, FEAT, None),
        P(CLAIM, FEAT, None),
        P(FEAT, None),
    )
    return jax.shard_map(
        per_device,
        mesh=fine,
        in_specs=placed,
        out_specs=(P(CLAIM + FEAT, None), P(FEAT + CLAIM, None), P()),
        check_vma=False,
    )
```

```python
import functools

import jax
import jax.numpy as jnp
from jax import lax
from jax.experimental import pallas as pl
from jax.experimental.pallas import tpu as pltpu
from jax.sharding import Mesh
from jax.sharding import PartitionSpec as P

BLK_ROWS = 64

HIGH = lax.Precision.HIGHEST

FINE = ("yh", "x", "z", "yl", "c")
CLAIM = ("yh", "x", "z")
FEAT = ("yl", "c")


TILES_PER_STEP = 16


def forward_kernel(rows_ref, cols_ref, scale_ref, tiles_ref, operand_ref, out_ref):
    step = pl.program_id(0)
    edge = tiles_ref.shape[-1]

    @pl.when(step == 0)
    def _():
        out_ref[...] = jnp.zeros_like(out_ref)

    for t in range(tiles_ref.shape[0]):
        b = step * tiles_ref.shape[0] + t
        picked = operand_ref[:, pl.ds(pl.multiple_of(cols_ref[b] * edge, edge), edge)]
        product = lax.dot_general(
            picked, tiles_ref[t], (((1,), (1,)), ((), ())), preferred_element_type=jnp.float32
        )
        target = pl.ds(pl.multiple_of(rows_ref[b] * edge, edge), edge)
        out_ref[:, target] = out_ref[:, target] + product * scale_ref[b]


def backward_kernel(rows_ref, cols_ref, scale_ref, tiles_ref, operand_ref, out_ref):
    step = pl.program_id(0)
    edge = tiles_ref.shape[-1]

    @pl.when(step == 0)
    def _():
        out_ref[...] = jnp.zeros_like(out_ref)

    for t in range(tiles_ref.shape[0]):
        b = step * tiles_ref.shape[0] + t
        picked = operand_ref[:, pl.ds(pl.multiple_of(rows_ref[b] * edge, edge), edge)]
        product = jnp.dot(picked, tiles_ref[t], preferred_element_type=jnp.float32) * scale_ref[b]
        target = pl.ds(pl.multiple_of(cols_ref[b] * edge, edge), edge)
        out_ref[:, target] = out_ref[:, target] + product


def block_product(kernel, block_tiles, block_scale, row_index, col_index, operand, out_shape):
    count, edge, _ = block_tiles.shape
    per = TILES_PER_STEP
    grid_spec = pltpu.PrefetchScalarGridSpec(
        num_scalar_prefetch=2,
        grid=(count // per,),
        in_specs=[
            pl.BlockSpec(memory_space=pltpu.SMEM),
            pl.BlockSpec((per, edge, edge), lambda i, rows, cols: (i, 0, 0)),
            pl.BlockSpec(operand.shape, lambda i, rows, cols: (0, 0)),
        ],
        out_specs=pl.BlockSpec(out_shape, lambda i, rows, cols: (0, 0)),
    )
    width = min(operand.shape)
    return pl.pallas_call(
        kernel,
        grid_spec=grid_spec,
        out_shape=jax.ShapeDtypeStruct(out_shape, jnp.float32),
        cost_estimate=pl.CostEstimate(
            flops=2 * count * edge * edge * width,
            bytes_accessed=block_tiles.size * 2 + operand.size * 2 + out_shape[0] * out_shape[1] * 4,
            transcendentals=0,
        ),
    )(row_index, col_index, block_scale, block_tiles, operand)


def forward_local(block_tiles, block_scale, row_index, col_index, operand):
    edge = block_tiles.shape[-1]
    out_shape = (operand.shape[-1], BLK_ROWS * edge)
    return block_product(
        forward_kernel, block_tiles, block_scale, row_index, col_index, operand.T, out_shape
    )


def backward_local(block_tiles, block_scale, row_index, col_index, operand_t, col_count):
    edge = block_tiles.shape[-1]
    out_shape = (operand_t.shape[0], col_count * edge)
    flipped = block_product(
        backward_kernel, block_tiles, block_scale, row_index, col_index, operand_t, out_shape
    )
    return flipped.T


def degree_local(block_tiles, block_scale, row_index, col_index, col_count):
    row_sums = jnp.sum(block_tiles, axis=2, dtype=jnp.float32) * block_scale[:, None]
    col_sums = jnp.sum(block_tiles, axis=1, dtype=jnp.float32) * block_scale[:, None]
    row_select = (row_index[None, :] == jnp.arange(BLK_ROWS, dtype=jnp.int32)[:, None]).astype(
        jnp.float32
    )
    col_select = (col_index[None, :] == jnp.arange(col_count, dtype=jnp.int32)[:, None]).astype(
        jnp.float32
    )
    row_part = jnp.einsum("rb,bi->ri", row_select, row_sums, precision=HIGH).reshape(-1)
    col_part = jnp.einsum("cb,bi->ci", col_select, col_sums, precision=HIGH).reshape(-1)
    return (row_part, col_part)


def gram_of(block):
    return jnp.dot(block.T, block, precision=HIGH)


def factor_kernel(g_ref, o_ref):
    n = g_ref.shape[0]
    o_ref[:, :n] = g_ref[...]
    rows = lax.broadcasted_iota(jnp.int32, (n, 2 * n), 0)
    cols = lax.broadcasted_iota(jnp.int32, (n, 2 * n), 1)
    o_ref[:, n:] = jnp.where(rows[:, n:] == cols[:, n:] - n, 1.0, 0.0).astype(o_ref.dtype)
    m = o_ref[...]
    below = lax.broadcasted_iota(jnp.int32, (n, 1), 0)
    for j in range(n):
        factor = jnp.where(below > j, m[:, j : j + 1], 0.0) * (1.0 / m[j : j + 1, j : j + 1])
        m = m - factor * m[j : j + 1, :]
    diagonal = jnp.sum(jnp.where(rows == cols, m, 0.0), axis=1, keepdims=True)
    m = m * lax.rsqrt(diagonal)
    o_ref[...] = jnp.where((cols < n) & (cols < rows), 0.0, m)


def factor_of(gram_total):
    n = gram_total.shape[0]
    both = pl.pallas_call(
        factor_kernel,
        out_shape=jax.ShapeDtypeStruct((n, 2 * n), jnp.float32),
        in_specs=[pl.BlockSpec(memory_space=pltpu.VMEM)],
        out_specs=pl.BlockSpec(memory_space=pltpu.VMEM),
    )(gram_total)
    return both[:, :n], both[:, n:]


def orthonormal(block, gram_total):
    upper, inverse = factor_of(gram_total)
    basis = jnp.dot(block, inverse.T, precision=HIGH)
    return (basis, upper)


def group_plan(groups, coords):
    plans = []
    for axes, sizes in groups:
        count = 1
        for size in sizes:
            count *= size
        me = 0
        for axis, size in zip(axes, sizes):
            me = me * size + coords[axis]
        targets = []
        for k in range(1, count):
            member = (me + k) % count
            place = list(coords)
            rest = member
            for axis, size in reversed(list(zip(axes, sizes))):
                place[axis] = rest % size
                rest = rest // size
            targets.append((tuple(place), (me + count - k) % count))
        plans.append((count, me, targets))
    return plans


def group_kernel(all_groups, *refs):
    n = len(all_groups)
    x_refs, o_refs, scratch = refs[:n], refs[n : 2 * n], refs[2 * n :]
    coords = [lax.axis_index(name) for name in FINE]
    plans = [group_plan(groups, coords) for groups in all_groups]
    barrier = pltpu.get_barrier_semaphore()
    total = 0
    for plan in plans:
        for count, me, targets in plan:
            for place, _ in targets:
                pl.semaphore_signal(barrier, inc=1, device_id=place, device_id_type=pl.DeviceIdType.MESH)
            total += len(targets)
    pl.semaphore_wait(barrier, total)
    for a in range(n):
        o_refs[a][...] = x_refs[a][...]
    for g in range(max(len(plan) for plan in plans)):
        started = []
        for a in range(n):
            if g >= len(plans[a]):
                continue
            o_ref = o_refs[a]
            slots, send_sem, recv_sem = scratch[3 * a : 3 * a + 3]
            count, me, targets = plans[a][g]
            slots[g, me] = o_ref[...]
            copies = []
            for k, (place, _) in enumerate(targets):
                copy = pltpu.make_async_remote_copy(
                    src_ref=o_ref,
                    dst_ref=slots.at[g, me],
                    send_sem=send_sem.at[g, k],
                    recv_sem=recv_sem.at[g, me],
                    device_id=place,
                    device_id_type=pl.DeviceIdType.MESH,
                )
                copy.start()
                copies.append(copy)
            started.append((a, copies))
        for a, copies in started:
            o_ref = o_refs[a]
            slots, send_sem, recv_sem = scratch[3 * a : 3 * a + 3]
            count, me, targets = plans[a][g]
            for copy in copies:
                copy.wait_send()
            for place, sender in targets:
                pltpu.make_async_remote_copy(
                    src_ref=o_ref,
                    dst_ref=slots.at[g, sender],
                    send_sem=send_sem.at[g, 0],
                    recv_sem=recv_sem.at[g, sender],
                    device_id=place,
                    device_id_type=pl.DeviceIdType.MESH,
                ).wait_recv()
            acc = slots[g, 0]
            for j in range(1, count):
                acc = acc + slots[g, j]
            o_ref[...] = acc


def group_sums(values, all_groups, cid):
    specs, flats, scratch = [], [], []
    for value, groups in zip(values, all_groups):
        spec = []
        widest = 1
        for names in groups:
            sizes = tuple(lax.axis_size(name) for name in names)
            count = 1
            for size in sizes:
                count *= size
            widest = max(widest, count)
            spec.append((tuple(FINE.index(name) for name in names), sizes))
        flat = value.reshape(-1, 128) if value.ndim == 1 else value
        specs.append(tuple(spec))
        flats.append(flat)
        scratch += [
            pltpu.VMEM((len(spec), widest) + flat.shape, flat.dtype),
            pltpu.SemaphoreType.DMA((len(spec), widest)),
            pltpu.SemaphoreType.DMA((len(spec), widest)),
        ]
    outs = pl.pallas_call(
        functools.partial(group_kernel, tuple(specs)),
        out_shape=[jax.ShapeDtypeStruct(flat.shape, flat.dtype) for flat in flats],
        in_specs=[pl.BlockSpec(memory_space=pltpu.VMEM)] * len(flats),
        out_specs=[pl.BlockSpec(memory_space=pltpu.VMEM)] * len(flats),
        scratch_shapes=scratch,
        compiler_params=pltpu.CompilerParams(collective_id=cid, has_side_effects=True),
    )(*flats)
    return [out.reshape(value.shape) for out, value in zip(outs, values)]


def group_sum(value, groups, cid):
    return group_sums([value], [groups], cid)[0]


ALL_GROUPS = (FEAT, ("z",), ("yh", "x"))
CLAIM_GROUPS = (("z",), ("yh", "x"))


def halving_kernel(stages, gather, x_ref, o_ref, *scratch):
    if gather:
        work, recv, back, rs_send, rs_recv, ag_send, ag_recv = o_ref, *scratch
    else:
        work, recv, rs_send, rs_recv = scratch
    coords = [lax.axis_index(name) for name in FINE]
    partners, bits = [], []
    for axis, step in stages:
        place = coords[axis]
        bit = (place // step) % 2
        flip = place + step * (1 - 2 * bit)
        partners.append(tuple(flip if i == axis else c for i, c in enumerate(coords)))
        bits.append(bit)
    barrier = pltpu.get_barrier_semaphore()
    for partner in partners:
        pl.semaphore_signal(barrier, inc=1, device_id=partner, device_id_type=pl.DeviceIdType.MESH)
    pl.semaphore_wait(barrier, len(partners))
    work[...] = x_ref[...]
    total = work.shape[0]
    base = 0
    pieces = []
    for s, partner in enumerate(partners):
        size = total >> s
        half = size // 2
        keep = base + bits[s] * half
        give = base + (1 - bits[s]) * half
        slot = pl.ds(total - size, half)
        copy = pltpu.make_async_remote_copy(
            src_ref=work.at[pl.ds(give, half)],
            dst_ref=recv.at[slot],
            send_sem=rs_send.at[s],
            recv_sem=rs_recv.at[s],
            device_id=partner,
            device_id_type=pl.DeviceIdType.MESH,
        )
        copy.start()
        copy.wait()
        work[pl.ds(keep, half), :] = work[pl.ds(keep, half), :] + recv[slot, :]
        pieces.append((keep, give, slot))
        base = keep
    if gather:
        for s in reversed(range(len(partners))):
            keep, give, slot = pieces[s]
            copy = pltpu.make_async_remote_copy(
                src_ref=work.at[pl.ds(keep, slot.size)],
                dst_ref=back.at[slot],
                send_sem=ag_send.at[s],
                recv_sem=ag_recv.at[s],
                device_id=partners[s],
                device_id_type=pl.DeviceIdType.MESH,
            )
            copy.start()
            copy.wait()
            work[pl.ds(give, slot.size), :] = back[slot, :]
    else:
        o_ref[...] = work[pl.ds(base, o_ref.shape[0]), :]


CLAIM_STAGES = (("z", 1), ("x", 1), ("z", 2), ("x", 2), ("yh", 1), ("z", 4))


def claim_halving(value, gather, cid):
    stages = tuple((FINE.index(name), step) for name, step in CLAIM_STAGES)
    count = len(stages)
    flat = value.reshape(-1, 128)
    rows = flat.shape[0]
    out_rows = rows if gather else rows >> count
    scratch = [] if gather else [pltpu.VMEM(flat.shape, flat.dtype)]
    scratch += [pltpu.VMEM(flat.shape, flat.dtype)] * (2 if gather else 1)
    scratch += [pltpu.SemaphoreType.DMA((count,))] * (4 if gather else 2)
    out = pl.pallas_call(
        functools.partial(halving_kernel, stages, gather),
        out_shape=jax.ShapeDtypeStruct((out_rows, 128), flat.dtype),
        in_specs=[pl.BlockSpec(memory_space=pltpu.VMEM)],
        out_specs=pl.BlockSpec(memory_space=pltpu.VMEM),
        scratch_shapes=scratch,
        compiler_params=pltpu.CompilerParams(collective_id=cid, has_side_effects=True),
    )(flat)
    return out


def claim_sum(value):
    part = lax.psum_scatter(value, "z", scatter_dimension=0, tiled=True)
    part = lax.psum(part, ("yh", "x"))
    return lax.all_gather(part, "z", axis=0, tiled=True)


def all_sum(value):
    value = lax.psum(value, FEAT)
    value = lax.psum(value, "z")
    return lax.psum(value, ("yh", "x"))


def claim_scatter(value):
    width = value.shape[-1]
    rows = value.shape[0] // lax.axis_size(CLAIM)
    bits = value.reshape(2, 2, 2, 2, 2, 2, rows, width)
    ordered = bits.transpose(5, 2, 4, 1, 0, 3, 6, 7).reshape(value.shape)
    return claim_halving(ordered, False, 5).reshape(rows, width)


def per_device(block_tiles, block_scale, row_index, col_index, start_basis):
    tiles_here = block_tiles.reshape(block_tiles.shape[-3:])
    scale_here = block_scale.reshape(-1)
    rows_here = row_index.reshape(-1)
    cols_here = col_index.reshape(-1)
    edge = tiles_here.shape[-1]
    col_count = start_basis.shape[0] // edge
    claim_count = lax.axis_size(CLAIM)
    own_cols = start_basis.shape[0] // claim_count
    own_first = lax.axis_index(CLAIM) * own_cols
    row_part, col_part = degree_local(tiles_here, scale_here, rows_here, cols_here, col_count)
    col_total, row_total, start_total = group_sums(
        [col_part, row_part, gram_of(start_basis)], [CLAIM_GROUPS, (FEAT,), (FEAT,)], 0
    )
    col_scale = lax.rsqrt(col_total + 1.0)
    row_scale_all = lax.rsqrt(row_total + 1.0)
    own_rows = row_part.shape[0] // lax.axis_size(FEAT)
    own_start = lax.axis_index(FEAT) * own_rows
    row_scale = lax.dynamic_slice_in_dim(row_scale_all, own_start, own_rows, 0)
    first_basis, _ = orthonormal(start_basis, start_total)
    first_operand = (col_scale[:, None] * first_basis).astype(jnp.bfloat16)
    first_partial = forward_local(tiles_here, scale_here, rows_here, cols_here, first_operand)

    def row_step(partial_t, previous_t, coupling, cid):
        sums_t = lax.psum_scatter(partial_t, FEAT, scatter_dimension=1, tiled=True)
        all_t = lax.all_gather(sums_t, FEAT, axis=1, tiled=True)
        block_t = row_scale[None, :] * sums_t
        wide_t = row_scale_all[None, :] * all_t
        if previous_t is not None:
            own_previous = lax.dynamic_slice_in_dim(previous_t, own_start, own_rows, 1)
            block_t = block_t - jnp.dot(coupling, own_previous, precision=HIGH)
            wide_t = wide_t - jnp.dot(coupling, previous_t, precision=HIGH)
        gram = jnp.dot(block_t, block_t.T, precision=HIGH)
        upper, inverse = factor_of(group_sum(gram, ALL_GROUPS, cid))
        return jnp.dot(inverse, wide_t, precision=HIGH), upper

    def backward_partial(basis_t):
        operand_t = (row_scale_all[None, :] * basis_t).astype(jnp.bfloat16)
        return backward_local(tiles_here, scale_here, rows_here, cols_here, operand_t, col_count)

    u_first, b_first = row_step(first_partial, None, None, 1)
    summed = claim_halving(backward_partial(u_first), True, 4).reshape(-1, first_basis.shape[-1])
    update = col_scale[:, None] * summed - jnp.dot(first_basis, b_first.T, precision=HIGH)
    v_second, a_second = orthonormal(update, lax.psum(gram_of(update), FEAT))
    scaled = (col_scale[:, None] * v_second).astype(jnp.bfloat16)
    second_partial = forward_local(tiles_here, scale_here, rows_here, cols_here, scaled)
    u_second, b_second = row_step(second_partial, u_first, a_second, 2)
    own_sums = claim_scatter(backward_partial(u_second))
    own_scale = lax.dynamic_slice_in_dim(col_scale, own_first, own_cols, 0)
    own_second = lax.dynamic_slice_in_dim(v_second, own_first, own_cols, 0)
    q_second = own_scale[:, None] * own_sums - jnp.dot(own_second, b_second.T, precision=HIGH)
    v_output, a_third = orthonormal(q_second, group_sum(gram_of(q_second), ALL_GROUPS, 3))
    bidiagonal = jnp.stack([b_first, a_second, b_second, a_third])
    u_output = lax.dynamic_slice_in_dim(u_second, own_start, own_rows, 1).T
    return (u_output, v_output, bidiagonal)


def solution(mesh):
    claim_n, feat_n = mesh.devices.shape
    fine = Mesh(mesh.devices.reshape(2, claim_n // 16, 8, 2, feat_n // 2), FINE)
    placed = (
        P(CLAIM, FEAT, None, None, None),
        P(CLAIM, FEAT, None),
        P(CLAIM, FEAT, None),
        P(CLAIM, FEAT, None),
        P(FEAT, None),
    )
    return jax.shard_map(
        per_device,
        mesh=fine,
        in_specs=placed,
        out_specs=(P(CLAIM + FEAT, None), P(FEAT + CLAIM, None), P()),
        check_vma=False,
    )
```

```python
import functools

import jax
import jax.numpy as jnp
from jax import lax
from jax.experimental import pallas as pl
from jax.experimental.pallas import tpu as pltpu
from jax.sharding import Mesh
from jax.sharding import PartitionSpec as P

BLK_ROWS = 64

HIGH = lax.Precision.HIGHEST

FINE = ("yh", "x", "z", "yl", "c")
CLAIM = ("yh", "x", "z")
FEAT = ("yl", "c")


TILES_PER_STEP = 16


def forward_kernel(rows_ref, cols_ref, scale_ref, tiles_ref, operand_ref, out_ref):
    step = pl.program_id(0)
    edge = tiles_ref.shape[-1]

    @pl.when(step == 0)
    def _():
        out_ref[...] = jnp.zeros_like(out_ref)

    for t in range(tiles_ref.shape[0]):
        b = step * tiles_ref.shape[0] + t
        picked = operand_ref[:, pl.ds(pl.multiple_of(cols_ref[b] * edge, edge), edge)]
        product = lax.dot_general(
            picked, tiles_ref[t], (((1,), (1,)), ((), ())), preferred_element_type=jnp.float32
        )
        target = pl.ds(pl.multiple_of(rows_ref[b] * edge, edge), edge)
        out_ref[:, target] = out_ref[:, target] + product * scale_ref[b]


def backward_kernel(rows_ref, cols_ref, scale_ref, tiles_ref, operand_ref, out_ref):
    step = pl.program_id(0)
    edge = tiles_ref.shape[-1]

    @pl.when(step == 0)
    def _():
        out_ref[...] = jnp.zeros_like(out_ref)

    for t in range(tiles_ref.shape[0]):
        b = step * tiles_ref.shape[0] + t
        picked = operand_ref[:, pl.ds(pl.multiple_of(rows_ref[b] * edge, edge), edge)]
        product = jnp.dot(picked, tiles_ref[t], preferred_element_type=jnp.float32) * scale_ref[b]
        target = pl.ds(pl.multiple_of(cols_ref[b] * edge, edge), edge)
        out_ref[:, target] = out_ref[:, target] + product


def block_product(kernel, block_tiles, block_scale, row_index, col_index, operand, out_shape):
    count, edge, _ = block_tiles.shape
    per = TILES_PER_STEP
    grid_spec = pltpu.PrefetchScalarGridSpec(
        num_scalar_prefetch=2,
        grid=(count // per,),
        in_specs=[
            pl.BlockSpec(memory_space=pltpu.SMEM),
            pl.BlockSpec((per, edge, edge), lambda i, rows, cols: (i, 0, 0)),
            pl.BlockSpec(operand.shape, lambda i, rows, cols: (0, 0)),
        ],
        out_specs=pl.BlockSpec(out_shape, lambda i, rows, cols: (0, 0)),
    )
    width = min(operand.shape)
    return pl.pallas_call(
        kernel,
        grid_spec=grid_spec,
        out_shape=jax.ShapeDtypeStruct(out_shape, jnp.float32),
        cost_estimate=pl.CostEstimate(
            flops=2 * count * edge * edge * width,
            bytes_accessed=block_tiles.size * 2 + operand.size * 2 + out_shape[0] * out_shape[1] * 4,
            transcendentals=0,
        ),
    )(row_index, col_index, block_scale, block_tiles, operand)


def forward_local(block_tiles, block_scale, row_index, col_index, operand):
    edge = block_tiles.shape[-1]
    out_shape = (operand.shape[-1], BLK_ROWS * edge)
    return block_product(
        forward_kernel, block_tiles, block_scale, row_index, col_index, operand.T, out_shape
    )


def backward_local(block_tiles, block_scale, row_index, col_index, operand_t, col_count):
    edge = block_tiles.shape[-1]
    out_shape = (operand_t.shape[0], col_count * edge)
    flipped = block_product(
        backward_kernel, block_tiles, block_scale, row_index, col_index, operand_t, out_shape
    )
    return flipped.T


def degree_local(block_tiles, block_scale, row_index, col_index, col_count):
    row_sums = jnp.sum(block_tiles, axis=2, dtype=jnp.float32) * block_scale[:, None]
    col_sums = jnp.sum(block_tiles, axis=1, dtype=jnp.float32) * block_scale[:, None]
    row_select = (row_index[None, :] == jnp.arange(BLK_ROWS, dtype=jnp.int32)[:, None]).astype(
        jnp.float32
    )
    col_select = (col_index[None, :] == jnp.arange(col_count, dtype=jnp.int32)[:, None]).astype(
        jnp.float32
    )
    row_part = jnp.einsum("rb,bi->ri", row_select, row_sums, precision=HIGH).reshape(-1)
    col_part = jnp.einsum("cb,bi->ci", col_select, col_sums, precision=HIGH).reshape(-1)
    return (row_part, col_part)


def gram_of(block):
    return jnp.dot(block.T, block, precision=HIGH)


def factor_kernel(g_ref, o_ref):
    eliminate(g_ref[...], o_ref)


def eliminate(gram, o_ref):
    n = gram.shape[0]
    o_ref[:, :n] = gram
    rows = lax.broadcasted_iota(jnp.int32, (n, 2 * n), 0)
    cols = lax.broadcasted_iota(jnp.int32, (n, 2 * n), 1)
    o_ref[:, n:] = jnp.where(rows[:, n:] == cols[:, n:] - n, 1.0, 0.0).astype(o_ref.dtype)
    m = o_ref[...]
    below = lax.broadcasted_iota(jnp.int32, (n, 1), 0)
    for j in range(n):
        factor = jnp.where(below > j, m[:, j : j + 1], 0.0) * (1.0 / m[j : j + 1, j : j + 1])
        m = m - factor * m[j : j + 1, :]
    diagonal = jnp.sum(jnp.where(rows == cols, m, 0.0), axis=1, keepdims=True)
    m = m * lax.rsqrt(diagonal)
    o_ref[...] = jnp.where((cols < n) & (cols < rows), 0.0, m)


def factor_of(gram_total):
    n = gram_total.shape[0]
    both = pl.pallas_call(
        factor_kernel,
        out_shape=jax.ShapeDtypeStruct((n, 2 * n), jnp.float32),
        in_specs=[pl.BlockSpec(memory_space=pltpu.VMEM)],
        out_specs=pl.BlockSpec(memory_space=pltpu.VMEM),
    )(gram_total)
    return both[:, :n], both[:, n:]


def orthonormal(block, gram_total):
    upper, inverse = factor_of(gram_total)
    basis = jnp.dot(block, inverse.T, precision=HIGH)
    return (basis, upper)


def group_plan(groups, coords):
    plans = []
    for axes, sizes in groups:
        count = 1
        for size in sizes:
            count *= size
        me = 0
        for axis, size in zip(axes, sizes):
            me = me * size + coords[axis]
        targets = []
        for k in range(1, count):
            member = (me + k) % count
            place = list(coords)
            rest = member
            for axis, size in reversed(list(zip(axes, sizes))):
                place[axis] = rest % size
                rest = rest // size
            targets.append((tuple(place), (me + count - k) % count))
        plans.append((count, me, targets))
    return plans


def group_kernel(all_groups, factored, *refs):
    n = len(all_groups)
    x_refs, o_refs = refs[:n], refs[n : 2 * n]
    f_refs, scratch = refs[2 * n : 2 * n + len(factored)], refs[2 * n + len(factored) :]
    coords = [lax.axis_index(name) for name in FINE]
    plans = [group_plan(groups, coords) for groups in all_groups]
    barrier = pltpu.get_barrier_semaphore()
    total = 0
    for plan in plans:
        for count, me, targets in plan:
            for place, _ in targets:
                pl.semaphore_signal(barrier, inc=1, device_id=place, device_id_type=pl.DeviceIdType.MESH)
            total += len(targets)
    pl.semaphore_wait(barrier, total)
    for a in range(n):
        o_refs[a][...] = x_refs[a][...]
    for g in range(max(len(plan) for plan in plans)):
        started = []
        for a in range(n):
            if g >= len(plans[a]):
                continue
            o_ref = o_refs[a]
            slots, send_sem, recv_sem = scratch[3 * a : 3 * a + 3]
            count, me, targets = plans[a][g]
            slots[g, me] = o_ref[...]
            copies = []
            for k, (place, _) in enumerate(targets):
                copy = pltpu.make_async_remote_copy(
                    src_ref=o_ref,
                    dst_ref=slots.at[g, me],
                    send_sem=send_sem.at[g, k],
                    recv_sem=recv_sem.at[g, me],
                    device_id=place,
                    device_id_type=pl.DeviceIdType.MESH,
                )
                copy.start()
                copies.append(copy)
            started.append((a, copies))
        for a, copies in started:
            o_ref = o_refs[a]
            slots, send_sem, recv_sem = scratch[3 * a : 3 * a + 3]
            count, me, targets = plans[a][g]
            for copy in copies:
                copy.wait_send()
            for place, sender in targets:
                pltpu.make_async_remote_copy(
                    src_ref=o_ref,
                    dst_ref=slots.at[g, sender],
                    send_sem=send_sem.at[g, 0],
                    recv_sem=recv_sem.at[g, sender],
                    device_id=place,
                    device_id_type=pl.DeviceIdType.MESH,
                ).wait_recv()
            acc = slots[g, 0]
            for j in range(1, count):
                acc = acc + slots[g, j]
            o_ref[...] = acc
    for a, f_ref in zip(factored, f_refs):
        eliminate(o_refs[a][...], f_ref)


def group_sums(values, all_groups, cid, factored=()):
    specs, flats, scratch = [], [], []
    for value, groups in zip(values, all_groups):
        spec = []
        widest = 1
        for names in groups:
            sizes = tuple(lax.axis_size(name) for name in names)
            count = 1
            for size in sizes:
                count *= size
            widest = max(widest, count)
            spec.append((tuple(FINE.index(name) for name in names), sizes))
        flat = value.reshape(-1, 128) if value.ndim == 1 else value
        specs.append(tuple(spec))
        flats.append(flat)
        scratch += [
            pltpu.VMEM((len(spec), widest) + flat.shape, flat.dtype),
            pltpu.SemaphoreType.DMA((len(spec), widest)),
            pltpu.SemaphoreType.DMA((len(spec), widest)),
        ]
    out_shape = [jax.ShapeDtypeStruct(flat.shape, flat.dtype) for flat in flats]
    out_shape += [jax.ShapeDtypeStruct((flats[a].shape[0], 2 * flats[a].shape[0]), jnp.float32) for a in factored]
    outs = pl.pallas_call(
        functools.partial(group_kernel, tuple(specs), tuple(factored)),
        out_shape=out_shape,
        in_specs=[pl.BlockSpec(memory_space=pltpu.VMEM)] * len(flats),
        out_specs=[pl.BlockSpec(memory_space=pltpu.VMEM)] * len(out_shape),
        scratch_shapes=scratch,
        compiler_params=pltpu.CompilerParams(collective_id=cid, has_side_effects=True),
    )(*flats)
    sums = [out.reshape(value.shape) for out, value in zip(outs, values)]
    factors = []
    for both in outs[len(flats) :]:
        half = both.shape[0]
        factors.append((both[:, :half], both[:, half:]))
    return sums, factors


def group_sum(value, groups, cid):
    return group_sums([value], [groups], cid)[0][0]


def group_factor(value, groups, cid):
    return group_sums([value], [groups], cid, factored=(0,))[1][0]


ALL_GROUPS = (FEAT, ("z",), ("yh", "x"))
CLAIM_GROUPS = (("z",), ("yh", "x"))


def halving_kernel(stages, gather, x_ref, o_ref, *scratch):
    if gather:
        work, recv, back, rs_send, rs_recv, ag_send, ag_recv = o_ref, *scratch
    else:
        work, recv, rs_send, rs_recv = scratch
    coords = [lax.axis_index(name) for name in FINE]
    partners, bits = [], []
    for axis, step in stages:
        place = coords[axis]
        bit = (place // step) % 2
        flip = place + step * (1 - 2 * bit)
        partners.append(tuple(flip if i == axis else c for i, c in enumerate(coords)))
        bits.append(bit)
    barrier = pltpu.get_barrier_semaphore()
    for partner in partners:
        pl.semaphore_signal(barrier, inc=1, device_id=partner, device_id_type=pl.DeviceIdType.MESH)
    pl.semaphore_wait(barrier, len(partners))
    work[...] = x_ref[...]
    total = work.shape[0]
    base = 0
    pieces = []
    for s, partner in enumerate(partners):
        size = total >> s
        half = size // 2
        keep = base + bits[s] * half
        give = base + (1 - bits[s]) * half
        slot = pl.ds(total - size, half)
        copy = pltpu.make_async_remote_copy(
            src_ref=work.at[pl.ds(give, half)],
            dst_ref=recv.at[slot],
            send_sem=rs_send.at[s],
            recv_sem=rs_recv.at[s],
            device_id=partner,
            device_id_type=pl.DeviceIdType.MESH,
        )
        copy.start()
        copy.wait()
        work[pl.ds(keep, half), :] = work[pl.ds(keep, half), :] + recv[slot, :]
        pieces.append((keep, give, slot))
        base = keep
    if gather:
        for s in reversed(range(len(partners))):
            keep, give, slot = pieces[s]
            copy = pltpu.make_async_remote_copy(
                src_ref=work.at[pl.ds(keep, slot.size)],
                dst_ref=back.at[slot],
                send_sem=ag_send.at[s],
                recv_sem=ag_recv.at[s],
                device_id=partners[s],
                device_id_type=pl.DeviceIdType.MESH,
            )
            copy.start()
            copy.wait()
            work[pl.ds(give, slot.size), :] = back[slot, :]
    else:
        o_ref[...] = work[pl.ds(base, o_ref.shape[0]), :]


CLAIM_STAGES = (("z", 1), ("x", 1), ("z", 2), ("x", 2), ("yh", 1), ("z", 4))


def claim_halving(value, gather, cid):
    stages = tuple((FINE.index(name), step) for name, step in CLAIM_STAGES)
    count = len(stages)
    flat = value.reshape(-1, 128)
    rows = flat.shape[0]
    out_rows = rows if gather else rows >> count
    scratch = [] if gather else [pltpu.VMEM(flat.shape, flat.dtype)]
    scratch += [pltpu.VMEM(flat.shape, flat.dtype)] * (2 if gather else 1)
    scratch += [pltpu.SemaphoreType.DMA((count,))] * (4 if gather else 2)
    out = pl.pallas_call(
        functools.partial(halving_kernel, stages, gather),
        out_shape=jax.ShapeDtypeStruct((out_rows, 128), flat.dtype),
        in_specs=[pl.BlockSpec(memory_space=pltpu.VMEM)],
        out_specs=pl.BlockSpec(memory_space=pltpu.VMEM),
        scratch_shapes=scratch,
        compiler_params=pltpu.CompilerParams(collective_id=cid, has_side_effects=True),
    )(flat)
    return out


def claim_sum(value):
    part = lax.psum_scatter(value, "z", scatter_dimension=0, tiled=True)
    part = lax.psum(part, ("yh", "x"))
    return lax.all_gather(part, "z", axis=0, tiled=True)


def all_sum(value):
    value = lax.psum(value, FEAT)
    value = lax.psum(value, "z")
    return lax.psum(value, ("yh", "x"))


def claim_scatter(value):
    width = value.shape[-1]
    rows = value.shape[0] // lax.axis_size(CLAIM)
    bits = value.reshape(2, 2, 2, 2, 2, 2, rows, width)
    ordered = bits.transpose(5, 2, 4, 1, 0, 3, 6, 7).reshape(value.shape)
    return claim_halving(ordered, False, 5).reshape(rows, width)


def per_device(block_tiles, block_scale, row_index, col_index, start_basis):
    tiles_here = block_tiles.reshape(block_tiles.shape[-3:])
    scale_here = block_scale.reshape(-1)
    rows_here = row_index.reshape(-1)
    cols_here = col_index.reshape(-1)
    edge = tiles_here.shape[-1]
    col_count = start_basis.shape[0] // edge
    claim_count = lax.axis_size(CLAIM)
    own_cols = start_basis.shape[0] // claim_count
    own_first = lax.axis_index(CLAIM) * own_cols
    row_part, col_part = degree_local(tiles_here, scale_here, rows_here, cols_here, col_count)
    (col_total, row_total, _), (start_factor,) = group_sums(
        [col_part, row_part, gram_of(start_basis)], [CLAIM_GROUPS, (FEAT,), (FEAT,)], 0, factored=(2,)
    )
    col_scale = lax.rsqrt(col_total + 1.0)
    row_scale_all = lax.rsqrt(row_total + 1.0)
    own_rows = row_part.shape[0] // lax.axis_size(FEAT)
    own_start = lax.axis_index(FEAT) * own_rows
    row_scale = lax.dynamic_slice_in_dim(row_scale_all, own_start, own_rows, 0)
    first_basis = jnp.dot(start_basis, start_factor[1].T, precision=HIGH)
    first_operand = (col_scale[:, None] * first_basis).astype(jnp.bfloat16)
    first_partial = forward_local(tiles_here, scale_here, rows_here, cols_here, first_operand)

    def row_step(partial_t, previous_t, coupling, cid):
        sums_t = lax.psum_scatter(partial_t, FEAT, scatter_dimension=1, tiled=True)
        all_t = lax.all_gather(sums_t, FEAT, axis=1, tiled=True)
        block_t = row_scale[None, :] * sums_t
        wide_t = row_scale_all[None, :] * all_t
        if previous_t is not None:
            own_previous = lax.dynamic_slice_in_dim(previous_t, own_start, own_rows, 1)
            block_t = block_t - jnp.dot(coupling, own_previous, precision=HIGH)
            wide_t = wide_t - jnp.dot(coupling, previous_t, precision=HIGH)
        gram = jnp.dot(block_t, block_t.T, precision=HIGH)
        upper, inverse = group_factor(gram, ALL_GROUPS, cid)
        return jnp.dot(inverse, wide_t, precision=HIGH), upper

    def backward_partial(basis_t):
        operand_t = (row_scale_all[None, :] * basis_t).astype(jnp.bfloat16)
        return backward_local(tiles_here, scale_here, rows_here, cols_here, operand_t, col_count)

    u_first, b_first = row_step(first_partial, None, None, 1)
    summed = claim_halving(backward_partial(u_first), True, 4).reshape(-1, first_basis.shape[-1])
    update = col_scale[:, None] * summed - jnp.dot(first_basis, b_first.T, precision=HIGH)
    v_second, a_second = orthonormal(update, lax.psum(gram_of(update), FEAT))
    scaled = (col_scale[:, None] * v_second).astype(jnp.bfloat16)
    second_partial = forward_local(tiles_here, scale_here, rows_here, cols_here, scaled)
    u_second, b_second = row_step(second_partial, u_first, a_second, 2)
    own_sums = claim_scatter(backward_partial(u_second))
    own_scale = lax.dynamic_slice_in_dim(col_scale, own_first, own_cols, 0)
    own_second = lax.dynamic_slice_in_dim(v_second, own_first, own_cols, 0)
    q_second = own_scale[:, None] * own_sums - jnp.dot(own_second, b_second.T, precision=HIGH)
    a_third, third_inverse = group_factor(gram_of(q_second), ALL_GROUPS, 3)
    v_output = jnp.dot(q_second, third_inverse.T, precision=HIGH)
    bidiagonal = jnp.stack([b_first, a_second, b_second, a_third])
    u_output = lax.dynamic_slice_in_dim(u_second, own_start, own_rows, 1).T
    return (u_output, v_output, bidiagonal)


def solution(mesh):
    claim_n, feat_n = mesh.devices.shape
    fine = Mesh(mesh.devices.reshape(2, claim_n // 16, 8, 2, feat_n // 2), FINE)
    placed = (
        P(CLAIM, FEAT, None, None, None),
        P(CLAIM, FEAT, None),
        P(CLAIM, FEAT, None),
        P(CLAIM, FEAT, None),
        P(FEAT, None),
    )
    return jax.shard_map(
        per_device,
        mesh=fine,
        in_specs=placed,
        out_specs=(P(CLAIM + FEAT, None), P(FEAT + CLAIM, None), P()),
        check_vma=False,
    )
```

```python
import functools

import jax
import jax.numpy as jnp
from jax import lax
from jax.experimental import pallas as pl
from jax.experimental.pallas import tpu as pltpu
from jax.sharding import Mesh
from jax.sharding import PartitionSpec as P

BLK_ROWS = 64

HIGH = lax.Precision.HIGHEST

FINE = ("yh", "x", "z", "yl", "c")
CLAIM = ("yh", "x", "z")
FEAT = ("yl", "c")


TILES_PER_STEP = 16


def forward_kernel(rows_ref, cols_ref, scale_ref, tiles_ref, operand_ref, out_ref):
    step = pl.program_id(0)
    edge = tiles_ref.shape[-1]

    @pl.when(step == 0)
    def _():
        out_ref[...] = jnp.zeros_like(out_ref)

    for t in range(tiles_ref.shape[0]):
        b = step * tiles_ref.shape[0] + t
        picked = operand_ref[:, pl.ds(pl.multiple_of(cols_ref[b] * edge, edge), edge)]
        product = lax.dot_general(
            picked, tiles_ref[t], (((1,), (1,)), ((), ())), preferred_element_type=jnp.float32
        )
        target = pl.ds(pl.multiple_of(rows_ref[b] * edge, edge), edge)
        out_ref[:, target] = out_ref[:, target] + product * scale_ref[b]


def backward_kernel(rows_ref, cols_ref, scale_ref, tiles_ref, operand_ref, out_ref):
    step = pl.program_id(0)
    edge = tiles_ref.shape[-1]

    @pl.when(step == 0)
    def _():
        out_ref[...] = jnp.zeros_like(out_ref)

    for t in range(tiles_ref.shape[0]):
        b = step * tiles_ref.shape[0] + t
        picked = operand_ref[:, pl.ds(pl.multiple_of(rows_ref[b] * edge, edge), edge)]
        product = jnp.dot(picked, tiles_ref[t], preferred_element_type=jnp.float32) * scale_ref[b]
        target = pl.ds(pl.multiple_of(cols_ref[b] * edge, edge), edge)
        out_ref[:, target] = out_ref[:, target] + product


def block_product(kernel, block_tiles, block_scale, row_index, col_index, operand, out_shape):
    count, edge, _ = block_tiles.shape
    per = TILES_PER_STEP
    grid_spec = pltpu.PrefetchScalarGridSpec(
        num_scalar_prefetch=2,
        grid=(count // per,),
        in_specs=[
            pl.BlockSpec(memory_space=pltpu.SMEM),
            pl.BlockSpec((per, edge, edge), lambda i, rows, cols: (i, 0, 0)),
            pl.BlockSpec(operand.shape, lambda i, rows, cols: (0, 0)),
        ],
        out_specs=pl.BlockSpec(out_shape, lambda i, rows, cols: (0, 0)),
    )
    width = min(operand.shape)
    return pl.pallas_call(
        kernel,
        grid_spec=grid_spec,
        out_shape=jax.ShapeDtypeStruct(out_shape, jnp.float32),
        cost_estimate=pl.CostEstimate(
            flops=2 * count * edge * edge * width,
            bytes_accessed=block_tiles.size * 2 + operand.size * 2 + out_shape[0] * out_shape[1] * 4,
            transcendentals=0,
        ),
    )(row_index, col_index, block_scale, block_tiles, operand)


def forward_local(block_tiles, block_scale, row_index, col_index, operand):
    edge = block_tiles.shape[-1]
    out_shape = (operand.shape[-1], BLK_ROWS * edge)
    return block_product(
        forward_kernel, block_tiles, block_scale, row_index, col_index, operand.T, out_shape
    )


def backward_local(block_tiles, block_scale, row_index, col_index, operand_t, col_count):
    edge = block_tiles.shape[-1]
    out_shape = (operand_t.shape[0], col_count * edge)
    flipped = block_product(
        backward_kernel, block_tiles, block_scale, row_index, col_index, operand_t, out_shape
    )
    return flipped.T


def degree_local(block_tiles, block_scale, row_index, col_index, col_count):
    row_sums = jnp.sum(block_tiles, axis=2, dtype=jnp.float32) * block_scale[:, None]
    col_sums = jnp.sum(block_tiles, axis=1, dtype=jnp.float32) * block_scale[:, None]
    row_select = (row_index[None, :] == jnp.arange(BLK_ROWS, dtype=jnp.int32)[:, None]).astype(
        jnp.float32
    )
    col_select = (col_index[None, :] == jnp.arange(col_count, dtype=jnp.int32)[:, None]).astype(
        jnp.float32
    )
    row_part = jnp.einsum("rb,bi->ri", row_select, row_sums, precision=HIGH).reshape(-1)
    col_part = jnp.einsum("cb,bi->ci", col_select, col_sums, precision=HIGH).reshape(-1)
    return (row_part, col_part)


def gram_of(block):
    return jnp.dot(block.T, block, precision=HIGH)


def factor_kernel(g_ref, o_ref):
    eliminate(g_ref[...], o_ref)


def eliminate(gram, o_ref):
    n = gram.shape[0]
    o_ref[:, :n] = gram
    rows = lax.broadcasted_iota(jnp.int32, (n, 2 * n), 0)
    cols = lax.broadcasted_iota(jnp.int32, (n, 2 * n), 1)
    o_ref[:, n:] = jnp.where(rows[:, n:] == cols[:, n:] - n, 1.0, 0.0).astype(o_ref.dtype)
    m = o_ref[...]
    below = lax.broadcasted_iota(jnp.int32, (n, 1), 0)
    for j in range(n):
        factor = jnp.where(below > j, m[:, j : j + 1], 0.0) * (1.0 / m[j : j + 1, j : j + 1])
        m = m - factor * m[j : j + 1, :]
    diagonal = jnp.sum(jnp.where(rows == cols, m, 0.0), axis=1, keepdims=True)
    m = m * lax.rsqrt(diagonal)
    o_ref[...] = jnp.where((cols < n) & (cols < rows), 0.0, m)


def factor_of(gram_total):
    n = gram_total.shape[0]
    both = pl.pallas_call(
        factor_kernel,
        out_shape=jax.ShapeDtypeStruct((n, 2 * n), jnp.float32),
        in_specs=[pl.BlockSpec(memory_space=pltpu.VMEM)],
        out_specs=pl.BlockSpec(memory_space=pltpu.VMEM),
    )(gram_total)
    return both[:, :n], both[:, n:]


def orthonormal(block, gram_total):
    upper, inverse = factor_of(gram_total)
    basis = jnp.dot(block, inverse.T, precision=HIGH)
    return (basis, upper)


def group_plan(groups, coords):
    plans = []
    for axes, sizes in groups:
        count = 1
        for size in sizes:
            count *= size
        me = 0
        for axis, size in zip(axes, sizes):
            me = me * size + coords[axis]
        targets = []
        for k in range(1, count):
            member = (me + k) % count
            place = list(coords)
            rest = member
            for axis, size in reversed(list(zip(axes, sizes))):
                place[axis] = rest % size
                rest = rest // size
            targets.append((tuple(place), (me + count - k) % count))
        plans.append((count, me, targets))
    return plans


def group_kernel(all_groups, factored, *refs):
    n = len(all_groups)
    x_refs, o_refs = refs[:n], refs[n : 2 * n]
    f_refs, scratch = refs[2 * n : 2 * n + len(factored)], refs[2 * n + len(factored) :]
    coords = [lax.axis_index(name) for name in FINE]
    plans = [group_plan(groups, coords) for groups in all_groups]
    barrier = pltpu.get_barrier_semaphore()
    total = 0
    for plan in plans:
        for count, me, targets in plan:
            for place, _ in targets:
                pl.semaphore_signal(barrier, inc=1, device_id=place, device_id_type=pl.DeviceIdType.MESH)
            total += len(targets)
    pl.semaphore_wait(barrier, total)
    for a in range(n):
        o_refs[a][...] = x_refs[a][...]
    for g in range(max(len(plan) for plan in plans)):
        started = []
        for a in range(n):
            if g >= len(plans[a]):
                continue
            o_ref = o_refs[a]
            slots, send_sem, recv_sem = scratch[3 * a : 3 * a + 3]
            count, me, targets = plans[a][g]
            slots[g, me] = o_ref[...]
            copies = []
            for k, (place, _) in enumerate(targets):
                copy = pltpu.make_async_remote_copy(
                    src_ref=o_ref,
                    dst_ref=slots.at[g, me],
                    send_sem=send_sem.at[g, k],
                    recv_sem=recv_sem.at[g, me],
                    device_id=place,
                    device_id_type=pl.DeviceIdType.MESH,
                )
                copy.start()
                copies.append(copy)
            started.append((a, copies))
        for a, copies in started:
            o_ref = o_refs[a]
            slots, send_sem, recv_sem = scratch[3 * a : 3 * a + 3]
            count, me, targets = plans[a][g]
            for copy in copies:
                copy.wait_send()
            for place, sender in targets:
                pltpu.make_async_remote_copy(
                    src_ref=o_ref,
                    dst_ref=slots.at[g, sender],
                    send_sem=send_sem.at[g, 0],
                    recv_sem=recv_sem.at[g, sender],
                    device_id=place,
                    device_id_type=pl.DeviceIdType.MESH,
                ).wait_recv()
            acc = slots[g, 0]
            for j in range(1, count):
                acc = acc + slots[g, j]
            o_ref[...] = acc
    for a, f_ref in zip(factored, f_refs):
        eliminate(o_refs[a][...], f_ref)


def group_sums(values, all_groups, cid, factored=()):
    specs, flats, scratch = [], [], []
    for value, groups in zip(values, all_groups):
        spec = []
        widest = 1
        for names in groups:
            sizes = tuple(lax.axis_size(name) for name in names)
            count = 1
            for size in sizes:
                count *= size
            widest = max(widest, count)
            spec.append((tuple(FINE.index(name) for name in names), sizes))
        flat = value.reshape(-1, 128) if value.ndim == 1 else value
        specs.append(tuple(spec))
        flats.append(flat)
        scratch += [
            pltpu.VMEM((len(spec), widest) + flat.shape, flat.dtype),
            pltpu.SemaphoreType.DMA((len(spec), widest)),
            pltpu.SemaphoreType.DMA((len(spec), widest)),
        ]
    out_shape = [jax.ShapeDtypeStruct(flat.shape, flat.dtype) for flat in flats]
    out_shape += [jax.ShapeDtypeStruct((flats[a].shape[0], 2 * flats[a].shape[0]), jnp.float32) for a in factored]
    outs = pl.pallas_call(
        functools.partial(group_kernel, tuple(specs), tuple(factored)),
        out_shape=out_shape,
        in_specs=[pl.BlockSpec(memory_space=pltpu.VMEM)] * len(flats),
        out_specs=[pl.BlockSpec(memory_space=pltpu.VMEM)] * len(out_shape),
        scratch_shapes=scratch,
        compiler_params=pltpu.CompilerParams(collective_id=cid, has_side_effects=True),
    )(*flats)
    sums = [out.reshape(value.shape) for out, value in zip(outs, values)]
    factors = []
    for both in outs[len(flats) :]:
        half = both.shape[0]
        factors.append((both[:, :half], both[:, half:]))
    return sums, factors


def group_sum(value, groups, cid):
    return group_sums([value], [groups], cid)[0][0]


def group_factor(value, groups, cid):
    return group_sums([value], [groups], cid, factored=(0,))[1][0]


ALL_GROUPS = (FEAT, ("z",), ("yh", "x"))
CLAIM_GROUPS = (("z",), ("yh", "x"))


def halving_kernel(stages, gather, x_ref, o_ref, *scratch):
    if gather:
        work, recv, back, rs_send, rs_recv, ag_send, ag_recv = o_ref, *scratch
    else:
        work, recv, rs_send, rs_recv = scratch
    coords = [lax.axis_index(name) for name in FINE]
    partners, bits = [], []
    for axis, step in stages:
        place = coords[axis]
        bit = (place // step) % 2
        flip = place + step * (1 - 2 * bit)
        partners.append(tuple(flip if i == axis else c for i, c in enumerate(coords)))
        bits.append(bit)
    barrier = pltpu.get_barrier_semaphore()
    for partner in partners:
        pl.semaphore_signal(barrier, inc=1, device_id=partner, device_id_type=pl.DeviceIdType.MESH)
    pl.semaphore_wait(barrier, len(partners))
    work[...] = x_ref[...]
    total = work.shape[0]
    base = 0
    pieces = []
    for s, partner in enumerate(partners):
        size = total >> s
        half = size // 2
        keep = base + bits[s] * half
        give = base + (1 - bits[s]) * half
        slot = pl.ds(total - size, half)
        copy = pltpu.make_async_remote_copy(
            src_ref=work.at[pl.ds(give, half)],
            dst_ref=recv.at[slot],
            send_sem=rs_send.at[s],
            recv_sem=rs_recv.at[s],
            device_id=partner,
            device_id_type=pl.DeviceIdType.MESH,
        )
        copy.start()
        copy.wait()
        work[pl.ds(keep, half), :] = work[pl.ds(keep, half), :] + recv[slot, :]
        pieces.append((keep, give, slot))
        base = keep
    if gather:
        for s in reversed(range(len(partners))):
            keep, give, slot = pieces[s]
            copy = pltpu.make_async_remote_copy(
                src_ref=work.at[pl.ds(keep, slot.size)],
                dst_ref=back.at[slot],
                send_sem=ag_send.at[s],
                recv_sem=ag_recv.at[s],
                device_id=partners[s],
                device_id_type=pl.DeviceIdType.MESH,
            )
            copy.start()
            copy.wait()
            work[pl.ds(give, slot.size), :] = back[slot, :]
    else:
        o_ref[...] = work[pl.ds(base, o_ref.shape[0]), :]


CLAIM_STAGES = (("z", 1), ("x", 1), ("z", 2), ("x", 2), ("yh", 1), ("z", 4))


def claim_halving(value, gather, cid):
    stages = tuple((FINE.index(name), step) for name, step in CLAIM_STAGES)
    count = len(stages)
    flat = value.reshape(-1, 128)
    rows = flat.shape[0]
    out_rows = rows if gather else rows >> count
    scratch = [] if gather else [pltpu.VMEM(flat.shape, flat.dtype)]
    scratch += [pltpu.VMEM(flat.shape, flat.dtype)] * (2 if gather else 1)
    scratch += [pltpu.SemaphoreType.DMA((count,))] * (4 if gather else 2)
    out = pl.pallas_call(
        functools.partial(halving_kernel, stages, gather),
        out_shape=jax.ShapeDtypeStruct((out_rows, 128), flat.dtype),
        in_specs=[pl.BlockSpec(memory_space=pltpu.VMEM)],
        out_specs=pl.BlockSpec(memory_space=pltpu.VMEM),
        scratch_shapes=scratch,
        compiler_params=pltpu.CompilerParams(collective_id=cid, has_side_effects=True),
    )(flat)
    return out


def claim_sum(value):
    part = lax.psum_scatter(value, "z", scatter_dimension=0, tiled=True)
    part = lax.psum(part, ("yh", "x"))
    return lax.all_gather(part, "z", axis=0, tiled=True)


def all_sum(value):
    value = lax.psum(value, FEAT)
    value = lax.psum(value, "z")
    return lax.psum(value, ("yh", "x"))


def claim_scatter(value):
    width = value.shape[-1]
    rows = value.shape[0] // lax.axis_size(CLAIM)
    bits = value.reshape(2, 2, 2, 2, 2, 2, rows, width)
    ordered = bits.transpose(5, 2, 4, 1, 0, 3, 6, 7).reshape(value.shape)
    return claim_halving(ordered, False, 5).reshape(rows, width)


def per_device(block_tiles, block_scale, row_index, col_index, start_basis):
    tiles_here = block_tiles.reshape(block_tiles.shape[-3:])
    scale_here = block_scale.reshape(-1)
    rows_here = row_index.reshape(-1)
    cols_here = col_index.reshape(-1)
    edge = tiles_here.shape[-1]
    col_count = start_basis.shape[0] // edge
    claim_count = lax.axis_size(CLAIM)
    own_cols = start_basis.shape[0] // claim_count
    own_first = lax.axis_index(CLAIM) * own_cols
    row_part, col_part = degree_local(tiles_here, scale_here, rows_here, cols_here, col_count)
    (col_total, row_total, _), (start_factor,) = group_sums(
        [col_part, row_part, gram_of(start_basis)], [CLAIM_GROUPS, (FEAT,), (FEAT,)], 0, factored=(2,)
    )
    col_scale = lax.rsqrt(col_total + 1.0)
    row_scale_all = lax.rsqrt(row_total + 1.0)
    own_rows = row_part.shape[0] // lax.axis_size(FEAT)
    own_start = lax.axis_index(FEAT) * own_rows
    row_scale = lax.dynamic_slice_in_dim(row_scale_all, own_start, own_rows, 0)
    first_basis = jnp.dot(start_basis, start_factor[1].T, precision=HIGH)
    first_operand = (col_scale[:, None] * first_basis).astype(jnp.bfloat16)
    first_partial = forward_local(tiles_here, scale_here, rows_here, cols_here, first_operand)

    def row_step(partial_t, previous_t, coupling, cid):
        sums_t = lax.psum_scatter(partial_t, FEAT, scatter_dimension=1, tiled=True)
        all_t = lax.all_gather(sums_t, FEAT, axis=1, tiled=True)
        block_t = row_scale[None, :] * sums_t
        wide_t = row_scale_all[None, :] * all_t
        if previous_t is not None:
            own_previous = lax.dynamic_slice_in_dim(previous_t, own_start, own_rows, 1)
            block_t = block_t - jnp.dot(coupling, own_previous, precision=HIGH)
            wide_t = wide_t - jnp.dot(coupling, previous_t, precision=HIGH)
        gram = jnp.dot(block_t, block_t.T, precision=HIGH)
        upper, inverse = group_factor(gram, ALL_GROUPS, cid)
        return jnp.dot(inverse, wide_t, precision=HIGH), upper

    def backward_partial(basis_t):
        operand_t = (row_scale_all[None, :] * basis_t).astype(jnp.bfloat16)
        return backward_local(tiles_here, scale_here, rows_here, cols_here, operand_t, col_count)

    u_first, b_first = row_step(first_partial, None, None, 1)
    summed = claim_halving(backward_partial(u_first), True, 4).reshape(-1, first_basis.shape[-1])
    update = col_scale[:, None] * summed - jnp.dot(first_basis, b_first.T, precision=HIGH)
    a_second, second_inverse = group_factor(gram_of(update), (FEAT,), 6)
    v_second = jnp.dot(update, second_inverse.T, precision=HIGH)
    scaled = (col_scale[:, None] * v_second).astype(jnp.bfloat16)
    second_partial = forward_local(tiles_here, scale_here, rows_here, cols_here, scaled)
    u_second, b_second = row_step(second_partial, u_first, a_second, 2)
    own_sums = claim_scatter(backward_partial(u_second))
    own_scale = lax.dynamic_slice_in_dim(col_scale, own_first, own_cols, 0)
    own_second = lax.dynamic_slice_in_dim(v_second, own_first, own_cols, 0)
    q_second = own_scale[:, None] * own_sums - jnp.dot(own_second, b_second.T, precision=HIGH)
    a_third, third_inverse = group_factor(gram_of(q_second), ALL_GROUPS, 3)
    v_output = jnp.dot(q_second, third_inverse.T, precision=HIGH)
    bidiagonal = jnp.stack([b_first, a_second, b_second, a_third])
    u_output = lax.dynamic_slice_in_dim(u_second, own_start, own_rows, 1).T
    return (u_output, v_output, bidiagonal)


def solution(mesh):
    claim_n, feat_n = mesh.devices.shape
    fine = Mesh(mesh.devices.reshape(2, claim_n // 16, 8, 2, feat_n // 2), FINE)
    placed = (
        P(CLAIM, FEAT, None, None, None),
        P(CLAIM, FEAT, None),
        P(CLAIM, FEAT, None),
        P(CLAIM, FEAT, None),
        P(FEAT, None),
    )
    return jax.shard_map(
        per_device,
        mesh=fine,
        in_specs=placed,
        out_specs=(P(CLAIM + FEAT, None), P(FEAT + CLAIM, None), P()),
        check_vma=False,
    )
```

```python
import functools

import jax
import jax.numpy as jnp
from jax import lax
from jax.experimental import pallas as pl
from jax.experimental.pallas import tpu as pltpu
from jax.sharding import Mesh
from jax.sharding import PartitionSpec as P

BLK_ROWS = 64

HIGH = lax.Precision.HIGHEST

FINE = ("yh", "x", "z", "yl", "c")
CLAIM = ("yh", "x", "z")
FEAT = ("yl", "c")


TILES_PER_STEP = 16


def forward_kernel(rows_ref, cols_ref, scale_ref, tiles_ref, operand_ref, out_ref):
    step = pl.program_id(0)
    edge = tiles_ref.shape[-1]

    @pl.when(step == 0)
    def _():
        out_ref[...] = jnp.zeros_like(out_ref)

    for t in range(tiles_ref.shape[0]):
        b = step * tiles_ref.shape[0] + t
        picked = operand_ref[:, pl.ds(pl.multiple_of(cols_ref[b] * edge, edge), edge)]
        product = lax.dot_general(
            picked, tiles_ref[t], (((1,), (1,)), ((), ())), preferred_element_type=jnp.float32
        )
        target = pl.ds(pl.multiple_of(rows_ref[b] * edge, edge), edge)
        out_ref[:, target] = out_ref[:, target] + product * scale_ref[b]


def backward_kernel(rows_ref, cols_ref, scale_ref, tiles_ref, operand_ref, out_ref):
    step = pl.program_id(0)
    edge = tiles_ref.shape[-1]

    @pl.when(step == 0)
    def _():
        out_ref[...] = jnp.zeros_like(out_ref)

    for t in range(tiles_ref.shape[0]):
        b = step * tiles_ref.shape[0] + t
        picked = operand_ref[:, pl.ds(pl.multiple_of(rows_ref[b] * edge, edge), edge)]
        product = jnp.dot(picked, tiles_ref[t], preferred_element_type=jnp.float32) * scale_ref[b]
        target = pl.ds(pl.multiple_of(cols_ref[b] * edge, edge), edge)
        out_ref[:, target] = out_ref[:, target] + product


def block_product(kernel, block_tiles, block_scale, row_index, col_index, operand, out_shape):
    count, edge, _ = block_tiles.shape
    per = TILES_PER_STEP
    grid_spec = pltpu.PrefetchScalarGridSpec(
        num_scalar_prefetch=2,
        grid=(count // per,),
        in_specs=[
            pl.BlockSpec(memory_space=pltpu.SMEM),
            pl.BlockSpec((per, edge, edge), lambda i, rows, cols: (i, 0, 0)),
            pl.BlockSpec(operand.shape, lambda i, rows, cols: (0, 0)),
        ],
        out_specs=pl.BlockSpec(out_shape, lambda i, rows, cols: (0, 0)),
    )
    width = min(operand.shape)
    return pl.pallas_call(
        kernel,
        grid_spec=grid_spec,
        out_shape=jax.ShapeDtypeStruct(out_shape, jnp.float32),
        cost_estimate=pl.CostEstimate(
            flops=2 * count * edge * edge * width,
            bytes_accessed=block_tiles.size * 2 + operand.size * 2 + out_shape[0] * out_shape[1] * 4,
            transcendentals=0,
        ),
    )(row_index, col_index, block_scale, block_tiles, operand)


def forward_local(block_tiles, block_scale, row_index, col_index, operand):
    edge = block_tiles.shape[-1]
    out_shape = (operand.shape[-1], BLK_ROWS * edge)
    return block_product(
        forward_kernel, block_tiles, block_scale, row_index, col_index, operand.T, out_shape
    )


def backward_local(block_tiles, block_scale, row_index, col_index, operand_t, col_count):
    edge = block_tiles.shape[-1]
    out_shape = (operand_t.shape[0], col_count * edge)
    flipped = block_product(
        backward_kernel, block_tiles, block_scale, row_index, col_index, operand_t, out_shape
    )
    return flipped.T


def degree_local(block_tiles, block_scale, row_index, col_index, col_count):
    row_sums = jnp.sum(block_tiles, axis=2, dtype=jnp.float32) * block_scale[:, None]
    col_sums = jnp.sum(block_tiles, axis=1, dtype=jnp.float32) * block_scale[:, None]
    row_select = (row_index[None, :] == jnp.arange(BLK_ROWS, dtype=jnp.int32)[:, None]).astype(
        jnp.float32
    )
    col_select = (col_index[None, :] == jnp.arange(col_count, dtype=jnp.int32)[:, None]).astype(
        jnp.float32
    )
    row_part = jnp.einsum("rb,bi->ri", row_select, row_sums, precision=HIGH).reshape(-1)
    col_part = jnp.einsum("cb,bi->ci", col_select, col_sums, precision=HIGH).reshape(-1)
    return (row_part, col_part)


def gram_of(block):
    return jnp.dot(block.T, block, precision=HIGH)


def factor_kernel(g_ref, o_ref):
    eliminate(g_ref[...], o_ref)


def eliminate(gram, o_ref):
    n = gram.shape[0]
    o_ref[:, :n] = gram
    rows = lax.broadcasted_iota(jnp.int32, (n, 2 * n), 0)
    cols = lax.broadcasted_iota(jnp.int32, (n, 2 * n), 1)
    o_ref[:, n:] = jnp.where(rows[:, n:] == cols[:, n:] - n, 1.0, 0.0).astype(o_ref.dtype)
    m = o_ref[...]
    below = lax.broadcasted_iota(jnp.int32, (n, 1), 0)
    for j in range(n):
        factor = jnp.where(below > j, m[:, j : j + 1], 0.0) * (1.0 / m[j : j + 1, j : j + 1])
        m = m - factor * m[j : j + 1, :]
    diagonal = jnp.sum(jnp.where(rows == cols, m, 0.0), axis=1, keepdims=True)
    m = m * lax.rsqrt(diagonal)
    o_ref[...] = jnp.where((cols < n) & (cols < rows), 0.0, m)


def factor_of(gram_total):
    n = gram_total.shape[0]
    both = pl.pallas_call(
        factor_kernel,
        out_shape=jax.ShapeDtypeStruct((n, 2 * n), jnp.float32),
        in_specs=[pl.BlockSpec(memory_space=pltpu.VMEM)],
        out_specs=pl.BlockSpec(memory_space=pltpu.VMEM),
    )(gram_total)
    return both[:, :n], both[:, n:]


def orthonormal(block, gram_total):
    upper, inverse = factor_of(gram_total)
    basis = jnp.dot(block, inverse.T, precision=HIGH)
    return (basis, upper)


def group_plan(groups, coords):
    plans = []
    for axes, sizes in groups:
        count = 1
        for size in sizes:
            count *= size
        me = 0
        for axis, size in zip(axes, sizes):
            me = me * size + coords[axis]
        targets = []
        for k in range(1, count):
            member = (me + k) % count
            place = list(coords)
            rest = member
            for axis, size in reversed(list(zip(axes, sizes))):
                place[axis] = rest % size
                rest = rest // size
            targets.append((tuple(place), (me + count - k) % count))
        plans.append((count, me, targets))
    return plans


def group_kernel(all_groups, factored, *refs):
    n = len(all_groups)
    x_refs, o_refs = refs[:n], refs[n : 2 * n]
    f_refs, scratch = refs[2 * n : 2 * n + len(factored)], refs[2 * n + len(factored) :]
    coords = [lax.axis_index(name) for name in FINE]
    plans = [group_plan(groups, coords) for groups in all_groups]
    barrier = pltpu.get_barrier_semaphore()
    total = 0
    for plan in plans:
        for count, me, targets in plan:
            for place, _ in targets:
                pl.semaphore_signal(barrier, inc=1, device_id=place, device_id_type=pl.DeviceIdType.MESH)
            total += len(targets)
    pl.semaphore_wait(barrier, total)
    for a in range(n):
        o_refs[a][...] = x_refs[a][...]
    for g in range(max(len(plan) for plan in plans)):
        started = []
        for a in range(n):
            if g >= len(plans[a]):
                continue
            o_ref = o_refs[a]
            slots, send_sem, recv_sem = scratch[3 * a : 3 * a + 3]
            count, me, targets = plans[a][g]
            slots[g, me] = o_ref[...]
            copies = []
            for k, (place, _) in enumerate(targets):
                copy = pltpu.make_async_remote_copy(
                    src_ref=o_ref,
                    dst_ref=slots.at[g, me],
                    send_sem=send_sem.at[g, k],
                    recv_sem=recv_sem.at[g, me],
                    device_id=place,
                    device_id_type=pl.DeviceIdType.MESH,
                )
                copy.start()
                copies.append(copy)
            started.append((a, copies))
        for a, copies in started:
            o_ref = o_refs[a]
            slots, send_sem, recv_sem = scratch[3 * a : 3 * a + 3]
            count, me, targets = plans[a][g]
            for copy in copies:
                copy.wait_send()
            for place, sender in targets:
                pltpu.make_async_remote_copy(
                    src_ref=o_ref,
                    dst_ref=slots.at[g, sender],
                    send_sem=send_sem.at[g, 0],
                    recv_sem=recv_sem.at[g, sender],
                    device_id=place,
                    device_id_type=pl.DeviceIdType.MESH,
                ).wait_recv()
            acc = slots[g, 0]
            for j in range(1, count):
                acc = acc + slots[g, j]
            o_ref[...] = acc
    for a, f_ref in zip(factored, f_refs):
        eliminate(o_refs[a][...], f_ref)


def group_sums(values, all_groups, cid, factored=()):
    specs, flats, scratch = [], [], []
    for value, groups in zip(values, all_groups):
        spec = []
        widest = 1
        for names in groups:
            sizes = tuple(lax.axis_size(name) for name in names)
            count = 1
            for size in sizes:
                count *= size
            widest = max(widest, count)
            spec.append((tuple(FINE.index(name) for name in names), sizes))
        flat = value.reshape(-1, 128) if value.ndim == 1 else value
        specs.append(tuple(spec))
        flats.append(flat)
        scratch += [
            pltpu.VMEM((len(spec), widest) + flat.shape, flat.dtype),
            pltpu.SemaphoreType.DMA((len(spec), widest)),
            pltpu.SemaphoreType.DMA((len(spec), widest)),
        ]
    out_shape = [jax.ShapeDtypeStruct(flat.shape, flat.dtype) for flat in flats]
    out_shape += [jax.ShapeDtypeStruct((flats[a].shape[0], 2 * flats[a].shape[0]), jnp.float32) for a in factored]
    outs = pl.pallas_call(
        functools.partial(group_kernel, tuple(specs), tuple(factored)),
        out_shape=out_shape,
        in_specs=[pl.BlockSpec(memory_space=pltpu.VMEM)] * len(flats),
        out_specs=[pl.BlockSpec(memory_space=pltpu.VMEM)] * len(out_shape),
        scratch_shapes=scratch,
        compiler_params=pltpu.CompilerParams(collective_id=cid, has_side_effects=True),
    )(*flats)
    sums = [out.reshape(value.shape) for out, value in zip(outs, values)]
    factors = []
    for both in outs[len(flats) :]:
        half = both.shape[0]
        factors.append((both[:, :half], both[:, half:]))
    return sums, factors


def group_sum(value, groups, cid):
    return group_sums([value], [groups], cid)[0][0]


def group_factor(value, groups, cid):
    return group_sums([value], [groups], cid, factored=(0,))[1][0]


ALL_GROUPS = (FEAT, ("z",), ("yh", "x"))
CLAIM_GROUPS = (("z",), ("yh", "x"))


def halving_kernel(stages, alternate, gather, x_ref, o_ref, *scratch):
    if gather:
        work, recv, back, rs_send, rs_recv, ag_send, ag_recv = o_ref, *scratch
    else:
        work, recv, rs_send, rs_recv = scratch
    coords = [lax.axis_index(name) for name in FINE]
    second = coords[FINE.index("c")]
    partners, bits = [], []
    for (axis, step), (other, other_step) in zip(stages, alternate):
        bit = (coords[axis] // step) % 2
        other_bit = (coords[other] // other_step) % 2
        place = list(coords)
        place[axis] = place[axis] + (1 - second) * step * (1 - 2 * bit)
        place[other] = place[other] + second * other_step * (1 - 2 * other_bit)
        partners.append(tuple(place))
        bits.append(bit + second * (other_bit - bit))
    barrier = pltpu.get_barrier_semaphore()
    for partner in partners:
        pl.semaphore_signal(barrier, inc=1, device_id=partner, device_id_type=pl.DeviceIdType.MESH)
    pl.semaphore_wait(barrier, len(partners))
    work[...] = x_ref[...]
    total = work.shape[0]
    base = 0
    pieces = []
    for s, partner in enumerate(partners):
        size = total >> s
        half = size // 2
        keep = base + bits[s] * half
        give = base + (1 - bits[s]) * half
        slot = pl.ds(total - size, half)
        copy = pltpu.make_async_remote_copy(
            src_ref=work.at[pl.ds(give, half)],
            dst_ref=recv.at[slot],
            send_sem=rs_send.at[s],
            recv_sem=rs_recv.at[s],
            device_id=partner,
            device_id_type=pl.DeviceIdType.MESH,
        )
        copy.start()
        copy.wait()
        work[pl.ds(keep, half), :] = work[pl.ds(keep, half), :] + recv[slot, :]
        pieces.append((keep, give, slot))
        base = keep
    if gather:
        for s in reversed(range(len(partners))):
            keep, give, slot = pieces[s]
            copy = pltpu.make_async_remote_copy(
                src_ref=work.at[pl.ds(keep, slot.size)],
                dst_ref=back.at[slot],
                send_sem=ag_send.at[s],
                recv_sem=ag_recv.at[s],
                device_id=partners[s],
                device_id_type=pl.DeviceIdType.MESH,
            )
            copy.start()
            copy.wait()
            work[pl.ds(give, slot.size), :] = back[slot, :]
    else:
        o_ref[...] = work[pl.ds(base, o_ref.shape[0]), :]


CLAIM_STAGES = (("z", 1), ("x", 1), ("z", 2), ("x", 2), ("yh", 1), ("z", 4))
SWAPPED_STAGES = (("x", 1), ("z", 1), ("x", 2), ("z", 2), ("yh", 1), ("z", 4))


def claim_halving(value, gather, cid, alternate_order=None):
    stages = tuple((FINE.index(name), step) for name, step in CLAIM_STAGES)
    alternate = tuple((FINE.index(name), step) for name, step in (alternate_order or CLAIM_STAGES))
    count = len(stages)
    flat = value.reshape(-1, 128)
    rows = flat.shape[0]
    out_rows = rows if gather else rows >> count
    scratch = [] if gather else [pltpu.VMEM(flat.shape, flat.dtype)]
    scratch += [pltpu.VMEM(flat.shape, flat.dtype)] * (2 if gather else 1)
    scratch += [pltpu.SemaphoreType.DMA((count,))] * (4 if gather else 2)
    out = pl.pallas_call(
        functools.partial(halving_kernel, stages, alternate, gather),
        out_shape=jax.ShapeDtypeStruct((out_rows, 128), flat.dtype),
        in_specs=[pl.BlockSpec(memory_space=pltpu.VMEM)],
        out_specs=pl.BlockSpec(memory_space=pltpu.VMEM),
        scratch_shapes=scratch,
        compiler_params=pltpu.CompilerParams(collective_id=cid, has_side_effects=True),
    )(flat)
    return out


def claim_sum(value):
    part = lax.psum_scatter(value, "z", scatter_dimension=0, tiled=True)
    part = lax.psum(part, ("yh", "x"))
    return lax.all_gather(part, "z", axis=0, tiled=True)


def all_sum(value):
    value = lax.psum(value, FEAT)
    value = lax.psum(value, "z")
    return lax.psum(value, ("yh", "x"))


def claim_scatter(value):
    width = value.shape[-1]
    rows = value.shape[0] // lax.axis_size(CLAIM)
    bits = value.reshape(2, 2, 2, 2, 2, 2, rows, width)
    ordered = bits.transpose(5, 2, 4, 1, 0, 3, 6, 7).reshape(value.shape)
    return claim_halving(ordered, False, 5).reshape(rows, width)


def per_device(block_tiles, block_scale, row_index, col_index, start_basis):
    tiles_here = block_tiles.reshape(block_tiles.shape[-3:])
    scale_here = block_scale.reshape(-1)
    rows_here = row_index.reshape(-1)
    cols_here = col_index.reshape(-1)
    edge = tiles_here.shape[-1]
    col_count = start_basis.shape[0] // edge
    claim_count = lax.axis_size(CLAIM)
    own_cols = start_basis.shape[0] // claim_count
    own_first = lax.axis_index(CLAIM) * own_cols
    row_part, col_part = degree_local(tiles_here, scale_here, rows_here, cols_here, col_count)
    (col_total, row_total, _), (start_factor,) = group_sums(
        [col_part, row_part, gram_of(start_basis)], [CLAIM_GROUPS, (FEAT,), (FEAT,)], 0, factored=(2,)
    )
    col_scale = lax.rsqrt(col_total + 1.0)
    row_scale_all = lax.rsqrt(row_total + 1.0)
    own_rows = row_part.shape[0] // lax.axis_size(FEAT)
    own_start = lax.axis_index(FEAT) * own_rows
    row_scale = lax.dynamic_slice_in_dim(row_scale_all, own_start, own_rows, 0)
    first_basis = jnp.dot(start_basis, start_factor[1].T, precision=HIGH)
    first_operand = (col_scale[:, None] * first_basis).astype(jnp.bfloat16)
    first_partial = forward_local(tiles_here, scale_here, rows_here, cols_here, first_operand)

    def row_step(partial_t, previous_t, coupling, cid):
        sums_t = lax.psum_scatter(partial_t, FEAT, scatter_dimension=1, tiled=True)
        all_t = lax.all_gather(sums_t, FEAT, axis=1, tiled=True)
        block_t = row_scale[None, :] * sums_t
        wide_t = row_scale_all[None, :] * all_t
        if previous_t is not None:
            own_previous = lax.dynamic_slice_in_dim(previous_t, own_start, own_rows, 1)
            block_t = block_t - jnp.dot(coupling, own_previous, precision=HIGH)
            wide_t = wide_t - jnp.dot(coupling, previous_t, precision=HIGH)
        gram = jnp.dot(block_t, block_t.T, precision=HIGH)
        upper, inverse = group_factor(gram, ALL_GROUPS, cid)
        return jnp.dot(inverse, wide_t, precision=HIGH), upper

    def backward_partial(basis_t):
        operand_t = (row_scale_all[None, :] * basis_t).astype(jnp.bfloat16)
        return backward_local(tiles_here, scale_here, rows_here, cols_here, operand_t, col_count)

    u_first, b_first = row_step(first_partial, None, None, 1)
    summed = claim_halving(backward_partial(u_first), True, 4, SWAPPED_STAGES).reshape(-1, first_basis.shape[-1])
    update = col_scale[:, None] * summed - jnp.dot(first_basis, b_first.T, precision=HIGH)
    a_second, second_inverse = group_factor(gram_of(update), (FEAT,), 6)
    v_second = jnp.dot(update, second_inverse.T, precision=HIGH)
    scaled = (col_scale[:, None] * v_second).astype(jnp.bfloat16)
    second_partial = forward_local(tiles_here, scale_here, rows_here, cols_here, scaled)
    u_second, b_second = row_step(second_partial, u_first, a_second, 2)
    own_sums = claim_scatter(backward_partial(u_second))
    own_scale = lax.dynamic_slice_in_dim(col_scale, own_first, own_cols, 0)
    own_second = lax.dynamic_slice_in_dim(v_second, own_first, own_cols, 0)
    q_second = own_scale[:, None] * own_sums - jnp.dot(own_second, b_second.T, precision=HIGH)
    a_third, third_inverse = group_factor(gram_of(q_second), ALL_GROUPS, 3)
    v_output = jnp.dot(q_second, third_inverse.T, precision=HIGH)
    bidiagonal = jnp.stack([b_first, a_second, b_second, a_third])
    u_output = lax.dynamic_slice_in_dim(u_second, own_start, own_rows, 1).T
    return (u_output, v_output, bidiagonal)


def solution(mesh):
    claim_n, feat_n = mesh.devices.shape
    fine = Mesh(mesh.devices.reshape(2, claim_n // 16, 8, 2, feat_n // 2), FINE)
    placed = (
        P(CLAIM, FEAT, None, None, None),
        P(CLAIM, FEAT, None),
        P(CLAIM, FEAT, None),
        P(CLAIM, FEAT, None),
        P(FEAT, None),
    )
    return jax.shard_map(
        per_device,
        mesh=fine,
        in_specs=placed,
        out_specs=(P(CLAIM + FEAT, None), P(FEAT + CLAIM, None), P()),
        check_vma=False,
    )
```

```python
import functools

import jax
import jax.numpy as jnp
from jax import lax
from jax.experimental import pallas as pl
from jax.experimental.pallas import tpu as pltpu
from jax.sharding import Mesh
from jax.sharding import PartitionSpec as P

BLK_ROWS = 64

HIGH = lax.Precision.HIGHEST

FINE = ("yh", "x", "z", "yl", "c")
CLAIM = ("yh", "x", "z")
FEAT = ("yl", "c")


TILES_PER_STEP = 16


def forward_kernel(rows_ref, cols_ref, scale_ref, tiles_ref, operand_ref, out_ref):
    step = pl.program_id(0)
    edge = tiles_ref.shape[-1]

    @pl.when(step == 0)
    def _():
        out_ref[...] = jnp.zeros_like(out_ref)

    for t in range(tiles_ref.shape[0]):
        b = step * tiles_ref.shape[0] + t
        picked = operand_ref[:, pl.ds(pl.multiple_of(cols_ref[b] * edge, edge), edge)]
        product = lax.dot_general(
            picked, tiles_ref[t], (((1,), (1,)), ((), ())), preferred_element_type=jnp.float32
        )
        target = pl.ds(pl.multiple_of(rows_ref[b] * edge, edge), edge)
        out_ref[:, target] = out_ref[:, target] + product * scale_ref[b]


def backward_kernel(rows_ref, cols_ref, scale_ref, tiles_ref, operand_ref, out_ref):
    step = pl.program_id(0)
    edge = tiles_ref.shape[-1]

    @pl.when(step == 0)
    def _():
        out_ref[...] = jnp.zeros_like(out_ref)

    for t in range(tiles_ref.shape[0]):
        b = step * tiles_ref.shape[0] + t
        picked = operand_ref[:, pl.ds(pl.multiple_of(rows_ref[b] * edge, edge), edge)]
        product = jnp.dot(picked, tiles_ref[t], preferred_element_type=jnp.float32) * scale_ref[b]
        target = pl.ds(pl.multiple_of(cols_ref[b] * edge, edge), edge)
        out_ref[:, target] = out_ref[:, target] + product


def block_product(kernel, block_tiles, block_scale, row_index, col_index, operand, out_shape):
    count, edge, _ = block_tiles.shape
    per = TILES_PER_STEP
    grid_spec = pltpu.PrefetchScalarGridSpec(
        num_scalar_prefetch=2,
        grid=(count // per,),
        in_specs=[
            pl.BlockSpec(memory_space=pltpu.SMEM),
            pl.BlockSpec((per, edge, edge), lambda i, rows, cols: (i, 0, 0)),
            pl.BlockSpec(operand.shape, lambda i, rows, cols: (0, 0)),
        ],
        out_specs=pl.BlockSpec(out_shape, lambda i, rows, cols: (0, 0)),
    )
    width = min(operand.shape)
    return pl.pallas_call(
        kernel,
        grid_spec=grid_spec,
        out_shape=jax.ShapeDtypeStruct(out_shape, jnp.float32),
        cost_estimate=pl.CostEstimate(
            flops=2 * count * edge * edge * width,
            bytes_accessed=block_tiles.size * 2 + operand.size * 2 + out_shape[0] * out_shape[1] * 4,
            transcendentals=0,
        ),
    )(row_index, col_index, block_scale, block_tiles, operand)


def forward_local(block_tiles, block_scale, row_index, col_index, operand):
    edge = block_tiles.shape[-1]
    out_shape = (operand.shape[-1], BLK_ROWS * edge)
    return block_product(
        forward_kernel, block_tiles, block_scale, row_index, col_index, operand.T, out_shape
    )


def backward_local(block_tiles, block_scale, row_index, col_index, operand_t, col_count):
    edge = block_tiles.shape[-1]
    out_shape = (operand_t.shape[0], col_count * edge)
    flipped = block_product(
        backward_kernel, block_tiles, block_scale, row_index, col_index, operand_t, out_shape
    )
    return flipped.T


def degree_local(block_tiles, block_scale, row_index, col_index, col_count):
    row_sums = jnp.sum(block_tiles, axis=2, dtype=jnp.float32) * block_scale[:, None]
    col_sums = jnp.sum(block_tiles, axis=1, dtype=jnp.float32) * block_scale[:, None]
    row_select = (row_index[None, :] == jnp.arange(BLK_ROWS, dtype=jnp.int32)[:, None]).astype(
        jnp.float32
    )
    col_select = (col_index[None, :] == jnp.arange(col_count, dtype=jnp.int32)[:, None]).astype(
        jnp.float32
    )
    row_part = jnp.einsum("rb,bi->ri", row_select, row_sums, precision=HIGH).reshape(-1)
    col_part = jnp.einsum("cb,bi->ci", col_select, col_sums, precision=HIGH).reshape(-1)
    return (row_part, col_part)


def gram_of(block):
    return jnp.dot(block.T, block, precision=HIGH)


def factor_kernel(g_ref, o_ref):
    eliminate(g_ref[...], o_ref)


def eliminate(gram, o_ref):
    n = gram.shape[0]
    o_ref[:, :n] = gram
    rows = lax.broadcasted_iota(jnp.int32, (n, 2 * n), 0)
    cols = lax.broadcasted_iota(jnp.int32, (n, 2 * n), 1)
    o_ref[:, n:] = jnp.where(rows[:, n:] == cols[:, n:] - n, 1.0, 0.0).astype(o_ref.dtype)
    m = o_ref[...]
    below = lax.broadcasted_iota(jnp.int32, (n, 1), 0)
    for j in range(n):
        factor = jnp.where(below > j, m[:, j : j + 1], 0.0) * (1.0 / m[j : j + 1, j : j + 1])
        m = m - factor * m[j : j + 1, :]
    diagonal = jnp.sum(jnp.where(rows == cols, m, 0.0), axis=1, keepdims=True)
    m = m * lax.rsqrt(diagonal)
    o_ref[...] = jnp.where((cols < n) & (cols < rows), 0.0, m)


def factor_of(gram_total):
    n = gram_total.shape[0]
    both = pl.pallas_call(
        factor_kernel,
        out_shape=jax.ShapeDtypeStruct((n, 2 * n), jnp.float32),
        in_specs=[pl.BlockSpec(memory_space=pltpu.VMEM)],
        out_specs=pl.BlockSpec(memory_space=pltpu.VMEM),
    )(gram_total)
    return both[:, :n], both[:, n:]


def orthonormal(block, gram_total):
    upper, inverse = factor_of(gram_total)
    basis = jnp.dot(block, inverse.T, precision=HIGH)
    return (basis, upper)


def group_plan(groups, coords):
    plans = []
    for axes, sizes in groups:
        count = 1
        for size in sizes:
            count *= size
        me = 0
        for axis, size in zip(axes, sizes):
            me = me * size + coords[axis]
        targets = []
        for k in range(1, count):
            member = (me + k) % count
            place = list(coords)
            rest = member
            for axis, size in reversed(list(zip(axes, sizes))):
                place[axis] = rest % size
                rest = rest // size
            targets.append((tuple(place), (me + count - k) % count))
        plans.append((count, me, targets))
    return plans


def group_kernel(all_groups, factored, *refs):
    n = len(all_groups)
    x_refs, o_refs = refs[:n], refs[n : 2 * n]
    f_refs, scratch = refs[2 * n : 2 * n + len(factored)], refs[2 * n + len(factored) :]
    coords = [lax.axis_index(name) for name in FINE]
    plans = [group_plan(groups, coords) for groups in all_groups]
    barrier = pltpu.get_barrier_semaphore()
    total = 0
    for plan in plans:
        for count, me, targets in plan:
            for place, _ in targets:
                pl.semaphore_signal(barrier, inc=1, device_id=place, device_id_type=pl.DeviceIdType.MESH)
            total += len(targets)
    pl.semaphore_wait(barrier, total)
    for a in range(n):
        o_refs[a][...] = x_refs[a][...]
    for g in range(max(len(plan) for plan in plans)):
        started = []
        for a in range(n):
            if g >= len(plans[a]):
                continue
            o_ref = o_refs[a]
            slots, send_sem, recv_sem = scratch[3 * a : 3 * a + 3]
            count, me, targets = plans[a][g]
            slots[g, me] = o_ref[...]
            copies = []
            for k, (place, _) in enumerate(targets):
                copy = pltpu.make_async_remote_copy(
                    src_ref=o_ref,
                    dst_ref=slots.at[g, me],
                    send_sem=send_sem.at[g, k],
                    recv_sem=recv_sem.at[g, me],
                    device_id=place,
                    device_id_type=pl.DeviceIdType.MESH,
                )
                copy.start()
                copies.append(copy)
            started.append((a, copies))
        for a, copies in started:
            o_ref = o_refs[a]
            slots, send_sem, recv_sem = scratch[3 * a : 3 * a + 3]
            count, me, targets = plans[a][g]
            for copy in copies:
                copy.wait_send()
            for place, sender in targets:
                pltpu.make_async_remote_copy(
                    src_ref=o_ref,
                    dst_ref=slots.at[g, sender],
                    send_sem=send_sem.at[g, 0],
                    recv_sem=recv_sem.at[g, sender],
                    device_id=place,
                    device_id_type=pl.DeviceIdType.MESH,
                ).wait_recv()
            acc = slots[g, 0]
            for j in range(1, count):
                acc = acc + slots[g, j]
            o_ref[...] = acc
    for a, f_ref in zip(factored, f_refs):
        eliminate(o_refs[a][...], f_ref)


def group_sums(values, all_groups, cid, factored=()):
    specs, flats, scratch = [], [], []
    for value, groups in zip(values, all_groups):
        spec = []
        widest = 1
        for names in groups:
            sizes = tuple(lax.axis_size(name) for name in names)
            count = 1
            for size in sizes:
                count *= size
            widest = max(widest, count)
            spec.append((tuple(FINE.index(name) for name in names), sizes))
        flat = value.reshape(-1, 128) if value.ndim == 1 else value
        specs.append(tuple(spec))
        flats.append(flat)
        scratch += [
            pltpu.VMEM((len(spec), widest) + flat.shape, flat.dtype),
            pltpu.SemaphoreType.DMA((len(spec), widest)),
            pltpu.SemaphoreType.DMA((len(spec), widest)),
        ]
    out_shape = [jax.ShapeDtypeStruct(flat.shape, flat.dtype) for flat in flats]
    out_shape += [jax.ShapeDtypeStruct((flats[a].shape[0], 2 * flats[a].shape[0]), jnp.float32) for a in factored]
    outs = pl.pallas_call(
        functools.partial(group_kernel, tuple(specs), tuple(factored)),
        out_shape=out_shape,
        in_specs=[pl.BlockSpec(memory_space=pltpu.VMEM)] * len(flats),
        out_specs=[pl.BlockSpec(memory_space=pltpu.VMEM)] * len(out_shape),
        scratch_shapes=scratch,
        compiler_params=pltpu.CompilerParams(collective_id=cid, has_side_effects=True),
    )(*flats)
    sums = [out.reshape(value.shape) for out, value in zip(outs, values)]
    factors = []
    for both in outs[len(flats) :]:
        half = both.shape[0]
        factors.append((both[:, :half], both[:, half:]))
    return sums, factors


def group_sum(value, groups, cid):
    return group_sums([value], [groups], cid)[0][0]


def group_factor(value, groups, cid):
    return group_sums([value], [groups], cid, factored=(0,))[1][0]


ALL_GROUPS = (FEAT, ("z",), ("yh", "x"))
CLAIM_GROUPS = (("z",), ("yh", "x"))


def halving_kernel(stages, alternate, gather, interleaved, x_ref, o_ref, *scratch):
    if gather:
        work, recv, back, rs_send, rs_recv, ag_send, ag_recv = o_ref, *scratch
    else:
        work, recv, rs_send, rs_recv = scratch
    coords = [lax.axis_index(name) for name in FINE]
    second = coords[FINE.index("c")]
    partners, bits = [], []
    for (axis, step), (other, other_step) in zip(stages, alternate):
        bit = (coords[axis] // step) % 2
        other_bit = (coords[other] // other_step) % 2
        place = list(coords)
        place[axis] = place[axis] + (1 - second) * step * (1 - 2 * bit)
        place[other] = place[other] + second * other_step * (1 - 2 * other_bit)
        partners.append(tuple(place))
        bits.append(bit + second * (other_bit - bit))
    barrier = pltpu.get_barrier_semaphore()
    for partner in partners:
        pl.semaphore_signal(barrier, inc=1, device_id=partner, device_id_type=pl.DeviceIdType.MESH)
    pl.semaphore_wait(barrier, len(partners))
    work[...] = x_ref[...]
    total = work.shape[0]
    base = 0
    pieces = []
    quarter = total // 4
    for s, partner in enumerate(partners):
        size = total >> s
        half = size // 2
        keep = base + bits[s] * half
        give = base + (1 - bits[s]) * half
        slot = pl.ds(total - size, half)
        if interleaved and s == 0:
            gap = (1 - second) * quarter + second * 2 * quarter
            give = (1 - second) * (1 - bits[0]) * 2 * quarter + second * (1 - bits[0]) * quarter
            keep = (1 - second) * bits[0] * 2 * quarter + second * bits[0] * quarter
            copies = []
            for part in range(2):
                copy = pltpu.make_async_remote_copy(
                    src_ref=work.at[pl.ds(give + part * gap, quarter)],
                    dst_ref=recv.at[pl.ds(part * quarter, quarter)],
                    send_sem=rs_send.at[len(partners) * part],
                    recv_sem=rs_recv.at[len(partners) * part],
                    device_id=partner,
                    device_id_type=pl.DeviceIdType.MESH,
                )
                copy.start()
                copies.append(copy)
            for copy in copies:
                copy.wait()
            for part in range(2):
                rows = pl.ds(keep + part * gap, quarter)
                work[rows, :] = work[rows, :] + recv[pl.ds(part * quarter, quarter), :]
            continue
        if interleaved and s == 1:
            first, now = bits[0], bits[1]
            keep = (1 - second) * (first * 2 * quarter + now * quarter) + second * (now * 2 * quarter + first * quarter)
            give = (1 - second) * (first * 2 * quarter + (1 - now) * quarter) + second * (
                (1 - now) * 2 * quarter + first * quarter
            )
        copy = pltpu.make_async_remote_copy(
            src_ref=work.at[pl.ds(give, half)],
            dst_ref=recv.at[slot],
            send_sem=rs_send.at[s],
            recv_sem=rs_recv.at[s],
            device_id=partner,
            device_id_type=pl.DeviceIdType.MESH,
        )
        copy.start()
        copy.wait()
        work[pl.ds(keep, half), :] = work[pl.ds(keep, half), :] + recv[slot, :]
        pieces.append((keep, give, slot))
        base = keep
    if gather:
        for s in reversed(range(len(partners))):
            keep, give, slot = pieces[s]
            copy = pltpu.make_async_remote_copy(
                src_ref=work.at[pl.ds(keep, slot.size)],
                dst_ref=back.at[slot],
                send_sem=ag_send.at[s],
                recv_sem=ag_recv.at[s],
                device_id=partners[s],
                device_id_type=pl.DeviceIdType.MESH,
            )
            copy.start()
            copy.wait()
            work[pl.ds(give, slot.size), :] = back[slot, :]
    else:
        o_ref[...] = work[pl.ds(base, o_ref.shape[0]), :]


CLAIM_STAGES = (("z", 1), ("x", 1), ("z", 2), ("x", 2), ("yh", 1), ("z", 4))
SWAPPED_STAGES = (("x", 1), ("z", 1), ("x", 2), ("z", 2), ("yh", 1), ("z", 4))
SWAPPED_FIRST = (("x", 1), ("z", 1), ("z", 2), ("x", 2), ("yh", 1), ("z", 4))


def claim_halving(value, gather, cid, alternate_order=None):
    stages = tuple((FINE.index(name), step) for name, step in CLAIM_STAGES)
    alternate = tuple((FINE.index(name), step) for name, step in (alternate_order or CLAIM_STAGES))
    interleaved = (not gather) and alternate != stages
    count = len(stages)
    flat = value.reshape(-1, 128)
    rows = flat.shape[0]
    out_rows = rows if gather else rows >> count
    scratch = [] if gather else [pltpu.VMEM(flat.shape, flat.dtype)]
    scratch += [pltpu.VMEM(flat.shape, flat.dtype)] * (2 if gather else 1)
    scratch += [pltpu.SemaphoreType.DMA((count + 1,))] * (4 if gather else 2)
    out = pl.pallas_call(
        functools.partial(halving_kernel, stages, alternate, gather, interleaved),
        out_shape=jax.ShapeDtypeStruct((out_rows, 128), flat.dtype),
        in_specs=[pl.BlockSpec(memory_space=pltpu.VMEM)],
        out_specs=pl.BlockSpec(memory_space=pltpu.VMEM),
        scratch_shapes=scratch,
        compiler_params=pltpu.CompilerParams(collective_id=cid, has_side_effects=True),
    )(flat)
    return out


def claim_sum(value):
    part = lax.psum_scatter(value, "z", scatter_dimension=0, tiled=True)
    part = lax.psum(part, ("yh", "x"))
    return lax.all_gather(part, "z", axis=0, tiled=True)


def all_sum(value):
    value = lax.psum(value, FEAT)
    value = lax.psum(value, "z")
    return lax.psum(value, ("yh", "x"))


def claim_scatter(value):
    width = value.shape[-1]
    rows = value.shape[0] // lax.axis_size(CLAIM)
    bits = value.reshape(2, 2, 2, 2, 2, 2, rows, width)
    ordered = bits.transpose(5, 2, 4, 1, 0, 3, 6, 7).reshape(value.shape)
    return claim_halving(ordered, False, 5, SWAPPED_FIRST).reshape(rows, width)


def per_device(block_tiles, block_scale, row_index, col_index, start_basis):
    tiles_here = block_tiles.reshape(block_tiles.shape[-3:])
    scale_here = block_scale.reshape(-1)
    rows_here = row_index.reshape(-1)
    cols_here = col_index.reshape(-1)
    edge = tiles_here.shape[-1]
    col_count = start_basis.shape[0] // edge
    claim_count = lax.axis_size(CLAIM)
    own_cols = start_basis.shape[0] // claim_count
    own_first = lax.axis_index(CLAIM) * own_cols
    row_part, col_part = degree_local(tiles_here, scale_here, rows_here, cols_here, col_count)
    (col_total, row_total, _), (start_factor,) = group_sums(
        [col_part, row_part, gram_of(start_basis)], [CLAIM_GROUPS, (FEAT,), (FEAT,)], 0, factored=(2,)
    )
    col_scale = lax.rsqrt(col_total + 1.0)
    row_scale_all = lax.rsqrt(row_total + 1.0)
    own_rows = row_part.shape[0] // lax.axis_size(FEAT)
    own_start = lax.axis_index(FEAT) * own_rows
    row_scale = lax.dynamic_slice_in_dim(row_scale_all, own_start, own_rows, 0)
    first_basis = jnp.dot(start_basis, start_factor[1].T, precision=HIGH)
    first_operand = (col_scale[:, None] * first_basis).astype(jnp.bfloat16)
    first_partial = forward_local(tiles_here, scale_here, rows_here, cols_here, first_operand)

    def row_step(partial_t, previous_t, coupling, cid):
        sums_t = lax.psum_scatter(partial_t, FEAT, scatter_dimension=1, tiled=True)
        all_t = lax.all_gather(sums_t, FEAT, axis=1, tiled=True)
        block_t = row_scale[None, :] * sums_t
        wide_t = row_scale_all[None, :] * all_t
        if previous_t is not None:
            own_previous = lax.dynamic_slice_in_dim(previous_t, own_start, own_rows, 1)
            block_t = block_t - jnp.dot(coupling, own_previous, precision=HIGH)
            wide_t = wide_t - jnp.dot(coupling, previous_t, precision=HIGH)
        gram = jnp.dot(block_t, block_t.T, precision=HIGH)
        upper, inverse = group_factor(gram, ALL_GROUPS, cid)
        return jnp.dot(inverse, wide_t, precision=HIGH), upper

    def backward_partial(basis_t):
        operand_t = (row_scale_all[None, :] * basis_t).astype(jnp.bfloat16)
        return backward_local(tiles_here, scale_here, rows_here, cols_here, operand_t, col_count)

    u_first, b_first = row_step(first_partial, None, None, 1)
    summed = claim_halving(backward_partial(u_first), True, 4, SWAPPED_STAGES).reshape(-1, first_basis.shape[-1])
    update = col_scale[:, None] * summed - jnp.dot(first_basis, b_first.T, precision=HIGH)
    a_second, second_inverse = group_factor(gram_of(update), (FEAT,), 6)
    v_second = jnp.dot(update, second_inverse.T, precision=HIGH)
    scaled = (col_scale[:, None] * v_second).astype(jnp.bfloat16)
    second_partial = forward_local(tiles_here, scale_here, rows_here, cols_here, scaled)
    u_second, b_second = row_step(second_partial, u_first, a_second, 2)
    own_sums = claim_scatter(backward_partial(u_second))
    own_scale = lax.dynamic_slice_in_dim(col_scale, own_first, own_cols, 0)
    own_second = lax.dynamic_slice_in_dim(v_second, own_first, own_cols, 0)
    q_second = own_scale[:, None] * own_sums - jnp.dot(own_second, b_second.T, precision=HIGH)
    a_third, third_inverse = group_factor(gram_of(q_second), ALL_GROUPS, 3)
    v_output = jnp.dot(q_second, third_inverse.T, precision=HIGH)
    bidiagonal = jnp.stack([b_first, a_second, b_second, a_third])
    u_output = lax.dynamic_slice_in_dim(u_second, own_start, own_rows, 1).T
    return (u_output, v_output, bidiagonal)


def solution(mesh):
    claim_n, feat_n = mesh.devices.shape
    fine = Mesh(mesh.devices.reshape(2, claim_n // 16, 8, 2, feat_n // 2), FINE)
    placed = (
        P(CLAIM, FEAT, None, None, None),
        P(CLAIM, FEAT, None),
        P(CLAIM, FEAT, None),
        P(CLAIM, FEAT, None),
        P(FEAT, None),
    )
    return jax.shard_map(
        per_device,
        mesh=fine,
        in_specs=placed,
        out_specs=(P(CLAIM + FEAT, None), P(FEAT + CLAIM, None), P()),
        check_vma=False,
    )
```

```python
import functools

import jax
import jax.numpy as jnp
from jax import lax
from jax.experimental import pallas as pl
from jax.experimental.pallas import tpu as pltpu
from jax.sharding import Mesh
from jax.sharding import PartitionSpec as P

BLK_ROWS = 64

HIGH = lax.Precision.HIGHEST

FINE = ("yh", "x", "z", "yl", "c")
CLAIM = ("yh", "x", "z")
FEAT = ("yl", "c")


TILES_PER_STEP = 32


def forward_kernel(rows_ref, cols_ref, scale_ref, tiles_ref, operand_ref, out_ref):
    step = pl.program_id(0)
    edge = tiles_ref.shape[-1]

    @pl.when(step == 0)
    def _():
        out_ref[...] = jnp.zeros_like(out_ref)

    def tile(t, carry):
        b = step * tiles_ref.shape[0] + t
        picked = operand_ref[:, pl.ds(pl.multiple_of(cols_ref[b] * edge, edge), edge)]
        product = lax.dot_general(
            picked, tiles_ref[t], (((1,), (1,)), ((), ())), preferred_element_type=jnp.float32
        )
        target = pl.ds(pl.multiple_of(rows_ref[b] * edge, edge), edge)
        out_ref[:, target] = out_ref[:, target] + product * scale_ref[b]
        return carry

    lax.fori_loop(0, tiles_ref.shape[0], tile, 0, unroll=8)


def backward_kernel(rows_ref, cols_ref, scale_ref, tiles_ref, operand_ref, out_ref):
    step = pl.program_id(0)
    edge = tiles_ref.shape[-1]

    @pl.when(step == 0)
    def _():
        out_ref[...] = jnp.zeros_like(out_ref)

    def tile(t, carry):
        b = step * tiles_ref.shape[0] + t
        picked = operand_ref[:, pl.ds(pl.multiple_of(rows_ref[b] * edge, edge), edge)]
        product = jnp.dot(picked, tiles_ref[t], preferred_element_type=jnp.float32) * scale_ref[b]
        target = pl.ds(pl.multiple_of(cols_ref[b] * edge, edge), edge)
        out_ref[:, target] = out_ref[:, target] + product
        return carry

    lax.fori_loop(0, tiles_ref.shape[0], tile, 0, unroll=8)


def block_product(kernel, block_tiles, block_scale, row_index, col_index, operand, out_shape):
    count, edge, _ = block_tiles.shape
    per = TILES_PER_STEP
    grid_spec = pltpu.PrefetchScalarGridSpec(
        num_scalar_prefetch=2,
        grid=(count // per,),
        in_specs=[
            pl.BlockSpec(memory_space=pltpu.SMEM),
            pl.BlockSpec((per, edge, edge), lambda i, rows, cols: (i, 0, 0)),
            pl.BlockSpec(operand.shape, lambda i, rows, cols: (0, 0)),
        ],
        out_specs=pl.BlockSpec(out_shape, lambda i, rows, cols: (0, 0)),
    )
    width = min(operand.shape)
    return pl.pallas_call(
        kernel,
        grid_spec=grid_spec,
        out_shape=jax.ShapeDtypeStruct(out_shape, jnp.float32),
        cost_estimate=pl.CostEstimate(
            flops=2 * count * edge * edge * width,
            bytes_accessed=block_tiles.size * 2 + operand.size * 2 + out_shape[0] * out_shape[1] * 4,
            transcendentals=0,
        ),
    )(row_index, col_index, block_scale, block_tiles, operand)


def forward_local(block_tiles, block_scale, row_index, col_index, operand):
    edge = block_tiles.shape[-1]
    out_shape = (operand.shape[-1], BLK_ROWS * edge)
    return block_product(
        forward_kernel, block_tiles, block_scale, row_index, col_index, operand.T, out_shape
    )


def backward_local(block_tiles, block_scale, row_index, col_index, operand_t, col_count):
    edge = block_tiles.shape[-1]
    out_shape = (operand_t.shape[0], col_count * edge)
    flipped = block_product(
        backward_kernel, block_tiles, block_scale, row_index, col_index, operand_t, out_shape
    )
    return flipped.T


def degree_local(block_tiles, block_scale, row_index, col_index, col_count):
    row_sums = jnp.sum(block_tiles, axis=2, dtype=jnp.float32) * block_scale[:, None]
    col_sums = jnp.sum(block_tiles, axis=1, dtype=jnp.float32) * block_scale[:, None]
    row_select = (row_index[None, :] == jnp.arange(BLK_ROWS, dtype=jnp.int32)[:, None]).astype(
        jnp.float32
    )
    col_select = (col_index[None, :] == jnp.arange(col_count, dtype=jnp.int32)[:, None]).astype(
        jnp.float32
    )
    row_part = jnp.einsum("rb,bi->ri", row_select, row_sums, precision=HIGH).reshape(-1)
    col_part = jnp.einsum("cb,bi->ci", col_select, col_sums, precision=HIGH).reshape(-1)
    return (row_part, col_part)


def gram_of(block):
    return jnp.dot(block.T, block, precision=HIGH)


def factor_kernel(g_ref, o_ref):
    eliminate(g_ref[...], o_ref)


def eliminate(gram, o_ref):
    n = gram.shape[0]
    o_ref[:, :n] = gram
    rows = lax.broadcasted_iota(jnp.int32, (n, 2 * n), 0)
    cols = lax.broadcasted_iota(jnp.int32, (n, 2 * n), 1)
    o_ref[:, n:] = jnp.where(rows[:, n:] == cols[:, n:] - n, 1.0, 0.0).astype(o_ref.dtype)
    m = o_ref[...]
    below = lax.broadcasted_iota(jnp.int32, (n, 1), 0)
    for j in range(n):
        factor = jnp.where(below > j, m[:, j : j + 1], 0.0) * (1.0 / m[j : j + 1, j : j + 1])
        m = m - factor * m[j : j + 1, :]
    diagonal = jnp.sum(jnp.where(rows == cols, m, 0.0), axis=1, keepdims=True)
    m = m * lax.rsqrt(diagonal)
    o_ref[...] = jnp.where((cols < n) & (cols < rows), 0.0, m)


def factor_of(gram_total):
    n = gram_total.shape[0]
    both = pl.pallas_call(
        factor_kernel,
        out_shape=jax.ShapeDtypeStruct((n, 2 * n), jnp.float32),
        in_specs=[pl.BlockSpec(memory_space=pltpu.VMEM)],
        out_specs=pl.BlockSpec(memory_space=pltpu.VMEM),
    )(gram_total)
    return both[:, :n], both[:, n:]


def orthonormal(block, gram_total):
    upper, inverse = factor_of(gram_total)
    basis = jnp.dot(block, inverse.T, precision=HIGH)
    return (basis, upper)


def group_plan(groups, coords):
    plans = []
    for axes, sizes in groups:
        count = 1
        for size in sizes:
            count *= size
        me = 0
        for axis, size in zip(axes, sizes):
            me = me * size + coords[axis]
        targets = []
        for k in range(1, count):
            member = (me + k) % count
            place = list(coords)
            rest = member
            for axis, size in reversed(list(zip(axes, sizes))):
                place[axis] = rest % size
                rest = rest // size
            targets.append((tuple(place), (me + count - k) % count))
        plans.append((count, me, targets))
    return plans


def group_kernel(all_groups, factored, *refs):
    n = len(all_groups)
    x_refs, o_refs = refs[:n], refs[n : 2 * n]
    f_refs, scratch = refs[2 * n : 2 * n + len(factored)], refs[2 * n + len(factored) :]
    coords = [lax.axis_index(name) for name in FINE]
    plans = [group_plan(groups, coords) for groups in all_groups]
    barrier = pltpu.get_barrier_semaphore()
    total = 0
    for plan in plans:
        for count, me, targets in plan:
            for place, _ in targets:
                pl.semaphore_signal(barrier, inc=1, device_id=place, device_id_type=pl.DeviceIdType.MESH)
            total += len(targets)
    pl.semaphore_wait(barrier, total)
    for a in range(n):
        o_refs[a][...] = x_refs[a][...]
    for g in range(max(len(plan) for plan in plans)):
        started = []
        for a in range(n):
            if g >= len(plans[a]):
                continue
            o_ref = o_refs[a]
            slots, send_sem, recv_sem = scratch[3 * a : 3 * a + 3]
            count, me, targets = plans[a][g]
            slots[g, me] = o_ref[...]
            copies = []
            for k, (place, _) in enumerate(targets):
                copy = pltpu.make_async_remote_copy(
                    src_ref=o_ref,
                    dst_ref=slots.at[g, me],
                    send_sem=send_sem.at[g, k],
                    recv_sem=recv_sem.at[g, me],
                    device_id=place,
                    device_id_type=pl.DeviceIdType.MESH,
                )
                copy.start()
                copies.append(copy)
            started.append((a, copies))
        for a, copies in started:
            o_ref = o_refs[a]
            slots, send_sem, recv_sem = scratch[3 * a : 3 * a + 3]
            count, me, targets = plans[a][g]
            for copy in copies:
                copy.wait_send()
            for place, sender in targets:
                pltpu.make_async_remote_copy(
                    src_ref=o_ref,
                    dst_ref=slots.at[g, sender],
                    send_sem=send_sem.at[g, 0],
                    recv_sem=recv_sem.at[g, sender],
                    device_id=place,
                    device_id_type=pl.DeviceIdType.MESH,
                ).wait_recv()
            acc = slots[g, 0]
            for j in range(1, count):
                acc = acc + slots[g, j]
            o_ref[...] = acc
    for a, f_ref in zip(factored, f_refs):
        eliminate(o_refs[a][...], f_ref)


def group_sums(values, all_groups, cid, factored=()):
    specs, flats, scratch = [], [], []
    for value, groups in zip(values, all_groups):
        spec = []
        widest = 1
        for names in groups:
            sizes = tuple(lax.axis_size(name) for name in names)
            count = 1
            for size in sizes:
                count *= size
            widest = max(widest, count)
            spec.append((tuple(FINE.index(name) for name in names), sizes))
        flat = value.reshape(-1, 128) if value.ndim == 1 else value
        specs.append(tuple(spec))
        flats.append(flat)
        scratch += [
            pltpu.VMEM((len(spec), widest) + flat.shape, flat.dtype),
            pltpu.SemaphoreType.DMA((len(spec), widest)),
            pltpu.SemaphoreType.DMA((len(spec), widest)),
        ]
    out_shape = [jax.ShapeDtypeStruct(flat.shape, flat.dtype) for flat in flats]
    out_shape += [jax.ShapeDtypeStruct((flats[a].shape[0], 2 * flats[a].shape[0]), jnp.float32) for a in factored]
    outs = pl.pallas_call(
        functools.partial(group_kernel, tuple(specs), tuple(factored)),
        out_shape=out_shape,
        in_specs=[pl.BlockSpec(memory_space=pltpu.VMEM)] * len(flats),
        out_specs=[pl.BlockSpec(memory_space=pltpu.VMEM)] * len(out_shape),
        scratch_shapes=scratch,
        compiler_params=pltpu.CompilerParams(collective_id=cid, has_side_effects=True),
    )(*flats)
    sums = [out.reshape(value.shape) for out, value in zip(outs, values)]
    factors = []
    for both in outs[len(flats) :]:
        half = both.shape[0]
        factors.append((both[:, :half], both[:, half:]))
    return sums, factors


def group_sum(value, groups, cid):
    return group_sums([value], [groups], cid)[0][0]


def group_factor(value, groups, cid):
    return group_sums([value], [groups], cid, factored=(0,))[1][0]


ALL_GROUPS = (FEAT, ("z",), ("yh", "x"))
CLAIM_GROUPS = (("z",), ("yh", "x"))


def halving_kernel(stages, alternate, gather, interleaved, x_ref, o_ref, *scratch):
    if gather:
        work, recv, back, rs_send, rs_recv, ag_send, ag_recv = o_ref, *scratch
    else:
        work, recv, rs_send, rs_recv = scratch
    coords = [lax.axis_index(name) for name in FINE]
    second = coords[FINE.index("c")]
    partners, bits = [], []
    for (axis, step), (other, other_step) in zip(stages, alternate):
        bit = (coords[axis] // step) % 2
        other_bit = (coords[other] // other_step) % 2
        place = list(coords)
        place[axis] = place[axis] + (1 - second) * step * (1 - 2 * bit)
        place[other] = place[other] + second * other_step * (1 - 2 * other_bit)
        partners.append(tuple(place))
        bits.append(bit + second * (other_bit - bit))
    barrier = pltpu.get_barrier_semaphore()
    for partner in partners:
        pl.semaphore_signal(barrier, inc=1, device_id=partner, device_id_type=pl.DeviceIdType.MESH)
    pl.semaphore_wait(barrier, len(partners))
    work[...] = x_ref[...]
    total = work.shape[0]
    base = 0
    pieces = []
    quarter = total // 4
    for s, partner in enumerate(partners):
        size = total >> s
        half = size // 2
        keep = base + bits[s] * half
        give = base + (1 - bits[s]) * half
        slot = pl.ds(total - size, half)
        if interleaved and s == 0:
            gap = (1 - second) * quarter + second * 2 * quarter
            give = (1 - second) * (1 - bits[0]) * 2 * quarter + second * (1 - bits[0]) * quarter
            keep = (1 - second) * bits[0] * 2 * quarter + second * bits[0] * quarter
            copies = []
            for part in range(2):
                copy = pltpu.make_async_remote_copy(
                    src_ref=work.at[pl.ds(give + part * gap, quarter)],
                    dst_ref=recv.at[pl.ds(part * quarter, quarter)],
                    send_sem=rs_send.at[len(partners) * part],
                    recv_sem=rs_recv.at[len(partners) * part],
                    device_id=partner,
                    device_id_type=pl.DeviceIdType.MESH,
                )
                copy.start()
                copies.append(copy)
            for copy in copies:
                copy.wait()
            for part in range(2):
                rows = pl.ds(keep + part * gap, quarter)
                work[rows, :] = work[rows, :] + recv[pl.ds(part * quarter, quarter), :]
            continue
        if interleaved and s == 1:
            first, now = bits[0], bits[1]
            keep = (1 - second) * (first * 2 * quarter + now * quarter) + second * (now * 2 * quarter + first * quarter)
            give = (1 - second) * (first * 2 * quarter + (1 - now) * quarter) + second * (
                (1 - now) * 2 * quarter + first * quarter
            )
        copy = pltpu.make_async_remote_copy(
            src_ref=work.at[pl.ds(give, half)],
            dst_ref=recv.at[slot],
            send_sem=rs_send.at[s],
            recv_sem=rs_recv.at[s],
            device_id=partner,
            device_id_type=pl.DeviceIdType.MESH,
        )
        copy.start()
        copy.wait()
        work[pl.ds(keep, half), :] = work[pl.ds(keep, half), :] + recv[slot, :]
        pieces.append((keep, give, slot))
        base = keep
    if gather:
        for s in reversed(range(len(partners))):
            keep, give, slot = pieces[s]
            copy = pltpu.make_async_remote_copy(
                src_ref=work.at[pl.ds(keep, slot.size)],
                dst_ref=back.at[slot],
                send_sem=ag_send.at[s],
                recv_sem=ag_recv.at[s],
                device_id=partners[s],
                device_id_type=pl.DeviceIdType.MESH,
            )
            copy.start()
            copy.wait()
            work[pl.ds(give, slot.size), :] = back[slot, :]
    else:
        o_ref[...] = work[pl.ds(base, o_ref.shape[0]), :]


CLAIM_STAGES = (("z", 1), ("x", 1), ("z", 2), ("x", 2), ("yh", 1), ("z", 4))
SWAPPED_STAGES = (("x", 1), ("z", 1), ("x", 2), ("z", 2), ("yh", 1), ("z", 4))
SWAPPED_FIRST = (("x", 1), ("z", 1), ("z", 2), ("x", 2), ("yh", 1), ("z", 4))


def claim_halving(value, gather, cid, alternate_order=None):
    stages = tuple((FINE.index(name), step) for name, step in CLAIM_STAGES)
    alternate = tuple((FINE.index(name), step) for name, step in (alternate_order or CLAIM_STAGES))
    interleaved = (not gather) and alternate != stages
    count = len(stages)
    flat = value.reshape(-1, 128)
    rows = flat.shape[0]
    out_rows = rows if gather else rows >> count
    scratch = [] if gather else [pltpu.VMEM(flat.shape, flat.dtype)]
    scratch += [pltpu.VMEM(flat.shape, flat.dtype)] * (2 if gather else 1)
    scratch += [pltpu.SemaphoreType.DMA((count + 1,))] * (4 if gather else 2)
    out = pl.pallas_call(
        functools.partial(halving_kernel, stages, alternate, gather, interleaved),
        out_shape=jax.ShapeDtypeStruct((out_rows, 128), flat.dtype),
        in_specs=[pl.BlockSpec(memory_space=pltpu.VMEM)],
        out_specs=pl.BlockSpec(memory_space=pltpu.VMEM),
        scratch_shapes=scratch,
        compiler_params=pltpu.CompilerParams(collective_id=cid, has_side_effects=True),
    )(flat)
    return out


def claim_sum(value):
    part = lax.psum_scatter(value, "z", scatter_dimension=0, tiled=True)
    part = lax.psum(part, ("yh", "x"))
    return lax.all_gather(part, "z", axis=0, tiled=True)


def all_sum(value):
    value = lax.psum(value, FEAT)
    value = lax.psum(value, "z")
    return lax.psum(value, ("yh", "x"))


def claim_scatter(value):
    width = value.shape[-1]
    rows = value.shape[0] // lax.axis_size(CLAIM)
    bits = value.reshape(2, 2, 2, 2, 2, 2, rows, width)
    ordered = bits.transpose(5, 2, 4, 1, 0, 3, 6, 7).reshape(value.shape)
    return claim_halving(ordered, False, 5, SWAPPED_FIRST).reshape(rows, width)


def per_device(block_tiles, block_scale, row_index, col_index, start_basis):
    tiles_here = block_tiles.reshape(block_tiles.shape[-3:])
    scale_here = block_scale.reshape(-1)
    rows_here = row_index.reshape(-1)
    cols_here = col_index.reshape(-1)
    edge = tiles_here.shape[-1]
    col_count = start_basis.shape[0] // edge
    claim_count = lax.axis_size(CLAIM)
    own_cols = start_basis.shape[0] // claim_count
    own_first = lax.axis_index(CLAIM) * own_cols
    row_part, col_part = degree_local(tiles_here, scale_here, rows_here, cols_here, col_count)
    (col_total, row_total, _), (start_factor,) = group_sums(
        [col_part, row_part, gram_of(start_basis)], [CLAIM_GROUPS, (FEAT,), (FEAT,)], 0, factored=(2,)
    )
    col_scale = lax.rsqrt(col_total + 1.0)
    row_scale_all = lax.rsqrt(row_total + 1.0)
    own_rows = row_part.shape[0] // lax.axis_size(FEAT)
    own_start = lax.axis_index(FEAT) * own_rows
    row_scale = lax.dynamic_slice_in_dim(row_scale_all, own_start, own_rows, 0)
    first_basis = jnp.dot(start_basis, start_factor[1].T, precision=HIGH)
    first_operand = (col_scale[:, None] * first_basis).astype(jnp.bfloat16)
    first_partial = forward_local(tiles_here, scale_here, rows_here, cols_here, first_operand)

    def row_step(partial_t, previous_t, coupling, cid):
        sums_t = lax.psum_scatter(partial_t, FEAT, scatter_dimension=1, tiled=True)
        all_t = lax.all_gather(sums_t, FEAT, axis=1, tiled=True)
        block_t = row_scale[None, :] * sums_t
        wide_t = row_scale_all[None, :] * all_t
        if previous_t is not None:
            own_previous = lax.dynamic_slice_in_dim(previous_t, own_start, own_rows, 1)
            block_t = block_t - jnp.dot(coupling, own_previous, precision=HIGH)
            wide_t = wide_t - jnp.dot(coupling, previous_t, precision=HIGH)
        gram = jnp.dot(block_t, block_t.T, precision=HIGH)
        upper, inverse = group_factor(gram, ALL_GROUPS, cid)
        return jnp.dot(inverse, wide_t, precision=HIGH), upper

    def backward_partial(basis_t):
        operand_t = (row_scale_all[None, :] * basis_t).astype(jnp.bfloat16)
        return backward_local(tiles_here, scale_here, rows_here, cols_here, operand_t, col_count)

    u_first, b_first = row_step(first_partial, None, None, 1)
    summed = claim_halving(backward_partial(u_first), True, 4, SWAPPED_STAGES).reshape(-1, first_basis.shape[-1])
    update = col_scale[:, None] * summed - jnp.dot(first_basis, b_first.T, precision=HIGH)
    a_second, second_inverse = group_factor(gram_of(update), (FEAT,), 6)
    v_second = jnp.dot(update, second_inverse.T, precision=HIGH)
    scaled = (col_scale[:, None] * v_second).astype(jnp.bfloat16)
    second_partial = forward_local(tiles_here, scale_here, rows_here, cols_here, scaled)
    u_second, b_second = row_step(second_partial, u_first, a_second, 2)
    own_sums = claim_scatter(backward_partial(u_second))
    own_scale = lax.dynamic_slice_in_dim(col_scale, own_first, own_cols, 0)
    own_second = lax.dynamic_slice_in_dim(v_second, own_first, own_cols, 0)
    q_second = own_scale[:, None] * own_sums - jnp.dot(own_second, b_second.T, precision=HIGH)
    a_third, third_inverse = group_factor(gram_of(q_second), ALL_GROUPS, 3)
    v_output = jnp.dot(q_second, third_inverse.T, precision=HIGH)
    bidiagonal = jnp.stack([b_first, a_second, b_second, a_third])
    u_output = lax.dynamic_slice_in_dim(u_second, own_start, own_rows, 1).T
    return (u_output, v_output, bidiagonal)


def solution(mesh):
    claim_n, feat_n = mesh.devices.shape
    fine = Mesh(mesh.devices.reshape(2, claim_n // 16, 8, 2, feat_n // 2), FINE)
    placed = (
        P(CLAIM, FEAT, None, None, None),
        P(CLAIM, FEAT, None),
        P(CLAIM, FEAT, None),
        P(CLAIM, FEAT, None),
        P(FEAT, None),
    )
    return jax.shard_map(
        per_device,
        mesh=fine,
        in_specs=placed,
        out_specs=(P(CLAIM + FEAT, None), P(FEAT + CLAIM, None), P()),
        check_vma=False,
    )
```
